32 devices in a mesh: dp: 8 (over z, y), sub: 4 (over x, core).
Axes of the slice: x: 2, y: 2, z: 4, core: 2. Of those that a mesh axis runs over, the one named last changes fastest.
Arguments:
- hidden_in: bfloat16 [32768, 768], P(('dp', 'sub')), may hold values from -6 to 6
- first_values: bfloat16 [32768, 384], P(('dp', 'sub')), may hold values from -6 to 6
- doc_lengths: int32 [32, 2], P(('dp', 'sub')), may hold values from 0 to 1024, as said below
- out_cotangent: bfloat16 [32768, 768], P(('dp', 'sub')), may hold values from -6 to 6
- query_weight: bfloat16 [589824], P(('dp', 'sub')), may hold values from -0.21875 to 0.21875
- key_weight: bfloat16 [589824], P(('dp', 'sub')), may hold values from -0.21875 to 0.21875
- value_weight: bfloat16 [294912], P(('dp', 'sub')), may hold values from -0.21875 to 0.21875
- output_weight: bfloat16 [589824], P(('dp', 'sub')), may hold values from -0.875 to 0.875
- up_weight: bfloat16 [2359296], P(('dp', 'sub')), may hold values from -0.21875 to 0.21875
- down_weight: bfloat16 [2359296], P(('dp', 'sub')), may hold values from -0.109375 to 0.109375
- vector_pieces: bfloat16 [8448], P(('dp', 'sub')), may hold values from -2 to 2
Outputs:
- hidden_out: bfloat16 [32768, 768], P(('dp', 'sub'))
- grad_hidden: float32 [32768, 768], P(('dp', 'sub'))
- grad_first_values: float32 [32768, 384], P(('dp', 'sub'))
- grad_query_weight: float32 [589824], P(('dp', 'sub'))
- grad_key_weight: float32 [589824], P(('dp', 'sub'))
- grad_value_weight: float32 [294912], P(('dp', 'sub'))
- grad_output_weight: float32 [589824], P(('dp', 'sub'))
- grad_up_weight: float32 [2359296], P(('dp', 'sub'))
- grad_down_weight: float32 [2359296], P(('dp', 'sub'))
- grad_vectors: float32 [8448], P(('dp', 'sub'))
The draws below stay inside these ranges and needn't reach their ends.
Inputs may be any that keep to these rules, and one draw needn't show every extreme that they name: `doc_lengths`: row i is (1024, 0) for one long sequence, (512, 512) for two short ones or (512, 0) for one short one; every draw has rows of the first and of the last kind.
All inputs are finite; a program needn't handle non-finite values.
Results may differ from the reference program's by a relative error of at most 0.012.
Values may be sent and summed in bfloat16 or wider, within the bound.
No kernel may reach another device: no remote copies, remote signals or barrier semaphores. Data moves between devices by JAX's collectives and lax.ppermute only.
A program may use at most 192 MiB of HBM per device.

```python
import math
import jax
import jax.numpy as jnp
from jax import lax

D = 768
HEADS = 12
FF = 3072
SHORT = 512
DV = 384
LONG = 1024
SLOTS = 32
TOKENS = 32768
VEC = 8448
N_DP = 8
N_SUB = 4


def draw_doc_lengths(key, part):
    kind_key = jax.random.fold_in(key, 11)
    place_key = jax.random.fold_in(key, 12)
    kinds = jax.random.randint(kind_key, (SLOTS,), 0, 3)
    chosen = jax.random.randint(place_key, (), 0, SLOTS)
    places = jnp.arange(SLOTS)
    kinds = jnp.where(places == chosen, 0, kinds)
    kinds = jnp.where(places == (chosen + 1) % SLOTS, 2, kinds)
    first_length = jnp.where(kinds == 0, LONG, SHORT)
    second_length = jnp.where(kinds == 1, SHORT, 0)
    return jnp.stack([first_length, second_length], axis=1).astype(jnp.int32)


def draw_vector_pieces(key, part):
    gain_key = jax.random.fold_in(key, 21)
    bias_key = jax.random.fold_in(key, 22)
    places = jnp.arange(VEC)
    gains = 1.0 + jax.random.uniform(gain_key, (VEC,), jnp.float32, -0.4, 0.4)
    biases = jnp.clip(0.5 * jax.random.normal(bias_key, (VEC,), jnp.float32), -2.0, 2.0)
    is_gain = (places < D) | (places >= 4 * D) & (places < 5 * D)
    return jnp.where(is_gain, gains, biases).astype(jnp.bfloat16)


def steps_of(key, shape, pieces, least, top_value):
    factor_of = 1.0
    for dim, blocks in pieces:
        heights = jax.random.uniform(jax.random.fold_in(jax.random.fold_in(key, 6), dim), (blocks,), jnp.float32, least / len(pieces), top_value / len(pieces))
        factor_of = factor_of * jnp.repeat(jnp.exp(heights), shape[dim] // blocks).reshape((-1,) + (1,) * (len(shape) - 1 - dim))
    return factor_of


def noise(stream_key, extent, scale, most, pieces=(), held_as=jnp.bfloat16):
    level = steps_of(stream_key, extent, pieces, -0.22, 0.18) if pieces else 1.0
    values = jax.random.normal(stream_key, extent, jnp.float32) * scale * level
    return jnp.minimum(jnp.maximum(values, -most), most).astype(held_as)


def setup_inputs(seed: int = 0) -> dict:
    splits = jax.random.split(jax.random.key(seed), 12)
    hidden_in = noise(splits[0], (TOKENS, D), 1.0, 6.0, ((0, 32),))
    first_values = noise(splits[1], (TOKENS, DV), 1.0, 6.0, ((0, 32),))
    doc_lengths = draw_doc_lengths(jax.random.fold_in(splits[11], 71), 0)
    out_cotangent = noise(splits[3], (TOKENS, D), 1.0, 6.0, ((0, 32),))
    query_weight = noise(splits[4], (D * D,), D ** -0.5, 0.21875, ((0, 32),))
    key_weight = noise(splits[5], (D * D,), D ** -0.5, 0.21875, ((0, 32),))
    value_weight = noise(splits[6], (D * DV,), D ** -0.5, 0.21875, ((0, 32),))
    output_weight = noise(splits[7], (D * D,), (D // 16) ** -0.5, 0.875, ((0, 32),))
    up_weight = noise(splits[8], (D * FF,), D ** -0.5, 0.21875, ((0, 32),))
    down_weight = noise(splits[9], (FF * D,), FF ** -0.5, 0.109375, ((0, 32),))
    vector_pieces = draw_vector_pieces(jax.random.fold_in(splits[11], 71), 0)
    return {"hidden_in": hidden_in, "first_values": first_values, "doc_lengths": doc_lengths, "out_cotangent": out_cotangent, "query_weight": query_weight, "key_weight": key_weight, "value_weight": value_weight, "output_weight": output_weight, "up_weight": up_weight, "down_weight": down_weight, "vector_pieces": vector_pieces}


@jax.custom_vjp
def low(v):
    return lax.optimization_barrier(v.astype(jnp.bfloat16)).astype(jnp.float32)

@jax.custom_vjp
def low_back(v):
    return v

def low_keep(v):
    return (low(v), None)

def low_pass(kept, grad):
    return (grad,)

def back_keep(v):
    return (v, None)

def back_low(kept, grad):
    return (low(grad),)
low.defvjp(low_keep, low_pass)
low_back.defvjp(back_keep, back_low)

def layer_norm(values, norm_gain, offset):
    centered = values - lax.optimization_barrier(jnp.mean(values, axis=-1, keepdims=True))
    spread = lax.optimization_barrier(jnp.mean(centered * centered, axis=-1, keepdims=True))
    return centered * lax.rsqrt(spread + 1e-05) * norm_gain + offset

def gelu_tanh(values):
    return 0.5 * values * (1.0 + jnp.tanh(0.7978845608028654 * (values + 0.044715 * values * values * values)))

def matmul(left, right):
    return jnp.dot(left, right, preferred_element_type=jnp.float32, precision=lax.Precision.HIGHEST)

def forward_slot(params, inputs, first_low, allowed):
    query_flat, key_flat, value_flat, output_flat, up_flat, down_flat, vector = params
    row_count, model_width = inputs.shape
    value_width = first_low.shape[1]
    hidden_units = up_flat.shape[0] // model_width
    query_w = query_flat.reshape(model_width, model_width)
    key_w = key_flat.reshape(model_width, model_width)
    value_w = value_flat.reshape(model_width, value_width)
    output_w = output_flat.reshape(model_width, model_width)
    up_w = up_flat.reshape(model_width, hidden_units)
    down_w = down_flat.reshape(hidden_units, model_width)
    sections = [vector[position * model_width:(position + 1) * model_width] for position in range(7)]
    up_bias = vector[7 * model_width:]
    normed = low(layer_norm(inputs, sections[0], sections[1]))
    queries = low_back(low(matmul(normed, query_w) + sections[2]))
    key_low = low_back(low(matmul(normed, key_w)))
    fresh_values = low_back(low(matmul(normed, value_w)))
    values = jnp.concatenate([fresh_values, first_low], axis=1)
    head_size = model_width // HEADS
    score_scale = 1.0 / math.sqrt(head_size)
    query_heads = queries.reshape(row_count, HEADS, head_size)
    key_heads = key_low.reshape(row_count, HEADS, head_size)
    value_heads = values.reshape(row_count, HEADS, head_size)
    scores = jnp.einsum('qhd,khd->hqk', query_heads, key_heads, precision=lax.Precision.HIGHEST) * score_scale
    scores = low_back(jnp.where(allowed[None], scores, -1e+30))
    probabilities = jax.nn.softmax(scores, axis=-1)
    context = jnp.einsum('hqk,khd->qhd', low(probabilities), value_heads, precision=lax.Precision.HIGHEST)
    context = low_back(low(context.reshape(row_count, model_width)))
    branch = low_back(matmul(context, output_w) + sections[3])
    middle = inputs + branch
    normed2 = low(layer_norm(middle, sections[4], sections[5]))
    hidden_pre = low_back(matmul(normed2, up_w) + up_bias)
    activated = low(gelu_tanh(hidden_pre))
    return middle + low_back(matmul(activated, down_w) + sections[6])

def reference(hidden_in, first_values, doc_lengths, out_cotangent, query_weight, key_weight, value_weight, output_weight, up_weight, down_weight, vector_pieces):
    slot_count = N_DP * N_SUB
    row_count = hidden_in.shape[0] // slot_count
    model_width = hidden_in.shape[1]
    value_width = first_values.shape[1]
    params = tuple((piece.astype(jnp.float32) for piece in (query_weight, key_weight, value_weight, output_weight, up_weight, down_weight, vector_pieces)))

    def one_slot(totals, slot_item):
        inputs_low, first_low, lengths, cotangent = slot_item
        places = jnp.arange(row_count, dtype=jnp.int32)
        segment = (places >= lengths[0]).astype(jnp.int32) + (places >= lengths[0] + lengths[1]).astype(jnp.int32)
        allowed = (segment[:, None] == segment[None, :]) & (places[None, :] <= places[:, None])
        live_rows = (segment < 2).astype(jnp.float32)[:, None]

        def forward_fixed(weights_now, inputs, first_now):
            return forward_slot(weights_now, inputs, first_now, allowed)
        result, pullback = jax.vjp(forward_fixed, params, inputs_low.astype(jnp.float32), first_low.astype(jnp.float32))
        grad_params, grad_inputs, grad_first = pullback(cotangent.astype(jnp.float32) * live_rows)
        totals = tuple((total + extra for total, extra in zip(totals, grad_params)))
        return (totals, ((result * live_rows).astype(jnp.bfloat16), grad_inputs, grad_first))
    start = tuple((jnp.zeros(piece.shape, jnp.float32) for piece in params))
    totals, outputs = lax.scan(one_slot, start, (hidden_in.reshape(slot_count, row_count, model_width), first_values.reshape(slot_count, row_count, value_width), doc_lengths, out_cotangent.reshape(slot_count, row_count, model_width)))
    hidden_out = outputs[0].reshape(slot_count * row_count, model_width)
    grad_hidden = outputs[1].reshape(slot_count * row_count, model_width)
    grad_first_values = outputs[2].reshape(slot_count * row_count, value_width)
    return (hidden_out, grad_hidden, grad_first_values, totals[0], totals[1], totals[2], totals[3], totals[4], totals[5], totals[6])
```

```python
import functools, math
import jax, jax.numpy as jnp
from jax import lax
from jax.experimental import pallas as pl
from jax.experimental.pallas import tpu as pltpu
bf=jnp.bfloat16; f32=jnp.float32
VL=60<<20
NT=(((1,),(1,)),((),()))
TN=(((0,),(0,)),((),()))
NN=(((1,),(0,)),((),()))
def dot(a,b,dn=NN):
    return lax.dot_general(a,b,dn,preferred_element_type=f32)
def cp(**k):
    return pltpu.CompilerParams(vmem_limit_bytes=VL,**k)
def full(shape):
    nd=len(shape)
    return pl.BlockSpec(shape,lambda *a:(0,)*nd)
def cost(fl,by,tr=0):
    return pl.CostEstimate(flops=int(fl),bytes_accessed=int(by),transcendentals=int(tr))

def norm_stats(v):
    c=v-jnp.mean(v,axis=-1,keepdims=True)
    r=lax.rsqrt(jnp.mean(c*c,axis=-1,keepdims=True)+1e-5)
    return c*r,r

def qkv_body(x_ref,first_ref,wq_ref,wk_ref,wv_ref,g_ref,b_ref,qb_ref,n_ref,q_ref,k_ref,v_ref):
    xh,_=norm_stats(x_ref[...].astype(f32))
    n=(xh*g_ref[...]+b_ref[...]).astype(bf)
    n_ref[...]=n
    q=(dot(n,wq_ref[...])+qb_ref[...]).astype(bf)
    q_ref[...]=q*0.125
    k_ref[...]=dot(n,wk_ref[...]).astype(bf)
    w=wv_ref.shape[1]
    v_ref[:,:w]=dot(n,wv_ref[...]).astype(bf)
    v_ref[:,w:]=first_ref[...]
def qkv(x,first,wq,wk,wv,g,b,qb,tm=256):
    t,d=x.shape; dv=first.shape[1]
    row=lambda c:pl.BlockSpec((tm,c),lambda i:(i,0))
    return pl.pallas_call(qkv_body,grid=(t//tm,),
        in_specs=[row(d),row(dv),full((d,d)),full((d,d)),full((d,dv)),full((1,d)),full((1,d)),full((1,d))],
        out_specs=[row(d)]*4,
        out_shape=[jax.ShapeDtypeStruct((t,d),bf)]*4,compiler_params=cp(),name="qkv",
        cost_estimate=cost(2*t*d*(2*d+dv),t*d*14+d*d*6))(x,first,wq,wk,wv,g,b,qb)

def afwd_body(len_ref,q_ref,k_ref,v_ref,o_ref,l_ref,*,bq):
    t=q_ref.shape[0]; half=t//2
    long_bias=jnp.where(len_ref[0]>half,0.0,-1e30)
    dh=q_ref.shape[1]//2
    p_id=pl.program_id(0)
    diag=lax.broadcasted_iota(jnp.int32,(bq,bq),0)>=lax.broadcasted_iota(jnp.int32,(bq,bq),1)
    for i in range(t//bq):
        outs=[]
        for h in range(2):
            q=q_ref[i*bq:(i+1)*bq,h*dh:(h+1)*dh]
            n=(i+1)*bq
            s=dot(q,k_ref[0:n,h*dh:(h+1)*dh],NT)
            parts=[]
            lo=half if i*bq>=half else 0
            if lo: parts.append(s[:,:lo]+long_bias)
            if i*bq>lo: parts.append(s[:,lo:i*bq])
            parts.append(jnp.where(diag,s[:,i*bq:],-1e30))
            s=jnp.concatenate(parts,axis=1) if len(parts)>1 else parts[0]
            m=jnp.max(s,axis=-1,keepdims=True)
            p=jnp.exp(s-m)
            l=jnp.sum(p,axis=-1,keepdims=True)
            o=dot(p.astype(bf),v_ref[0:n,h*dh:(h+1)*dh])
            outs.append((o*(1.0/l)).astype(bf))
            lse=m+jnp.log(l)
            l_ref[pl.ds(2*p_id+h,1),i*bq:(i+1)*bq]=jnp.transpose(jnp.broadcast_to(lse,(bq,128)))[0:1,:]
        o_ref[i*bq:(i+1)*bq,:]=jnp.concatenate(outs,axis=1)
def afwd(lens,q,k,v,bq=256):
    t,d=q.shape
    col=pl.BlockSpec((t,128),lambda p,*a:(0,p))
    return pl.pallas_call(functools.partial(afwd_body,bq=bq),
        grid_spec=pltpu.PrefetchScalarGridSpec(num_scalar_prefetch=1,grid=(d//128,),in_specs=[col]*3,
            out_specs=[col,pl.BlockSpec((16,t),lambda p,*a:(0,0))]),
        out_shape=[jax.ShapeDtypeStruct((t,d),bf),jax.ShapeDtypeStruct((16,t),f32)],compiler_params=cp(),name="afwd",
        cost_estimate=cost(4*t*t*d*0.6*4,t*d*8,t*t*6))(lens,q,k,v)

def abwd_body(len_ref,q_ref,k_ref,v_ref,do_ref,l_ref,dl_ref,dq_ref,dk_ref,dv_ref,*,bk,first_pair,dqt):
    t=q_ref.shape[0]; half=t//2
    long_bias=jnp.where(len_ref[0]>half,0.0,-1e30)
    dh=q_ref.shape[1]//2
    p_id=pl.program_id(0)+first_pair
    diag=lax.broadcasted_iota(jnp.int32,(bk,bk),0)<=lax.broadcasted_iota(jnp.int32,(bk,bk),1)
    dqs=[]
    dks=[]; dvs=[]
    for h in range(2):
        sl=slice(h*dh,(h+1)*dh)
        lrow=l_ref[pl.ds(2*p_id+h,1),:]; drow=dl_ref[pl.ds(2*p_id+h,1),:]
        dq=None; dkh=[]; dvh=[]
        for j in range(t//bk):
            k=k_ref[j*bk:(j+1)*bk,sl]; v=v_ref[j*bk:(j+1)*bk,sl]
            a=j*bk
            q=q_ref[a:,sl]; do=do_ref[a:,sl]
            st=dot(k,q,NT)
            pieces=[jnp.where(diag,st[:,:bk],-1e30)]
            hi=max(half,a+bk) if a<half else t
            if hi>a+bk: pieces.append(st[:,bk:hi-a])
            if a<half: pieces.append(st[:,hi-a:]+long_bias)
            st=jnp.concatenate(pieces,axis=1) if len(pieces)>1 else pieces[0]
            p=jnp.exp(st-lrow[:,a:])
            dp=dot(v,do,NT)
            ds=(p*(dp-drow[:,a:])).astype(bf)
            dvh.append(dot(p.astype(bf),do))
            dkh.append(dot(ds,q))
            if dqt: c=dot(k,ds,TN)
            else: c=dot(ds,k,TN)
            ax=1 if dqt else 0
            if dq is None: dq=c
            else:
                if dqt: dq=jnp.concatenate([dq[:,:a],dq[:,a:]+c],axis=1)
                else: dq=jnp.concatenate([dq[:a],dq[a:]+c],axis=0)
        dqs.append(jnp.transpose(dq) if dqt else dq)
        dks.append(jnp.concatenate(dkh,axis=0)); dvs.append(jnp.concatenate(dvh,axis=0))
    dq_ref[...]=(jnp.concatenate(dqs,axis=1)*0.125).astype(bf)
    dk_ref[...]=jnp.concatenate(dks,axis=1).astype(bf)
    dv_ref[...]=jnp.concatenate(dvs,axis=1).astype(dv_ref.dtype)
def abwd(lens,q,k,v,do,lse,delta,first_pair,pairs,dv_dtype,bk=256,dqt=True):
    t,d=q.shape
    col=pl.BlockSpec((t,128),lambda p,*a:(0,p+first_pair))
    ocol=pl.BlockSpec((t,128),lambda p,*a:(0,p))
    st=pl.BlockSpec((16,t),lambda p,*a:(0,0))
    w=pairs*128
    return pl.pallas_call(functools.partial(abwd_body,bk=bk,first_pair=first_pair,dqt=dqt),
        grid_spec=pltpu.PrefetchScalarGridSpec(num_scalar_prefetch=1,grid=(pairs,),in_specs=[col]*4+[st]*2,
            out_specs=[ocol]*3),
        out_shape=[jax.ShapeDtypeStruct((t,w),bf)]*2+[jax.ShapeDtypeStruct((t,w),dv_dtype)],compiler_params=cp(),name="abwd",
        cost_estimate=cost(10*t*t*w*0.6*4,t*w*16,t*t*w//64*0.6))(lens,q,k,v,do,lse,delta)

def mid_body(len_ref,ctx_ref,x_ref,cot_ref,wo_ref,wu_ref,wd_ref,ob_ref,g_ref,b_ref,db_ref,ub_ref,
             out_ref,act_ref,gp_ref,n2_ref,gb_ref,dm_ref,gc_ref,dl_ref,s768_ref,sub_ref,*,fc,heads):
    tm=x_ref.shape[0]; d=x_ref.shape[1]; ff=wu_ref.shape[1]
    i=pl.program_id(0)
    pos=lax.broadcasted_iota(jnp.int32,(tm,1),0)+i*tm
    live=jnp.where(pos<len_ref[0]+len_ref[1],1.0,0.0)
    ctx=ctx_ref[...]
    middle=x_ref[...].astype(f32)+(dot(ctx,wo_ref[...])+ob_ref[...])
    xh,r=norm_stats(middle)
    n2=(xh*g_ref[...]+b_ref[...]).astype(bf)
    n2_ref[...]=n2
    gr=cot_ref[...].astype(f32)*live
    g2=gr.astype(bf)
    acc=jnp.zeros((tm,d),f32); dn=jnp.zeros((tm,d),f32)
    @pl.when(i==0)
    def _():
        s768_ref[...]=jnp.zeros_like(s768_ref); sub_ref[...]=jnp.zeros_like(sub_ref)
    for c in range(ff//fc):
        cs=slice(c*fc,(c+1)*fc)
        h=dot(n2,wu_ref[:,cs])+ub_ref[:,cs]
        da=dot(g2,wd_ref[cs,:],NT)
        h2=h*h
        t=jnp.tanh(h*(0.7978845608028654+(0.7978845608028654*0.044715)*h2))
        u=0.5+0.5*t
        act=(h*u).astype(bf)
        dg=u+(0.5*h)*((1.0-t*t)*(0.7978845608028654+(3*0.7978845608028654*0.044715)*h2))
        gp=da*dg
        gpb=gp.astype(bf)
        act_ref[:,cs]=act; gp_ref[:,cs]=gpb
        sub_ref[:,cs]+=jnp.sum(gpb.astype(f32),axis=0,keepdims=True)
        acc=acc+dot(act,wd_ref[cs,:])
        dn=dn+dot(gpb,wu_ref[:,cs],NT)
    out_ref[...]=((middle+(acc+db_ref[...]))*live).astype(bf)
    e=dn*g_ref[...]
    dm=gr+r*(e-jnp.mean(e,axis=-1,keepdims=True)-xh*jnp.mean(e*xh,axis=-1,keepdims=True))
    dm_ref[...]=dm
    gb=dm.astype(bf)
    gb_ref[...]=gb
    gc=dot(gb,wo_ref[...],NT).astype(bf)
    gc_ref[...]=gc
    pr=gc.astype(f32)*ctx.astype(f32)
    hi=pr.astype(bf); lo=(pr-hi.astype(f32)).astype(bf)
    dh=d//heads
    ind=(lax.broadcasted_iota(jnp.int32,(16,d),1)//dh==lax.broadcasted_iota(jnp.int32,(16,d),0)).astype(bf)
    dl_ref[...]=dot(ind,hi,NT)+dot(ind,lo,NT)
    def cs_(v): return jnp.sum(v,axis=0,keepdims=True)
    s768_ref[0:1,:]+=cs_(gb.astype(f32))
    s768_ref[1:2,:]+=cs_(dn*xh)
    s768_ref[2:3,:]+=cs_(dn)
    s768_ref[3:4,:]+=cs_(gr)
def mid(lens,ctx,x,cot,wo,wu,wd,ob,g,b,db,ub,heads=12,tm=256,fc=768):
    t,d=x.shape; ff=wu.shape[1]
    row=lambda c:pl.BlockSpec((tm,c),lambda i,*a:(i,0))
    one=lambda s:pl.BlockSpec(s,lambda i,*a:(0,0),pipeline_mode=pl.Buffered(1))
    sd=jax.ShapeDtypeStruct
    return pl.pallas_call(functools.partial(mid_body,fc=fc,heads=heads),
        grid_spec=pltpu.PrefetchScalarGridSpec(num_scalar_prefetch=1,grid=(t//tm,),
            in_specs=[row(d)]*3+[one((d,d)),one((d,ff)),one((ff,d))]+[one((1,d))]*4+[one((1,ff))],
            out_specs=[row(d),row(ff),row(ff),row(d),row(d),row(d),row(d),pl.BlockSpec((16,tm),lambda i,*a:(0,i)),one((8,d)),one((1,ff))]),
        out_shape=[sd((t,d),bf),sd((t,ff),bf),sd((t,ff),bf),sd((t,d),bf),sd((t,d),bf),sd((t,d),f32),sd((t,d),bf),sd((16,t),f32),sd((8,d),f32),sd((1,ff),f32)],
        compiler_params=cp(),name="mid",cost_estimate=cost(2*t*d*(2*d+4*ff),t*d*20+t*ff*4+d*ff*4,t*ff))(lens,ctx,x,cot,wo,wu,wd,ob,g,b,db,ub)

def wg_body(a_ref,b_ref,o_ref):
    o_ref[...]=dot(a_ref[...],b_ref[...],TN).astype(o_ref.dtype)
def wg(a,b,tm,tn,name="wg"):
    t,m=a.shape; n=b.shape[1]
    return pl.pallas_call(wg_body,grid=(m//tm,n//tn),
        in_specs=[pl.BlockSpec((t,tm),lambda i,j:(0,i)),pl.BlockSpec((t,tn),lambda i,j:(0,j))],
        out_specs=pl.BlockSpec((tm,tn),lambda i,j:(i,j)),
        out_shape=jax.ShapeDtypeStruct((m,n),bf),compiler_params=cp(),name=name,
        cost_estimate=cost(2*t*m*n,t*(m+n)*2+m*n*2))(a,b)

def qb_body(x_ref,dm_ref,dqa_ref,dqb_ref,dka_ref,dkb_ref,df_ref,wq_ref,wk_ref,wv_ref,g_ref,gh_ref,s_ref):
    i=pl.program_id(0)
    w=dqa_ref.shape[1]
    dn=dot(dqa_ref[...],wq_ref[:,:w],NT)+dot(dqb_ref[...],wq_ref[:,w:],NT)
    dn=dn+dot(dka_ref[...],wk_ref[:,:w],NT)+dot(dkb_ref[...],wk_ref[:,w:],NT)
    dn=dn+dot(df_ref[...],wv_ref[...],NT)
    xh,r=norm_stats(x_ref[...].astype(f32))
    e=dn*g_ref[...]
    gh_ref[...]=dm_ref[...]+r*(e-jnp.mean(e,axis=-1,keepdims=True)-xh*jnp.mean(e*xh,axis=-1,keepdims=True))
    @pl.when(i==0)
    def _(): s_ref[...]=jnp.zeros_like(s_ref)
    def cs_(v): return jnp.sum(v,axis=0,keepdims=True)
    s_ref[0:1,:]+=cs_(dn*xh)
    s_ref[1:2,:]+=cs_(dn)
    s_ref[2:3,:w]+=cs_(dqa_ref[...].astype(f32))
    s_ref[2:3,w:]+=cs_(dqb_ref[...].astype(f32))
def qkv_back(x,dm,dqa,dqb,dka,dkb,df,wq,wk,wv,g,tm=256):
    t,d=x.shape; dv=df.shape[1]; w=dqa.shape[1]
    row=lambda c:pl.BlockSpec((tm,c),lambda i:(i,0))
    return pl.pallas_call(qb_body,grid=(t//tm,),
        in_specs=[row(d),row(d)]+[row(w)]*4+[row(dv),full((d,d)),full((d,d)),full((d,dv)),full((1,d))],
        out_specs=[row(d),full((8,d))],
        out_shape=[jax.ShapeDtypeStruct((t,d),f32),jax.ShapeDtypeStruct((8,d),f32)],compiler_params=cp(),name="qkvback",
        cost_estimate=cost(2*t*d*(2*d+dv),t*d*16+d*d*5))(x,dm,dqa,dqb,dka,dkb,df,wq,wk,wv,g)

from jax.sharding import PartitionSpec as P
AXES=("dp","sub")

def index_bits(sizes):
    return [(a,b) for a in reversed(AXES) for b in range(sizes[a].bit_length()-1)]

def swap(v,axis,bit,size):
    return lax.ppermute(v,axis,[(i,i^(1<<bit)) for i in range(size)])

def scatter_sum(g,sizes,order):
    n,rows,cols=g.shape
    bits=index_bits(sizes)
    left=list(reversed(range(len(bits))))
    g=g.reshape((2,)*len(bits)+(rows,cols))
    for step,b in enumerate(order):
        axis,k=bits[b]
        mine=(lax.axis_index(axis)>>k)&1
        pos=left.index(b); left.pop(pos)
        send=lax.dynamic_index_in_dim(g,1-mine,pos,keepdims=False)
        keep=lax.dynamic_index_in_dim(g,mine,pos,keepdims=False)
        got=swap(send,axis,k,sizes[axis])
        g=keep.astype(f32)+got.astype(f32)
        if step<len(order)-1: g=g.astype(bf)
    return g

def shards(sizes,hidden_in,first_values,doc_lengths,out_cotangent,query_weight,key_weight,value_weight,output_weight,up_weight,down_weight,vector_pieces):
    n=sizes["dp"]*sizes["sub"]
    t,d=hidden_in.shape; dv=first_values.shape[1]
    ff=up_weight.shape[0]*n//d
    nb=len(index_bits(sizes))
    ra=d//n; rv=dv//n
    vs=vector_pieces.shape[0]
    flat=jnp.concatenate([query_weight,key_weight,value_weight,output_weight,up_weight,down_weight,vector_pieces])
    w=flat.shape[0]; cols=768
    flat=jnp.pad(flat,(0,-w%cols)).reshape(-1,cols)
    all_w=lax.all_gather(flat,AXES,axis=0,tiled=False).reshape(n,-1)
    def take(off,size): return all_w[:,off:off+size].reshape(-1)
    offs=[0]
    for a in (query_weight,key_weight,value_weight,output_weight,up_weight,down_weight,vector_pieces): offs.append(offs[-1]+a.shape[0])
    parts=[take(offs[i],offs[i+1]-offs[i]) for i in range(7)]
    wq,wk,wv,wo=parts[0].reshape(d,d),parts[1].reshape(d,d),parts[2].reshape(d,dv),parts[3].reshape(d,d)
    wu,wd=parts[4].reshape(d,ff),parts[5].reshape(ff,d)
    vec=parts[6].astype(f32)
    r=lambda i:vec[i*d:(i+1)*d].reshape(1,d)
    ub=vec[7*d:].reshape(1,ff)
    lens=doc_lengths[0]
    x=hidden_in; cot=out_cotangent
    nrm,q,k,v=qkv(x,first_values,wq,wk,wv,r(0),r(1),r(2))
    ctx,lse=afwd(lens,q,k,v)
    out,act,gp,n2,gb,dm,gc,dl,s768,sub=mid(lens,ctx,x,cot,wo,wu,wd,r(3),r(4),r(5),r(6),ub)
    g2=jnp.where((jnp.arange(t)<lens[0]+lens[1])[:,None],cot,jnp.zeros_like(cot))
    A=list(range(nb)); B=A[:]
    s=sizes["sub"].bit_length()-1
    if s>=2 and nb>s: B[1],B[s]=B[s],B[1]
    pc=lambda m:m.reshape(n,-1,m.shape[1])
    d_down=scatter_sum(pc(wg(act,g2,768,768,"dwd")),sizes,A)
    d_up=scatter_sum(pc(wg(n2,gp,768,768,"dwu")),sizes,B)
    d_out=scatter_sum(pc(wg(ctx,gb,768,768,"dwo")),sizes,A)
    dqa,dka,df=abwd(lens,q,k,v,gc,lse,dl,0,3,bf)
    h=d//2
    one=jnp.concatenate([pc(wg(nrm,dqa,768,h,"dwqa")),pc(wg(nrm,dka,768,h,"dwka")),pc(wg(nrm,df,768,h,"dwv"))],axis=1)
    one=scatter_sum(one,sizes,B)
    dqb,dkb,gf=abwd(lens,q,k,v,gc,lse,dl,3,3,f32)
    gh,s1=qkv_back(x,dm,dqa,dqb,dka,dkb,df,wq,wk,wv,r(0))
    vg=jnp.concatenate([s1[0],s1[1],s1[2],s768[0],s768[1],s768[2],s768[3],sub[0]]).reshape(n,vs)
    vg=jnp.pad(vg,((0,0),(0,-vs%h))).reshape(n,-1,h)
    vg=jnp.pad(vg,((0,0),(0,-vg.shape[1]%8),(0,0))).astype(bf)
    two=jnp.concatenate([pc(wg(nrm,dqb,768,h,"dwqb")),pc(wg(nrm,dkb,768,h,"dwkb")),vg],axis=1)
    two=scatter_sum(two,sizes,A)
    gq=jnp.concatenate([one[:ra],two[:ra]],axis=1).reshape(-1)
    gk=jnp.concatenate([one[ra:2*ra],two[ra:2*ra]],axis=1).reshape(-1)
    gv=one[2*ra:].reshape(-1)
    gvec=two[2*ra:].reshape(-1)[:vs]
    return (out,gh,gf,gq,gk,gv,d_out.reshape(-1),d_up.reshape(-1),d_down.reshape(-1),gvec)

def solution(mesh):
    s2=P(AXES,None); s1=P(AXES)
    return jax.shard_map(functools.partial(shards,dict(mesh.shape)),mesh=mesh,in_specs=(s2,)*4+(s1,)*7,out_specs=(s2,)*3+(s1,)*7,check_vma=False)
```

```python
import functools, math
import jax, jax.numpy as jnp
from jax import lax
from jax.experimental import pallas as pl
from jax.experimental.pallas import tpu as pltpu
bf=jnp.bfloat16; f32=jnp.float32
NT=(((1,),(1,)),((),()))
TN=(((0,),(0,)),((),()))
NN=(((1,),(0,)),((),()))
def dot(a,b,dn=NN):
    return lax.dot_general(a,b,dn,preferred_element_type=f32)
def cp(mb):
    return pltpu.CompilerParams(vmem_limit_bytes=mb<<20)
def full(shape):
    nd=len(shape)
    return pl.BlockSpec(shape,lambda *a:(0,)*nd)
def cost(fl,by,tr=0):
    return pl.CostEstimate(flops=1000,bytes_accessed=1000,transcendentals=0)

def norm_stats(v):
    c=v-jnp.mean(v,axis=-1,keepdims=True)
    r=lax.rsqrt(jnp.mean(c*c,axis=-1,keepdims=True)+1e-5)
    return c*r,r

ANY=pl.BlockSpec(memory_space=pl.ANY)
def stage(n,rows,cols):
    return pltpu.VMEM((n,rows,cols) if rows%16 else (1,16,128),bf)
def place(bufs,pos_ref,w_ref,st_ref,sem,col=0):
    rows,w=bufs[0].shape[1:]
    p=0
    for b in bufs:
        for a in range(b.shape[0]):
            if rows%16: to=st_ref.at[pos_ref[p],:,pl.ds(col,w)]
            else: to=w_ref.at[pl.ds(pl.multiple_of(pos_ref[p]*rows,16),rows),pl.ds(col,w)]
            pltpu.make_async_copy(b.at[a],to,sem).start()
            p+=1
def placed(w_ref,st_ref,sem,rows):
    if rows%16==0:
        pltpu.make_async_copy(w_ref,w_ref,sem).wait()
        return
    pltpu.make_async_copy(st_ref,st_ref,sem).wait()
    k=16//math.gcd(rows,16); cols=w_ref.shape[1]
    def move(u,_):
        v=jnp.concatenate([st_ref[k*u+i,:,0:cols].astype(f32) for i in range(k)],axis=0)
        w_ref[pl.ds(pl.multiple_of(u*(k*rows),16),k*rows),:]=v.astype(bf)
        return 0
    lax.fori_loop(0,st_ref.shape[0]//k,move,0)
def cs_(v): return jnp.sum(v,axis=0,keepdims=True)

def qkv_body(pa_ref,pb_ref,x_ref,first_ref,vin_ref,*refs,na,nb,per):
    abufs=refs[:na]; bbufs=refs[na:na+nb]
    n_ref,q_ref,k_ref,v_ref,vec_ref,wa,wb,sa,sb,flat,sems=refs[na+nb:]
    d=x_ref.shape[1]; w=first_ref.shape[1]
    @pl.when(pl.program_id(0)==0)
    def _():
        place(bbufs,pb_ref,wb,sb,sems.at[1]); place(abufs,pa_ref,wa,sa,sems.at[0])
        placed(wb,sb,sems.at[1],bbufs[0].shape[1])
        if per:
            for o in range(sb.shape[0]):
                v=sb[o,:,d:d+128].astype(f32)
                for s in range(-(-per//128)):
                    flat[0:1,per*o+128*s:per*o+128*(s+1)]=v[s:s+1,:]
            for i in range(vec_ref.shape[0]):
                vec_ref[i:i+1,:]=flat[0:1,d*i:d*(i+1)]
        else:
            vec_ref[...]=vin_ref[...]
        placed(wa,sa,sems.at[0],abufs[0].shape[1])
    xh,_=norm_stats(x_ref[...].astype(f32))
    n=(xh*vec_ref[0:1,:]+vec_ref[1:2,:]).astype(bf)
    n_ref[...]=n
    q=(dot(n,wa[:,:d])+vec_ref[2:3,:]).astype(bf)
    q_ref[...]=q*0.125
    k_ref[...]=dot(n,wb[...]).astype(bf)
    v_ref[:,:w]=dot(n,wa[:,d:]).astype(bf)
    v_ref[:,w:]=first_ref[...]
def qkv(x,first,wa,wb,per,vin,tm=256):
    t,d=x.shape; dv=first.shape[1]
    (abufs,pa),(bbufs,pb)=wa,wb
    n=sum(b.shape[0] for b in bbufs); nvec=vin.shape[0]
    row=lambda c:pl.BlockSpec((tm,c),lambda i,*a:(i,0))
    return pl.pallas_call(functools.partial(qkv_body,na=len(abufs),nb=len(bbufs),per=per),
        grid_spec=pltpu.PrefetchScalarGridSpec(num_scalar_prefetch=2,grid=(t//tm,),
            in_specs=[row(d),row(dv),full(vin.shape)]+[ANY]*(len(abufs)+len(bbufs)),
            out_specs=[row(d)]*4+[pl.BlockSpec((nvec,d),lambda i,*a:(0,0))],scratch_shapes=[pltpu.VMEM((d,d+dv),bf),pltpu.VMEM((d,d),bf),stage(n,*abufs[0].shape[1:]),stage(n,*bbufs[0].shape[1:]),pltpu.VMEM((1,nvec*d+256),f32),pltpu.SemaphoreType.DMA((2,))]),
        out_shape=[jax.ShapeDtypeStruct((t,d),bf)]*4+[jax.ShapeDtypeStruct((nvec,d),f32)],compiler_params=cp(60),name="qkv",
        cost_estimate=cost(2*t*d*(2*d+dv),t*d*14+d*d*6))(pa,pb,x,first,vin,*abufs,*bbufs)

def afwd_body(len_ref,q_ref,k_ref,v_ref,o_ref,l_ref,*,bq):
    t=q_ref.shape[0]; half=t//2
    long_bias=jnp.where(len_ref[0]>half,0.0,-1e30)
    dh=q_ref.shape[1]//2
    diag=lax.broadcasted_iota(jnp.int32,(bq,bq),0)>=lax.broadcasted_iota(jnp.int32,(bq,bq),1)
    for i in range(t//bq):
        outs=[]
        for h in range(2):
            q=q_ref[i*bq:(i+1)*bq,h*dh:(h+1)*dh]
            n=(i+1)*bq
            s=dot(q,k_ref[0:n,h*dh:(h+1)*dh],NT)
            parts=[]
            lo=half if i*bq>=half else 0
            if lo: parts.append(s[:,:lo]+long_bias)
            if i*bq>lo: parts.append(s[:,lo:i*bq])
            parts.append(jnp.where(diag,s[:,i*bq:],-1e30))
            s=jnp.concatenate(parts,axis=1) if len(parts)>1 else parts[0]
            m=jnp.max(s,axis=-1,keepdims=True)
            p=jnp.exp(s-m)
            l=jnp.sum(p,axis=-1,keepdims=True)
            o=dot(p.astype(bf),v_ref[0:n,h*dh:(h+1)*dh])
            outs.append((o*(1.0/l)).astype(bf))
            lse=m+jnp.log(l)
            l_ref[0,h:h+1,i*bq:(i+1)*bq]=jnp.transpose(jnp.broadcast_to(lse,(bq,128)))[0:1,:]
        o_ref[i*bq:(i+1)*bq,:]=jnp.concatenate(outs,axis=1)
def afwd(lens,q,k,v,first_pair,pairs,bq=256):
    t=q.shape[0]
    col=pl.BlockSpec((t,128),lambda p,*a:(0,p+first_pair))
    return pl.pallas_call(functools.partial(afwd_body,bq=bq),
        grid_spec=pltpu.PrefetchScalarGridSpec(num_scalar_prefetch=1,grid=(pairs,),in_specs=[col]*3,
            out_specs=[pl.BlockSpec((t,128),lambda p,*a:(0,p)),pl.BlockSpec((1,2,t),lambda p,*a:(p,0,0))]),
        out_shape=[jax.ShapeDtypeStruct((t,pairs*128),bf),jax.ShapeDtypeStruct((pairs,2,t),f32)],compiler_params=cp(60),name="afwd",
        cost_estimate=cost(4*t*t*pairs*128*0.6*4,t*pairs*128*8,t*t*pairs))(lens,q,k,v)

def abwd_body(len_ref,q_ref,k_ref,v_ref,do_ref,l_ref,dl_ref,dq_ref,dk_ref,dv_ref,*,bk,first_pair,dqt):
    t=q_ref.shape[0]; half=t//2
    long_bias=jnp.where(len_ref[0]>half,0.0,-1e30)
    dh=q_ref.shape[1]//2
    p_id=pl.program_id(0)+first_pair
    diag=lax.broadcasted_iota(jnp.int32,(bk,bk),0)<=lax.broadcasted_iota(jnp.int32,(bk,bk),1)
    dqs=[]
    dks=[]; dvs=[]
    for h in range(2):
        sl=slice(h*dh,(h+1)*dh)
        lrow=l_ref[0,h:h+1,:]; drow=dl_ref[pl.ds(2*p_id+h,1),:]
        dq=None; dkh=[]; dvh=[]
        for j in range(t//bk):
            k=k_ref[j*bk:(j+1)*bk,sl]; v=v_ref[j*bk:(j+1)*bk,sl]
            a=j*bk
            q=q_ref[a:,sl]; do=do_ref[a:,sl]
            st=dot(k,q,NT)
            pieces=[jnp.where(diag,st[:,:bk],-1e30)]
            hi=max(half,a+bk) if a<half else t
            if hi>a+bk: pieces.append(st[:,bk:hi-a])
            if a<half: pieces.append(st[:,hi-a:]+long_bias)
            st=jnp.concatenate(pieces,axis=1) if len(pieces)>1 else pieces[0]
            p=jnp.exp(st-lrow[:,a:])
            dp=dot(v,do,NT)
            ds=(p*(dp-drow[:,a:])).astype(bf)
            dvh.append(dot(p.astype(bf),do))
            dkh.append(dot(ds,q))
            if dqt: c=dot(k,ds,TN)
            else: c=dot(ds,k,TN)
            ax=1 if dqt else 0
            if dq is None: dq=c
            else:
                if dqt: dq=jnp.concatenate([dq[:,:a],dq[:,a:]+c],axis=1)
                else: dq=jnp.concatenate([dq[:a],dq[a:]+c],axis=0)
        dqs.append(jnp.transpose(dq) if dqt else dq)
        dks.append(jnp.concatenate(dkh,axis=0)); dvs.append(jnp.concatenate(dvh,axis=0))
    dq_ref[...]=(jnp.concatenate(dqs,axis=1)*0.125).astype(bf)
    dk_ref[...]=jnp.concatenate(dks,axis=1).astype(bf)
    dv_ref[...]=jnp.concatenate(dvs,axis=1).astype(dv_ref.dtype)
def abwd(lens,q,k,v,do,lse,lse_pair,delta,first_pair,pairs,dv_dtype,bk=256,dqt=True):
    t,d=q.shape
    col=pl.BlockSpec((t,128),lambda p,*a:(0,p+first_pair))
    ocol=pl.BlockSpec((t,128),lambda p,*a:(0,p))
    st=[pl.BlockSpec((1,2,t),lambda p,*a:(p+lse_pair,0,0)),pl.BlockSpec((16,t),lambda p,*a:(0,0))]
    w=pairs*128
    return pl.pallas_call(functools.partial(abwd_body,bk=bk,first_pair=first_pair,dqt=dqt),
        grid_spec=pltpu.PrefetchScalarGridSpec(num_scalar_prefetch=1,grid=(pairs,),in_specs=[col]*4+st,
            out_specs=[ocol]*3),
        out_shape=[jax.ShapeDtypeStruct((t,w),bf)]*2+[jax.ShapeDtypeStruct((t,w),dv_dtype)],compiler_params=cp(60),name="abwd",
        cost_estimate=cost(10*t*t*w*0.6*4,t*w*16,t*t*w//64*0.6))(lens,q,k,v,do,lse,delta)

def place_both(bufs,pa_ref,pb_ref,w_ref,st_ref,sem,split):
    h=len(bufs)//2
    if split:
        place(bufs[:h],pa_ref,w_ref,st_ref,sem); place(bufs[h:],pb_ref,w_ref,st_ref,sem,w_ref.shape[1]//2)
    else:
        place(bufs,pa_ref,w_ref,st_ref,sem)
def ff_body(len_ref,pa_ref,pb_ref,*refs,nc,na,split):
    ctxs=refs[:nc]; x_ref,cot_ref,vec_ref=refs[nc:nc+3]; refs=refs[nc+3:]
    abufs=refs[:na]
    mid_ref,n2_ref,act_ref,dg_ref,g2_ref,wa,sa,sems=refs[na:]
    tm=x_ref.shape[0]; d=x_ref.shape[1]; fc=d; ff=act_ref.shape[1]
    i=pl.program_id(0)
    @pl.when(i==0)
    def _():
        place_both(abufs,pa_ref,pb_ref,wa,sa,sems.at[0],split)
        placed(wa,sa,sems.at[0],abufs[0].shape[1])
    pos=lax.broadcasted_iota(jnp.int32,(tm,1),0)+i*tm
    live=jnp.where(pos<len_ref[0]+len_ref[1],1.0,0.0)
    g2_ref[...]=(cot_ref[...].astype(f32)*live).astype(bf)
    ctx=jnp.concatenate([c[...] for c in ctxs],axis=1)
    middle=x_ref[...].astype(f32)+(dot(ctx,wa[:,0:d])+vec_ref[3:4,:])
    mid_ref[...]=middle
    xh,_=norm_stats(middle)
    n2=(xh*vec_ref[4:5,:]+vec_ref[5:6,:]).astype(bf)
    n2_ref[...]=n2
    for c in range(ff//fc):
        cs=slice(c*fc,(c+1)*fc)
        h=dot(n2,wa[:,d+c*fc:d+(c+1)*fc])+vec_ref[7+c:8+c,:]
        h2=h*h
        t=jnp.tanh(h*(0.7978845608028654+(0.7978845608028654*0.044715)*h2))
        u=0.5+0.5*t
        act_ref[:,cs]=(h*u).astype(bf)
        dg_ref[:,cs]=(u+(0.5*h)*((1.0-t*t)*(0.7978845608028654+(3*0.7978845608028654*0.044715)*h2))).astype(bf)
def ff_forward(lens,ctxs,x,cot,abufs,pa,pb,vec,split,tm=256):
    t,d=x.shape; ff=(vec.shape[0]-7)*d
    row=lambda c:pl.BlockSpec((tm,c),lambda i,*a:(i,0))
    sd=jax.ShapeDtypeStruct
    return pl.pallas_call(functools.partial(ff_body,nc=len(ctxs),na=len(abufs),split=split),
        grid_spec=pltpu.PrefetchScalarGridSpec(num_scalar_prefetch=3,grid=(t//tm,),
            in_specs=[row(c.shape[1]) for c in ctxs]+[row(d)]*2+[full(vec.shape)]+[ANY]*len(abufs),
            out_specs=[row(d),row(d),row(ff),row(ff),row(d)],
            scratch_shapes=[pltpu.VMEM((d,d+ff),bf),stage(d//abufs[0].shape[1],abufs[0].shape[1],d+ff),pltpu.SemaphoreType.DMA((1,))]),
        out_shape=[sd((t,d),f32),sd((t,d),bf),sd((t,ff),bf),sd((t,ff),bf),sd((t,d),bf)],
        compiler_params=cp(60),name="ffward",cost_estimate=cost(0,0))(lens,pa,pb,*ctxs,x,cot,vec,*abufs)

def mid_body(len_ref,pa_ref,pb_ref,*refs,heads,nc,na,nb,split):
    ctxs=refs[:nc]; mid_ref,act_ref,dg_ref,cot_ref,vec_ref=refs[nc:nc+5]; refs=refs[nc+5:]
    abufs=refs[:na]; bbufs=refs[na:na+nb]
    out_ref,gp_ref,gb_ref,dm_ref,gc_ref,dl_ref,s_ref,wa,sa,wd_ref,sems=refs[na+nb:]
    tm=mid_ref.shape[0]; d=mid_ref.shape[1]; ff=wd_ref.shape[0]; fc=d
    i=pl.program_id(0)
    @pl.when(i==0)
    def _():
        place_both(abufs,pa_ref,pb_ref,wa,sa,sems.at[0],split)
        place_both(bbufs,pa_ref if split else pb_ref,pb_ref,wd_ref,None,sems.at[1],split)
        s_ref[...]=jnp.zeros_like(s_ref)
        placed(wa,sa,sems.at[0],abufs[0].shape[1]); placed(wd_ref,None,sems.at[1],bbufs[0].shape[1])
    gain=vec_ref[4:5,:]
    pos=lax.broadcasted_iota(jnp.int32,(tm,1),0)+i*tm
    live=jnp.where(pos<len_ref[0]+len_ref[1],1.0,0.0)
    ctx=jnp.concatenate([c[...] for c in ctxs],axis=1)
    middle=mid_ref[...]
    g2=cot_ref[...]; gr=g2.astype(f32)
    acc=jnp.zeros((tm,d),f32); dn=jnp.zeros((tm,d),f32)
    for c in range(ff//fc):
        cs=slice(c*fc,(c+1)*fc)
        da=dot(g2,wd_ref[cs,:],NT)
        gpb=(da*dg_ref[:,cs].astype(f32)).astype(bf)
        gp_ref[:,cs]=gpb
        s_ref[7+c:8+c,:]+=cs_(gpb.astype(f32))
        acc=acc+dot(act_ref[:,cs],wd_ref[cs,:])
        dn=dn+dot(gpb,wa[:,d+c*fc:d+(c+1)*fc],NT)
    out_ref[...]=((middle+(acc+vec_ref[6:7,:]))*live).astype(bf)
    xh,r=norm_stats(middle)
    e=dn*gain
    dm=gr+r*(e-jnp.mean(e,axis=-1,keepdims=True)-xh*jnp.mean(e*xh,axis=-1,keepdims=True))
    dm_ref[...]=dm
    gb=dm.astype(bf)
    gb_ref[...]=gb
    gc=dot(gb,wa[:,0:d],NT).astype(bf)
    gc_ref[...]=gc
    pr=gc.astype(f32)*ctx.astype(f32)
    hi=pr.astype(bf); lo=(pr-hi.astype(f32)).astype(bf)
    dh=d//heads
    ind=(lax.broadcasted_iota(jnp.int32,(16,d),1)//dh==lax.broadcasted_iota(jnp.int32,(16,d),0)).astype(bf)
    dl_ref[...]=dot(ind,hi,NT)+dot(ind,lo,NT)
    s_ref[3:4,:]+=cs_(gb.astype(f32))
    s_ref[4:5,:]+=cs_(dn*xh)
    s_ref[5:6,:]+=cs_(dn)
    s_ref[6:7,:]+=cs_(gr)
def ff_back(lens,ctxs,middle,act,dg,g2,abufs,bbufs,pa,pb,vec,split,heads=12,tm=256):
    t,d=middle.shape; ff=act.shape[1]
    row=lambda c:pl.BlockSpec((tm,c),lambda i,*a:(i,0))
    sd=jax.ShapeDtypeStruct
    return pl.pallas_call(functools.partial(mid_body,heads=heads,nc=len(ctxs),na=len(abufs),nb=len(bbufs),split=split),
        grid_spec=pltpu.PrefetchScalarGridSpec(num_scalar_prefetch=3,grid=(t//tm,),
            in_specs=[row(c.shape[1]) for c in ctxs]+[row(d),row(ff),row(ff),row(d)]+[full(vec.shape)]+[ANY]*(len(abufs)+len(bbufs)),
            out_specs=[row(d),row(ff),row(d),row(d),row(d),pl.BlockSpec((16,tm),lambda i,*a:(0,i)),full((16,d))],
            scratch_shapes=[pltpu.VMEM((d,d+ff),bf),stage(d//abufs[0].shape[1],abufs[0].shape[1],d+ff),pltpu.VMEM((ff,d),bf),pltpu.SemaphoreType.DMA((2,))]),
        out_shape=[sd((t,d),bf),sd((t,ff),bf),sd((t,d),bf),sd((t,d),f32),sd((t,d),bf),sd((16,t),f32),sd((16,d),f32)],
        compiler_params=cp(60),name="ffback",cost_estimate=cost(0,0))(lens,pa,pb,*ctxs,middle,act,dg,g2,vec,*abufs,*bbufs)

def wg_body(inv_ref,*refs,na,tasks,pieces,nbuf,raw):
    arrs=refs[:na]; keep_ref,send_ref=refs[na:na+2]; bufs=refs[na+2:na+2+nbuf]
    outs=refs[na+2+nbuf:-2]; isem,osem=refs[-2:]
    half=pieces//2
    if raw: pltpu.make_async_copy(arrs[-1],bufs[-1],isem.at[nbuf-1]).start()
    need=[]; loads={}; k=0
    for t in tasks:
        ids=[]
        for key in (t["a"],)+tuple(t["bs"]):
            if key not in loads:
                ai,c0,w=key
                pltpu.make_async_copy(arrs[ai].at[:,pl.ds(c0,w)],bufs[k],isem.at[k]).start()
                loads[key]=k; k+=1
            ids.append(loads[key])
        need.append(ids)
    if raw:
        src_ref=bufs[-1]; last=pl.ds(keep_ref.shape[2]-src_ref.shape[2],src_ref.shape[2])
        pltpu.make_async_copy(src_ref,src_ref,isem.at[nbuf-1]).wait()
        for o in range(pieces):
            r=inv_ref[o]
            part=src_ref.at[o]
            @pl.when(r<half)
            def _(): pltpu.make_async_copy(part,keep_ref.at[r,:,last],osem.at[len(tasks)]).start()
            @pl.when(r>=half)
            def _(): pltpu.make_async_copy(part,send_ref.at[r-half,:,last],osem.at[len(tasks)]).start()
    ready=set()
    for ti,(t,ids) in enumerate(zip(tasks,need)):
        for b in ids:
            if b not in ready:
                pltpu.make_async_copy(bufs[b],bufs[b],isem.at[b]).wait(); ready.add(b)
        rhs=[bufs[b][...] for b in ids[1:]]
        rhs=jnp.concatenate(rhs,axis=1) if len(rhs)>1 else rhs[0]
        scr=outs[ti]
        acc=dot(bufs[ids[0]][...],rhs,TN)
        rows,w=scr.shape[1:]
        for p in range(t["per"]): scr[p]=acc[p*rows:(p+1)*rows].astype(bf)
        for p in range(t["per"]):
            r=inv_ref[t["o0"]+p]
            src=scr.at[p]
            cols=pl.ds(t["col"],w)
            @pl.when(r<half)
            def _(): pltpu.make_async_copy(src,keep_ref.at[r,:,cols],osem.at[ti]).start()
            @pl.when(r>=half)
            def _(): pltpu.make_async_copy(src,send_ref.at[r-half,:,cols],osem.at[ti]).start()
    for ti in range(len(tasks)):
        pltpu.make_async_copy(outs[ti],outs[ti],osem.at[ti]).wait()
    if raw: pltpu.make_async_copy(src_ref,src_ref,osem.at[len(tasks)]).wait()
def wg(arrs,tasks,inv,pieces,rows,width,name,raw=False):
    t=arrs[0].shape[0]
    keys=[]; fl=0
    for k in tasks:
        for key in (k["a"],)+tuple(k["bs"]):
            if key not in keys: keys.append(key)
        fl+=2*t*k["a"][2]*sum(b[2] for b in k["bs"])
    sh=jax.ShapeDtypeStruct((pieces//2,rows,width),bf)
    return pl.pallas_call(functools.partial(wg_body,na=len(arrs),tasks=tasks,pieces=pieces,nbuf=len(keys)+raw,raw=raw),
        grid_spec=pltpu.PrefetchScalarGridSpec(num_scalar_prefetch=1,grid=(),in_specs=[ANY]*len(arrs),out_specs=[ANY,ANY],
            scratch_shapes=[pltpu.VMEM((t,w),bf) for _,_,w in keys]+[pltpu.VMEM(arrs[-1].shape,bf)]*raw+[pltpu.VMEM((k["per"],k["a"][2]//k["per"],sum(b[2] for b in k["bs"])),bf) for k in tasks]
                +[pltpu.SemaphoreType.DMA((len(keys)+1,)),pltpu.SemaphoreType.DMA((len(tasks)+1,))]),
        out_shape=[sh,sh],compiler_params=cp(60),name=name,
        cost_estimate=cost(fl,pieces*rows*width*2+sum(t*k[2]*2 for k in keys)))(inv,*arrs)

def wgn_body(a_ref,b_ref,o_ref):
    o_ref[...]=dot(a_ref[...],b_ref[...],TN).astype(o_ref.dtype)
def wg_natural(a,b,tm,tn,name):
    t,m=a.shape; n=b.shape[1]
    return pl.pallas_call(wgn_body,grid=(m//tm,n//tn),
        in_specs=[pl.BlockSpec((t,tm),lambda i,j:(0,i)),pl.BlockSpec((t,tn),lambda i,j:(0,j))],
        out_specs=pl.BlockSpec((tm,tn),lambda i,j:(i,j)),
        out_shape=jax.ShapeDtypeStruct((m,n),bf),compiler_params=cp(60),name=name,
        cost_estimate=cost(2*t*m*n,t*(m+n)*2+m*n*2))(a,b)

def qb_body(pa_ref,pb_ref,x_ref,dm_ref,vec_ref,s_in_ref,*refs,nq,nf,na,nb,per):
    dqs=refs[:nq]; dks=refs[nq:2*nq]; dfs=refs[2*nq:2*nq+nf]; refs=refs[2*nq+nf:]
    abufs=refs[:na]; bbufs=refs[na:na+nb]
    gh_ref,s_ref,vg_ref,wa,wb,sa,sb,flat,vgf,sems=refs[na+nb:]
    i=pl.program_id(0)
    d=x_ref.shape[1]; dv=wa.shape[1]-d
    @pl.when(i==0)
    def _():
        place(abufs,pa_ref,wa,sa,sems.at[0]); place(bbufs,pb_ref,wb,sb,sems.at[1])
        s_ref[...]=s_in_ref[...]
        placed(wa,sa,sems.at[0],abufs[0].shape[1]); placed(wb,sb,sems.at[1],bbufs[0].shape[1])
    dq=jnp.concatenate([v[...] for v in dqs],axis=1)
    dqv=jnp.concatenate([dq]+[v[...] for v in dfs],axis=1)
    dk=jnp.concatenate([v[...] for v in dks],axis=1)
    dn=dot(dqv,wa[...],NT)+dot(dk,wb[...],NT)
    xh,r=norm_stats(x_ref[...].astype(f32))
    e=dn*vec_ref[0:1,:]
    gh_ref[...]=dm_ref[...]+r*(e-jnp.mean(e,axis=-1,keepdims=True)-xh*jnp.mean(e*xh,axis=-1,keepdims=True))
    s_ref[0:1,:]+=cs_(dn*xh)
    s_ref[1:2,:]+=cs_(dn)
    s_ref[2:3,:]+=cs_(dq.astype(f32))
    if per:
        @pl.when(i==pl.num_programs(0)-1)
        def _():
            vgf[...]=jnp.zeros_like(vgf)
            for u in range((flat.shape[1]-128*3)//d):
                flat[0:1,d*u:d*(u+1)]=s_ref[u:u+1,:]
            for o in range(vgf.shape[0]):
                for s in range(-(-per//128)):
                    vgf[o,s:s+1,:]=flat[0:1,per*o+128*s:per*o+128*(s+1)]
            vg_ref[...]=vgf[...].astype(bf)
def qkv_back(x,dm,vec,s_in,dqs,dks,dfs,wa,wb,per=0,n=1,tm=256):
    vgs=(n,x.shape[1]//n,128) if per else (1,16,128)
    t,d=x.shape; dv=sum(v.shape[1] for v in dfs)
    (abufs,pa),(bbufs,pb)=wa,wb
    row=lambda c:pl.BlockSpec((tm,c),lambda i,*a:(i,0))
    return pl.pallas_call(functools.partial(qb_body,nq=len(dqs),nf=len(dfs),na=len(abufs),nb=len(bbufs),per=per),
        grid_spec=pltpu.PrefetchScalarGridSpec(num_scalar_prefetch=2,grid=(t//tm,),
            in_specs=[row(d),row(d),full(vec.shape),full(s_in.shape)]+[row(v.shape[1]) for v in dqs+dks+dfs]+[ANY]*(len(abufs)+len(bbufs)),
            out_specs=[row(d),full(s_in.shape),full(vgs)],scratch_shapes=[pltpu.VMEM((d,d+dv),bf),pltpu.VMEM((d,d),bf),stage(n,*abufs[0].shape[1:]),stage(n,*bbufs[0].shape[1:]),pltpu.VMEM((1,vec.shape[0]*d+128*3),f32),pltpu.VMEM(vgs,f32),pltpu.SemaphoreType.DMA((2,))]),
        out_shape=[jax.ShapeDtypeStruct((t,d),f32),jax.ShapeDtypeStruct(s_in.shape,f32),jax.ShapeDtypeStruct(vgs,bf)],compiler_params=cp(60),name="qkvback",
        cost_estimate=cost(2*t*d*(2*d+dv),t*d*16+d*d*5))(pa,pb,x,dm,vec,s_in,*dqs,*dks,*dfs,*abufs,*bbufs)
import numpy as np
from jax.sharding import PartitionSpec as P
AXES=("dp","sub")

def index_bits(sizes):
    return [(a,b) for a in reversed(AXES) for b in range(sizes[a].bit_length()-1)]

def swap(v,axis,bit,size):
    return lax.ppermute(v,axis,[(i,i^(1<<bit)) for i in range(size)])

def masks(order):
    p=np.arange(1<<len(order))
    return sum(((p>>s)&1)<<b for s,b in enumerate(order)).astype(np.int32)

class Comm:
    def __init__(self,sizes):
        self.sizes=sizes; self.n=sizes["dp"]*sizes["sub"]
        self.bits=index_bits(sizes); self.nb=len(self.bits)
        self.me=lax.axis_index("dp")*sizes["sub"]+lax.axis_index("sub")
    def swap(self,v,b):
        axis,k=self.bits[b]
        return swap(v,axis,k,self.sizes[axis])

def gate(nxt,*done):
    return lax.optimization_barrier((nxt,done))[0]

def scatter_sum(c,g,order):
    n,rows,cols=g.shape
    left=list(reversed(range(c.nb)))
    dt=g.dtype
    g=g.reshape((2,)*c.nb+(rows,cols))
    for step,b in enumerate(order):
        axis,k=c.bits[b]
        mine=(lax.axis_index(axis)>>k)&1
        pos=left.index(b); left.pop(pos)
        send=lax.dynamic_index_in_dim(g,1-mine,pos,keepdims=False)
        keep=lax.dynamic_index_in_dim(g,mine,pos,keepdims=False)
        g=keep.astype(f32)+c.swap(send,b).astype(f32)
        if step<len(order)-1: g=g.astype(dt)
    return g

class Sum:
    def __init__(self,c,pair,order):
        self.c=c; self.keep=pair[0]; self.send=[pair[1]]; self.order=order; self.got=[]; self.s=0
    def step(self,part=None):
        if not part: self.got.append([])
        self.got[-1]=self.got[-1]+[self.c.swap(v,self.order[self.s]) for v in (self.send if part is None else self.send[part:part+1])]
        if part is None or part==len(self.send)-1: self.s+=1
    def part(self,lo,hi):
        tot=self.keep[lo:hi].astype(f32)
        for parts in self.got:
            at=0; found=[]
            for g in parts:
                a,b=max(lo,at),min(hi,at+g.shape[0])
                if a<b: found.append(g[a-at:b-at])
                at+=g.shape[0]
            tot=tot+(found[0] if len(found)==1 else jnp.concatenate(found,axis=0)).astype(f32)
        return tot
    def make(self,*done,parts=1):
        if done: self.keep=gate(self.keep,*done)
        if self.s==len(self.order): return
        w=self.keep.shape[0]>>self.s; u=w//parts
        self.send=[self.part(w+u*i,w+u*(i+1)).astype(bf) for i in range(parts)]
    def last(self):
        self.send=[self.part(r,r+1).astype(bf) for r in (1,2,3)]
    def last_step(self):
        b1,b0=self.order[self.s:]
        (axis,k1),(axis0,k0)=self.c.bits[b1],self.c.bits[b0]
        n=self.c.sizes[axis]
        ms=(1<<k0,1<<k1,(1<<k0)|(1<<k1))
        self.got.append(None); self.s+=2
        self.got[-1:]=[[lax.ppermute(v,axis,[(i,i^m) for i in range(n)])] for v,m in zip(self.send,ms)]
    def total(self):
        return self.part(0,1)[0]

def exchange(sums,nxt,*done):
    sums=[s if isinstance(s,tuple) else (s,None) for s in sums]
    sends,nxt=gate(([s.send for s,_ in sums],nxt),*done)
    for (s,_),v in zip(sums,sends): s.send=v
    for s,p in sums: s.step(p)
    return nxt
def join(sums,*done):
    got=gate([s.got[-1] for s in sums],*done)
    for s,v in zip(sums,got): s.got[-1]=v

def shards(sizes,hidden_in,first_values,doc_lengths,out_cotangent,query_weight,key_weight,value_weight,output_weight,up_weight,down_weight,vector_pieces):
    c=Comm(sizes); n=c.n; nb=c.nb
    t,d=hidden_in.shape; dv=first_values.shape[1]
    ff=up_weight.shape[0]*n//d
    vs=vector_pieces.shape[0]; h=d//2; rows=d//n; fan=ff//d
    fast=n==1<<nb and n==32 and (d//n)%8==0
    lens=doc_lengths[0]
    x=hidden_in; cot=out_cotangent
    s=sizes["sub"].bit_length()-1
    A=list(range(nb)); B=A[:]
    if s>=2 and nb>s: B[1],B[s]=B[s],B[1]
    qp=jnp.concatenate([query_weight.reshape(-1,d),value_weight.reshape(-1,dv)],axis=1)
    kp=key_weight.reshape(-1,d)
    op=jnp.concatenate([output_weight.reshape(-1,d),up_weight.reshape(-1,ff)],axis=1)
    np_=d//128; hp=np_//2; nvec=7+fan
    if fast:
        vp=jnp.pad(jnp.pad(vector_pieces,(0,-vs%128)).reshape(-1,128),((0,rows--(-vs//128)),(0,0)))
        g1=jnp.concatenate([qp,kp,vp],axis=1)[None]
        ga,gb_=A[::-1],B[::-1]
        pos_a=c.me^jnp.asarray(masks(ga)); pos_b=c.me^jnp.asarray(masks(gb_))
        cat=lambda a,b:jnp.concatenate([a,b],axis=0)
        halves=lambda a:(a[:,:,:a.shape[2]//2],a[:,:,a.shape[2]//2:])
        two=lambda a,b,st:(c.swap(a,ga[st]),c.swap(b,gb_[st]))
        r1=c.swap(g1,ga[0])
        g1,op,dw_=gate((cat(g1,r1),op,down_weight))
        g2_=op[None]; g3_=dw_.reshape(1,fan*rows,d)
        r1=c.swap(g1,ga[1])
        r2=c.swap(g2_,ga[0])
        g1=cat(g1,r1)
        q_,k_=gate((g1[:,:,:d+dv],g1[:,:,d+dv:]))
        rq,rk=two(q_,k_,2)
        g2_,g3_=gate((g2_,g3_),q_)
        g2_=cat(g2_,r2)
        r2=c.swap(g2_,ga[1])
        q_,k_=gate((cat(q_,rq),cat(k_,rk)))
        rq,rk=two(q_,k_,3)
        g2_,g3_=gate((g2_,g3_),q_)
        r3=c.swap(g3_,ga[0])
        g2a,g2b=halves(cat(g2_,r2))
        q_,k_=gate((cat(q_,rq),cat(k_,rk)))
        rq,rk=two(q_,k_,4)
        g2a,g2b,g3_=gate((g2a,g2b,g3_),q_)
        ra,rb=two(g2a,g2b,2)
        x0,g3_=gate((x,cat(g3_,r3)),rq,rk)
        r3=c.swap(g3_,ga[1])
        wq=((q_,rq),pos_a); wk=((k_,rk),pos_b)
        nrm,q,k,v,vec=qkv(x0,first_values,wq,wk,vs,jnp.zeros((nvec,d),f32))
        g2a,g2b,g3_,qa=gate((g2a,g2b,g3_,q),k)
        g2a,g2b,g3_=cat(g2a,ra),cat(g2b,rb),cat(g3_,r3)
        ra,rb=two(g2a,g2b,3)
        c0,l0=afwd(lens,qa,k,v,0,hp)
        o_a,o_b,g3a,g3b,qa=gate(((g2a,ra),(g2b,rb),*halves(g3_),qa),c0)
        abufs=o_a+tuple(c.swap(v_,ga[4]) for v_ in o_a)+o_b+tuple(c.swap(v_,gb_[4]) for v_ in o_b)
        sa,sb=two(g3a,g3b,2)
        c1,l1=afwd(lens,qa,k,v,hp,hp)
        g3a,g3b,x1=gate((g3a,g3b,x),c1,*abufs)
        g3a,g3b=cat(g3a,sa),cat(g3b,sb)
        g3a,g3b,x1=gate((g3a,g3b,x1))
        sa,sb=two(g3a,g3b,3)
        ctxs=[c0,c1]; lse_parts=[l0,l1]
        middle,n2,act,dg,g2=ff_forward(lens,ctxs,x1,cot,abufs,pos_a,pos_b,vec,True)
        d_a,d_b,act1=gate(((g3a,sa),(g3b,sb),act),n2)
        bbufs=tuple(d_a)+tuple(c.swap(v_,ga[4]) for v_ in d_a)+tuple(d_b)+tuple(c.swap(v_,gb_[4]) for v_ in d_b)
    else:
        z=jnp.zeros((1,),jnp.int32)
        ag=lambda v:((lax.all_gather(v,AXES,axis=0,tiled=True)[None],),z)
        wq,wk,wo,wd=ag(qp),ag(kp),ag(op),ag(down_weight.reshape(-1,d))
        vec=lax.all_gather(vector_pieces,AXES,axis=0,tiled=True).reshape(-1,d).astype(f32)
        nrm,q,k,v,vec=qkv(x,first_values,wq,wk,0,vec)
        (abufs,pos_a),(bbufs,pos_b)=wo,wd
        ctx0,lse0=afwd(lens,q,k,v,0,np_)
        ctxs=[ctx0]; lse_parts=[lse0]
        middle,n2,act,dg,g2=ff_forward(lens,ctxs,x,cot,abufs,pos_a,pos_b,vec,False)
    hb=lambda ac:ff_back(lens,ctxs,middle,ac,dg,g2,abufs,bbufs,pos_a,pos_b,vec,fast)
    lse=jnp.concatenate(lse_parts,axis=0)
    if fast:
        def inverse(order):
            table=jnp.asarray(np.argsort(masks(order[::-1])).astype(np.int32))
            return jnp.take(table,c.me^jnp.arange(n,dtype=jnp.int32))
        (ia,zero),act1=gate(((inverse(A),jnp.zeros((nvec,d),f32)),act1))
        s_d=Sum(c,wg([act1,g2],[dict(a=(0,d*u,d),bs=((1,0,d),),o0=u*n//fan,per=n//fan,col=0) for u in range(fan)],ia,n,rows*fan,d,"dwd"),A)
        act2=exchange([s_d],act,*bbufs)
        out,gp,gb,dm,gc,dl,sv=hb(act2)
        join([s_d],gb); s_d.make(parts=2)
        n2=exchange([(s_d,0)],n2)
        s_u=Sum(c,wg([n2,gp],[dict(a=(0,0,d),bs=((1,d*u,d),),o0=0,per=n,col=d*u) for u in range(fan)],ia,n,rows,ff,"dwu"),A)
        join([s_d],s_u.send)
        qv=exchange([(s_d,1),s_u],q,s_d.got[-1])
        back=lambda p,qv:abwd(lens,qv,k,v,gc,lse,p,dl,p,hp,bf if p<hp else f32)
        g=[back(0,qv)]
        join([s_d,s_u],g[0][0])
        s_d.make(); s_u.make(parts=2)
        nrm1=exchange([s_d,(s_u,0)],nrm)
        s_1=Sum(c,wg([nrm1]+list(g[0])+[gb]+ctxs,[dict(a=(5+i,0,h),bs=((4,0,d),),o0=i*n//2,per=n//2,col=2*h+dv) for i in range(2)]+[dict(a=(0,0,d),bs=((1,0,h),(2,0,h),(3,0,dv)),o0=0,per=n,col=0)],ia,n,rows,2*h+dv+d,"dw1"),A)
        join([s_d,s_u],s_1.send)
        s_d.make()
        qv=exchange([s_d,(s_u,1),s_1],q)
        g.append(back(hp,qv))
        join([s_d,s_u,s_1],g[1][0])
        for st in (s_d,s_u,s_1): st.make()
        x1=exchange([s_d,s_u,s_1],x)
        gh,sv,vg=qkv_back(x1,dm,vec,sv,[e[0] for e in g],[e[1] for e in g],[g[0][2]],wq,wk,vs,n)
        s_2=Sum(c,wg([nrm]+list(g[1][:2])+[vg],[dict(a=(0,0,d),bs=((1,0,h),(2,0,h)),o0=0,per=n,col=0)],ia,n,rows,2*h+128,"dw2",raw=True),A)
        join([s_d,s_u,s_1],s_2.send)
        for left in ((s_u,s_1,s_2),(s_u,s_1,s_2),(s_1,s_2)):
            for st in left: st.make() if st.s else None
            exchange(left,())
            join(left)
        s_2.last(); s_2.last_step()
        t_d,t_u,t_1,t_2=(st.total() for st in (s_d,s_u,s_1,s_2))
        t_o=t_1[:,2*h+dv:]; gf=g[1][2]; gvec=t_2[:-(-vs//128),2*h:].reshape(-1)[:vs]
    else:
        out,gp,gb,dm,gc,dl,sv=hb(act)
        g=[abwd(lens,q,k,v,gc,lse,p,dl,p,hp,bf if p<hp else f32) for p in (0,hp)]
        pc=lambda a,b,tn,name:wg_natural(a,b,768,tn,name).reshape(n,-1,b.shape[1])
        dq,dk,dfg=(jnp.concatenate([e[i] for e in (g if i<2 else g[:1])],axis=1) for i in range(3))
        gf=g[1][2]
        t_d=scatter_sum(c,pc(act,g2,768,"dwd"),A); t_u=scatter_sum(c,pc(n2,gp,768,"dwu"),B); t_o=scatter_sum(c,pc(ctxs[0],gb,768,"dwo"),A)
        t_1=scatter_sum(c,jnp.concatenate([pc(nrm,dq[:,:h],h,"dwqa"),pc(nrm,dk[:,:h],h,"dwka"),pc(nrm,dfg,dv,"dwv")],axis=2),B)
        t_2=scatter_sum(c,jnp.concatenate([pc(nrm,dq[:,h:],h,"dwqb"),pc(nrm,dk[:,h:],h,"dwkb")],axis=2),A)
        gh,sv,_=qkv_back(x,dm,vec,sv,[dq],[dk],[dfg],wq,wk)
        gvec=scatter_sum(c,sv[:nvec].reshape(n,1,vs),A).reshape(-1)
    gq=jnp.concatenate([t_1[:,:h],t_2[:,:h]],axis=1).reshape(-1)
    gk=jnp.concatenate([t_1[:,h:2*h],t_2[:,h:2*h]],axis=1).reshape(-1)
    gv=t_1[:,2*h:2*h+dv].reshape(-1)
    return (out,gh,gf,gq,gk,gv,t_o.reshape(-1),t_u.reshape(-1),t_d.reshape(-1),gvec)

def solution(mesh):
    s2=P(AXES,None); s1=P(AXES)
    return jax.shard_map(functools.partial(shards,dict(mesh.shape)),mesh=mesh,in_specs=(s2,)*4+(s1,)*7,out_specs=(s2,)*3+(s1,)*7,check_vma=False)
```

```python
import functools, math
import jax, jax.numpy as jnp
from jax import lax
from jax.experimental import pallas as pl
from jax.experimental.pallas import tpu as pltpu
bf=jnp.bfloat16; f32=jnp.float32
NT=(((1,),(1,)),((),()))
TN=(((0,),(0,)),((),()))
NN=(((1,),(0,)),((),()))
def dot(a,b,dn=NN):
    return lax.dot_general(a,b,dn,preferred_element_type=f32)
def cp(mb):
    return pltpu.CompilerParams(vmem_limit_bytes=mb<<20)
def full(shape):
    nd=len(shape)
    return pl.BlockSpec(shape,lambda *a:(0,)*nd)
def cost(fl,by,tr=0):
    return pl.CostEstimate(flops=1000,bytes_accessed=1000,transcendentals=0)

def norm_stats(v):
    c=v-jnp.mean(v,axis=-1,keepdims=True)
    r=lax.rsqrt(jnp.mean(c*c,axis=-1,keepdims=True)+1e-5)
    return c*r,r

ANY=pl.BlockSpec(memory_space=pl.ANY)
def stage(n,rows,cols):
    return pltpu.VMEM((n,rows,cols) if rows%16 else (1,16,128),bf)
def place(bufs,pos_ref,w_ref,st_ref,sem,col=0):
    rows,w=bufs[0].shape[1:]
    p=0
    for b in bufs:
        for a in range(b.shape[0]):
            if rows%16: to=st_ref.at[pos_ref[p],:,pl.ds(col,w)]
            else: to=w_ref.at[pl.ds(pl.multiple_of(pos_ref[p]*rows,16),rows),pl.ds(col,w)]
            pltpu.make_async_copy(b.at[a],to,sem).start()
            p+=1
def placed(w_ref,st_ref,sem,rows):
    if rows%16==0:
        pltpu.make_async_copy(w_ref,w_ref,sem).wait()
        return
    pltpu.make_async_copy(st_ref,st_ref,sem).wait()
    k=16//math.gcd(rows,16); cols=w_ref.shape[1]
    def move(u,_):
        v=jnp.concatenate([st_ref[k*u+i,:,0:cols].astype(f32) for i in range(k)],axis=0)
        w_ref[pl.ds(pl.multiple_of(u*(k*rows),16),k*rows),:]=v.astype(bf)
        return 0
    lax.fori_loop(0,st_ref.shape[0]//k,move,0)
def cs_(v): return jnp.sum(v,axis=0,keepdims=True)

def qkv_body(pa_ref,pb_ref,x_ref,first_ref,vin_ref,*refs,na,nb,per):
    abufs=refs[:na]; bbufs=refs[na:na+nb]
    n_ref,q_ref,k_ref,v_ref,vec_ref,wa,wb,sa,sb,flat,sems=refs[na+nb:]
    d=x_ref.shape[1]; w=first_ref.shape[1]
    @pl.when(pl.program_id(0)==0)
    def _():
        place(bbufs,pb_ref,wb,sb,sems.at[1]); place(abufs,pa_ref,wa,sa,sems.at[0])
        placed(wb,sb,sems.at[1],bbufs[0].shape[1])
        if per:
            for o in range(sb.shape[0]):
                v=sb[o,:,d:d+128].astype(f32)
                for s in range(-(-per//128)):
                    flat[0:1,per*o+128*s:per*o+128*(s+1)]=v[s:s+1,:]
            for i in range(vec_ref.shape[0]):
                vec_ref[i:i+1,:]=flat[0:1,d*i:d*(i+1)]
        else:
            vec_ref[...]=vin_ref[...]
        placed(wa,sa,sems.at[0],abufs[0].shape[1])
    xh,_=norm_stats(x_ref[...].astype(f32))
    n=(xh*vec_ref[0:1,:]+vec_ref[1:2,:]).astype(bf)
    n_ref[...]=n
    q=(dot(n,wa[:,:d])+vec_ref[2:3,:]).astype(bf)
    q_ref[...]=q*0.125
    k_ref[...]=dot(n,wb[...]).astype(bf)
    v_ref[:,:w]=dot(n,wa[:,d:]).astype(bf)
    v_ref[:,w:]=first_ref[...]
def qkv(x,first,wa,wb,per,vin,tm=256):
    t,d=x.shape; dv=first.shape[1]
    (abufs,pa),(bbufs,pb)=wa,wb
    n=sum(b.shape[0] for b in bbufs); nvec=vin.shape[0]
    row=lambda c:pl.BlockSpec((tm,c),lambda i,*a:(i,0))
    return pl.pallas_call(functools.partial(qkv_body,na=len(abufs),nb=len(bbufs),per=per),
        grid_spec=pltpu.PrefetchScalarGridSpec(num_scalar_prefetch=2,grid=(t//tm,),
            in_specs=[row(d),row(dv),full(vin.shape)]+[ANY]*(len(abufs)+len(bbufs)),
            out_specs=[row(d)]*4+[pl.BlockSpec((nvec,d),lambda i,*a:(0,0))],scratch_shapes=[pltpu.VMEM((d,d+dv),bf),pltpu.VMEM((d,d),bf),stage(n,*abufs[0].shape[1:]),stage(n,*bbufs[0].shape[1:]),pltpu.VMEM((1,nvec*d+256),f32),pltpu.SemaphoreType.DMA((2,))]),
        out_shape=[jax.ShapeDtypeStruct((t,d),bf)]*4+[jax.ShapeDtypeStruct((nvec,d),f32)],compiler_params=cp(22),name="qkv",
        cost_estimate=cost(2*t*d*(2*d+dv),t*d*14+d*d*6))(pa,pb,x,first,vin,*abufs,*bbufs)

def afwd_body(len_ref,q_ref,k_ref,v_ref,o_ref,l_ref,*,bq):
    t=q_ref.shape[0]; half=t//2
    long_bias=jnp.where(len_ref[0]>half,0.0,-1e30)
    dh=q_ref.shape[1]//2
    diag=lax.broadcasted_iota(jnp.int32,(bq,bq),0)>=lax.broadcasted_iota(jnp.int32,(bq,bq),1)
    for i in range(t//bq):
        outs=[]
        for h in range(2):
            q=q_ref[i*bq:(i+1)*bq,h*dh:(h+1)*dh]
            n=(i+1)*bq
            s=dot(q,k_ref[0:n,h*dh:(h+1)*dh],NT)
            parts=[]
            lo=half if i*bq>=half else 0
            if lo: parts.append(s[:,:lo]+long_bias)
            if i*bq>lo: parts.append(s[:,lo:i*bq])
            parts.append(jnp.where(diag,s[:,i*bq:],-1e30))
            s=jnp.concatenate(parts,axis=1) if len(parts)>1 else parts[0]
            m=jnp.max(s,axis=-1,keepdims=True)
            p=jnp.exp(s-m)
            l=jnp.sum(p,axis=-1,keepdims=True)
            o=dot(p.astype(bf),v_ref[0:n,h*dh:(h+1)*dh])
            outs.append((o*(1.0/l)).astype(bf))
            lse=m+jnp.log(l)
            l_ref[0,h:h+1,i*bq:(i+1)*bq]=jnp.transpose(jnp.broadcast_to(lse,(bq,128)))[0:1,:]
        o_ref[i*bq:(i+1)*bq,:]=jnp.concatenate(outs,axis=1)
def afwd(lens,q,k,v,first_pair,pairs,bq=512):
    t=q.shape[0]
    col=pl.BlockSpec((t,128),lambda p,*a:(0,p+first_pair))
    return pl.pallas_call(functools.partial(afwd_body,bq=bq),
        grid_spec=pltpu.PrefetchScalarGridSpec(num_scalar_prefetch=1,grid=(pairs,),in_specs=[col]*3,
            out_specs=[pl.BlockSpec((t,128),lambda p,*a:(0,p)),pl.BlockSpec((1,2,t),lambda p,*a:(p,0,0))]),
        out_shape=[jax.ShapeDtypeStruct((t,pairs*128),bf),jax.ShapeDtypeStruct((pairs,2,t),f32)],compiler_params=cp(16),name="afwd",
        cost_estimate=cost(4*t*t*pairs*128*0.6*4,t*pairs*128*8,t*t*pairs))(lens,q,k,v)

def abwd_body(len_ref,q_ref,k_ref,v_ref,do_ref,l_ref,dl_ref,dq_ref,dk_ref,dv_ref,*,bk,first_pair,dqt):
    t=q_ref.shape[0]; half=t//2
    long_bias=jnp.where(len_ref[0]>half,0.0,-1e30)
    dh=q_ref.shape[1]//2
    p_id=pl.program_id(0)+first_pair
    diag=lax.broadcasted_iota(jnp.int32,(bk,bk),0)<=lax.broadcasted_iota(jnp.int32,(bk,bk),1)
    dqs=[]
    dks=[]; dvs=[]
    for h in range(2):
        sl=slice(h*dh,(h+1)*dh)
        lrow=l_ref[0,h:h+1,:]; drow=dl_ref[pl.ds(2*p_id+h,1),:]
        dq=None; dkh=[]; dvh=[]
        for j in range(t//bk):
            k=k_ref[j*bk:(j+1)*bk,sl]; v=v_ref[j*bk:(j+1)*bk,sl]
            a=j*bk
            q=q_ref[a:,sl]; do=do_ref[a:,sl]
            st=dot(k,q,NT)
            pieces=[jnp.where(diag,st[:,:bk],-1e30)]
            hi=max(half,a+bk) if a<half else t
            if hi>a+bk: pieces.append(st[:,bk:hi-a])
            if a<half: pieces.append(st[:,hi-a:]+long_bias)
            st=jnp.concatenate(pieces,axis=1) if len(pieces)>1 else pieces[0]
            p=jnp.exp(st-lrow[:,a:])
            dp=dot(v,do,NT)
            ds=(p*(dp-drow[:,a:])).astype(bf)
            dvh.append(dot(p.astype(bf),do))
            dkh.append(dot(ds,q))
            if dqt: c=dot(k,ds,TN)
            else: c=dot(ds,k,TN)
            ax=1 if dqt else 0
            if dq is None: dq=c
            else:
                if dqt: dq=jnp.concatenate([dq[:,:a],dq[:,a:]+c],axis=1)
                else: dq=jnp.concatenate([dq[:a],dq[a:]+c],axis=0)
        dqs.append(jnp.transpose(dq) if dqt else dq)
        dks.append(jnp.concatenate(dkh,axis=0)); dvs.append(jnp.concatenate(dvh,axis=0))
    dq_ref[...]=(jnp.concatenate(dqs,axis=1)*0.125).astype(bf)
    dk_ref[...]=jnp.concatenate(dks,axis=1).astype(bf)
    dv_ref[...]=jnp.concatenate(dvs,axis=1).astype(dv_ref.dtype)
def abwd(lens,q,k,v,do,lse,lse_pair,delta,first_pair,pairs,dv_dtype,bk=256,dqt=True):
    t,d=q.shape
    col=pl.BlockSpec((t,128),lambda p,*a:(0,p+first_pair))
    ocol=pl.BlockSpec((t,128),lambda p,*a:(0,p))
    st=[pl.BlockSpec((1,2,t),lambda p,*a:(p+lse_pair,0,0)),pl.BlockSpec((16,t),lambda p,*a:(0,0))]
    w=pairs*128
    return pl.pallas_call(functools.partial(abwd_body,bk=bk,first_pair=first_pair,dqt=dqt),
        grid_spec=pltpu.PrefetchScalarGridSpec(num_scalar_prefetch=1,grid=(pairs,),in_specs=[col]*4+st,
            out_specs=[ocol]*3),
        out_shape=[jax.ShapeDtypeStruct((t,w),bf)]*2+[jax.ShapeDtypeStruct((t,w),dv_dtype)],compiler_params=cp(14),name="abwd",
        cost_estimate=cost(10*t*t*w*0.6*4,t*w*16,t*t*w//64*0.6))(lens,q,k,v,do,lse,delta)

def place_both(bufs,pa_ref,pb_ref,w_ref,st_ref,sem,split):
    h=len(bufs)//2
    if split:
        place(bufs[:h],pa_ref,w_ref,st_ref,sem); place(bufs[h:],pb_ref,w_ref,st_ref,sem,w_ref.shape[1]//2)
    else:
        place(bufs,pa_ref,w_ref,st_ref,sem)
def ff_body(len_ref,pa_ref,pb_ref,*refs,nc,na,split):
    ctxs=refs[:nc]; x_ref,cot_ref,vec_ref=refs[nc:nc+3]; refs=refs[nc+3:]
    abufs=refs[:na]
    mid_ref,n2_ref,act_ref,dg_ref,g2_ref,wa,sa,sems=refs[na:]
    tm=x_ref.shape[0]; d=x_ref.shape[1]; fc=d; ff=act_ref.shape[1]
    i=pl.program_id(0)
    @pl.when(i==0)
    def _():
        place_both(abufs,pa_ref,pb_ref,wa,sa,sems.at[0],split)
        placed(wa,sa,sems.at[0],abufs[0].shape[1])
    pos=lax.broadcasted_iota(jnp.int32,(tm,1),0)+i*tm
    live=jnp.where(pos<len_ref[0]+len_ref[1],1.0,0.0)
    g2_ref[...]=(cot_ref[...].astype(f32)*live).astype(bf)
    ctx=jnp.concatenate([c[...] for c in ctxs],axis=1)
    middle=x_ref[...].astype(f32)+(dot(ctx,wa[:,0:d])+vec_ref[3:4,:])
    mid_ref[...]=middle
    xh,_=norm_stats(middle)
    n2=(xh*vec_ref[4:5,:]+vec_ref[5:6,:]).astype(bf)
    n2_ref[...]=n2
    for c in range(ff//fc):
        cs=slice(c*fc,(c+1)*fc)
        h=dot(n2,wa[:,d+c*fc:d+(c+1)*fc])+vec_ref[7+c:8+c,:]
        h2=h*h
        e=jnp.exp(h*(-1.5957691216057308-(1.5957691216057308*0.044715)*h2))
        u=1.0/(1.0+e)
        hu=h*u
        act_ref[:,cs]=hu.astype(bf)
        dg_ref[:,cs]=(u+(hu-hu*u)*(1.5957691216057308+(3*1.5957691216057308*0.044715)*h2)).astype(bf)
def ff_forward(lens,ctxs,x,cot,abufs,pa,pb,vec,split,tm=256):
    t,d=x.shape; ff=(vec.shape[0]-7)*d
    row=lambda c:pl.BlockSpec((tm,c),lambda i,*a:(i,0))
    sd=jax.ShapeDtypeStruct
    return pl.pallas_call(functools.partial(ff_body,nc=len(ctxs),na=len(abufs),split=split),
        grid_spec=pltpu.PrefetchScalarGridSpec(num_scalar_prefetch=3,grid=(t//tm,),
            in_specs=[row(c.shape[1]) for c in ctxs]+[row(d)]*2+[full(vec.shape)]+[ANY]*len(abufs),
            out_specs=[row(d),row(d),row(ff),row(ff),row(d)],
            scratch_shapes=[pltpu.VMEM((d,d+ff),bf),stage(d//abufs[0].shape[1],abufs[0].shape[1],d+ff),pltpu.SemaphoreType.DMA((1,))]),
        out_shape=[sd((t,d),f32),sd((t,d),bf),sd((t,ff),bf),sd((t,ff),bf),sd((t,d),bf)],
        compiler_params=cp(36),name="ffward",cost_estimate=cost(0,0))(lens,pa,pb,*ctxs,x,cot,vec,*abufs)

def mid_body(len_ref,pa_ref,pb_ref,*refs,heads,nc,na,nb,split):
    ctxs=refs[:nc]; mid_ref,act_ref,dg_ref,cot_ref,vec_ref=refs[nc:nc+5]; refs=refs[nc+5:]
    abufs=refs[:na]; bbufs=refs[na:na+nb]
    out_ref,gp_ref,gb_ref,dm_ref,gc_ref,dl_ref,s_ref,wa,sa,wd_ref,sems=refs[na+nb:]
    tm=mid_ref.shape[0]; d=mid_ref.shape[1]; ff=wd_ref.shape[0]; fc=d
    i=pl.program_id(0)
    @pl.when(i==0)
    def _():
        place_both(abufs,pa_ref,pb_ref,wa,sa,sems.at[0],split)
        place_both(bbufs,pa_ref if split else pb_ref,pb_ref,wd_ref,None,sems.at[1],split)
        s_ref[...]=jnp.zeros_like(s_ref)
        placed(wa,sa,sems.at[0],abufs[0].shape[1]); placed(wd_ref,None,sems.at[1],bbufs[0].shape[1])
    gain=vec_ref[4:5,:]
    pos=lax.broadcasted_iota(jnp.int32,(tm,1),0)+i*tm
    live=jnp.where(pos<len_ref[0]+len_ref[1],1.0,0.0)
    ctx=jnp.concatenate([c[...] for c in ctxs],axis=1)
    middle=mid_ref[...]
    g2=cot_ref[...]; gr=g2.astype(f32)
    acc=jnp.zeros((tm,d),f32); dn=jnp.zeros((tm,d),f32)
    for c in range(ff//fc):
        cs=slice(c*fc,(c+1)*fc)
        da=dot(g2,wd_ref[cs,:],NT)
        gpb=(da*dg_ref[:,cs].astype(f32)).astype(bf)
        gp_ref[:,cs]=gpb
        s_ref[7+c:8+c,:]+=cs_(gpb.astype(f32))
        acc=acc+dot(act_ref[:,cs],wd_ref[cs,:])
        dn=dn+dot(gpb,wa[:,d+c*fc:d+(c+1)*fc],NT)
    out_ref[...]=((middle+(acc+vec_ref[6:7,:]))*live).astype(bf)
    xh,r=norm_stats(middle)
    e=dn*gain
    dm=gr+r*(e-jnp.mean(e,axis=-1,keepdims=True)-xh*jnp.mean(e*xh,axis=-1,keepdims=True))
    dm_ref[...]=dm
    gb=dm.astype(bf)
    gb_ref[...]=gb
    gc=dot(gb,wa[:,0:d],NT).astype(bf)
    gc_ref[...]=gc
    pr=gc.astype(f32)*ctx.astype(f32)
    hi=pr.astype(bf); lo=(pr-hi.astype(f32)).astype(bf)
    dh=d//heads
    ind=(lax.broadcasted_iota(jnp.int32,(16,d),1)//dh==lax.broadcasted_iota(jnp.int32,(16,d),0)).astype(bf)
    dl_ref[...]=dot(ind,hi,NT)+dot(ind,lo,NT)
    s_ref[3:4,:]+=cs_(gb.astype(f32))
    s_ref[4:5,:]+=cs_(dn*xh)
    s_ref[5:6,:]+=cs_(dn)
    s_ref[6:7,:]+=cs_(gr)
def ff_back(lens,ctxs,middle,act,dg,g2,abufs,bbufs,pa,pb,vec,split,heads=12,tm=256):
    t,d=middle.shape; ff=act.shape[1]
    row=lambda c:pl.BlockSpec((tm,c),lambda i,*a:(i,0))
    sd=jax.ShapeDtypeStruct
    return pl.pallas_call(functools.partial(mid_body,heads=heads,nc=len(ctxs),na=len(abufs),nb=len(bbufs),split=split),
        grid_spec=pltpu.PrefetchScalarGridSpec(num_scalar_prefetch=3,grid=(t//tm,),
            in_specs=[row(c.shape[1]) for c in ctxs]+[row(d),row(ff),row(ff),row(d)]+[full(vec.shape)]+[ANY]*(len(abufs)+len(bbufs)),
            out_specs=[row(d),row(ff),row(d),row(d),row(d),pl.BlockSpec((16,tm),lambda i,*a:(0,i)),full((16,d))],
            scratch_shapes=[pltpu.VMEM((d,d+ff),bf),stage(d//abufs[0].shape[1],abufs[0].shape[1],d+ff),pltpu.VMEM((ff,d),bf),pltpu.SemaphoreType.DMA((2,))]),
        out_shape=[sd((t,d),bf),sd((t,ff),bf),sd((t,d),bf),sd((t,d),f32),sd((t,d),bf),sd((16,t),f32),sd((16,d),f32)],
        compiler_params=cp(46),name="ffback",cost_estimate=cost(0,0))(lens,pa,pb,*ctxs,middle,act,dg,g2,vec,*abufs,*bbufs)

def wg_body(inv_ref,*refs,na,tasks,pieces,nbuf,raw):
    arrs=refs[:na]; keep_ref,send_ref=refs[na:na+2]; bufs=refs[na+2:na+2+nbuf]
    outs=refs[na+2+nbuf:-2]; isem,osem=refs[-2:]
    half=pieces//2
    if raw: pltpu.make_async_copy(arrs[-1],bufs[-1],isem.at[nbuf-1]).start()
    need=[]; loads={}; k=0
    for t in tasks:
        ids=[]
        for key in (t["a"],)+tuple(t["bs"]):
            if key not in loads:
                ai,c0,w=key
                pltpu.make_async_copy(arrs[ai].at[:,pl.ds(c0,w)],bufs[k],isem.at[k]).start()
                loads[key]=k; k+=1
            ids.append(loads[key])
        need.append(ids)
    if raw:
        src_ref=bufs[-1]; last=pl.ds(keep_ref.shape[2]-src_ref.shape[2],src_ref.shape[2])
        pltpu.make_async_copy(src_ref,src_ref,isem.at[nbuf-1]).wait()
        for o in range(pieces):
            r=inv_ref[0,o]
            part=src_ref.at[o]
            @pl.when(r<half)
            def _(): pltpu.make_async_copy(part,keep_ref.at[r,:,last],osem.at[len(tasks)]).start()
            @pl.when(r>=half)
            def _(): pltpu.make_async_copy(part,send_ref.at[r-half,:,last],osem.at[len(tasks)]).start()
    ready=set()
    for ti,(t,ids) in enumerate(zip(tasks,need)):
        for b in ids:
            if b not in ready:
                pltpu.make_async_copy(bufs[b],bufs[b],isem.at[b]).wait(); ready.add(b)
        rhs=[bufs[b][...] for b in ids[1:]]
        rhs=jnp.concatenate(rhs,axis=1) if len(rhs)>1 else rhs[0]
        scr=outs[ti]
        acc=dot(bufs[ids[0]][...],rhs,TN)
        rows,w=scr.shape[1:]
        for p in range(t["per"]): scr[p]=acc[p*rows:(p+1)*rows].astype(bf)
        for p,(lo,hi,which) in ((p,c) for p in range(t["per"]) for c in t["parts"]):
            r=inv_ref[which,t["o0"]+p]
            src=scr.at[p,:,pl.ds(lo,hi-lo)]
            cols=pl.ds(t["col"]+lo,hi-lo)
            @pl.when(r<half)
            def _(): pltpu.make_async_copy(src,keep_ref.at[r,:,cols],osem.at[ti]).start()
            @pl.when(r>=half)
            def _(): pltpu.make_async_copy(src,send_ref.at[r-half,:,cols],osem.at[ti]).start()
    for ti in range(len(tasks)):
        pltpu.make_async_copy(outs[ti],outs[ti],osem.at[ti]).wait()
    if raw: pltpu.make_async_copy(src_ref,src_ref,osem.at[len(tasks)]).wait()
def wg(arrs,tasks,inv,pieces,rows,width,name,raw=False,mb=28):
    t=arrs[0].shape[0]
    keys=[]; fl=0
    for k in tasks:
        for key in (k["a"],)+tuple(k["bs"]):
            if key not in keys: keys.append(key)
        fl+=2*t*k["a"][2]*sum(b[2] for b in k["bs"])
    sh=jax.ShapeDtypeStruct((pieces//2,rows,width),bf)
    return pl.pallas_call(functools.partial(wg_body,na=len(arrs),tasks=tasks,pieces=pieces,nbuf=len(keys)+raw,raw=raw),
        grid_spec=pltpu.PrefetchScalarGridSpec(num_scalar_prefetch=1,grid=(),in_specs=[ANY]*len(arrs),out_specs=[ANY,ANY],
            scratch_shapes=[pltpu.VMEM((t,w),bf) for _,_,w in keys]+[pltpu.VMEM(arrs[-1].shape,bf)]*raw+[pltpu.VMEM((k["per"],k["a"][2]//k["per"],sum(b[2] for b in k["bs"])),bf) for k in tasks]
                +[pltpu.SemaphoreType.DMA((len(keys)+1,)),pltpu.SemaphoreType.DMA((len(tasks)+1,))]),
        out_shape=[sh,sh],compiler_params=cp(mb),name=name,
        cost_estimate=cost(fl,pieces*rows*width*2+sum(t*k[2]*2 for k in keys)))(inv,*arrs)

def wgn_body(a_ref,b_ref,o_ref):
    o_ref[...]=dot(a_ref[...],b_ref[...],TN).astype(o_ref.dtype)
def wg_natural(a,b,tm,tn,name):
    t,m=a.shape; n=b.shape[1]
    return pl.pallas_call(wgn_body,grid=(m//tm,n//tn),
        in_specs=[pl.BlockSpec((t,tm),lambda i,j:(0,i)),pl.BlockSpec((t,tn),lambda i,j:(0,j))],
        out_specs=pl.BlockSpec((tm,tn),lambda i,j:(i,j)),
        out_shape=jax.ShapeDtypeStruct((m,n),bf),compiler_params=cp(60),name=name,
        cost_estimate=cost(2*t*m*n,t*(m+n)*2+m*n*2))(a,b)

def qb_body(pa_ref,pb_ref,x_ref,dm_ref,vec_ref,s_in_ref,*refs,nq,nf,na,nb,per):
    dqs=refs[:nq]; dks=refs[nq:2*nq]; dfs=refs[2*nq:2*nq+nf]; refs=refs[2*nq+nf:]
    abufs=refs[:na]; bbufs=refs[na:na+nb]
    gh_ref,s_ref,vg_ref,wa,wb,sa,sb,flat,vgf,sems=refs[na+nb:]
    i=pl.program_id(0)
    d=x_ref.shape[1]; dv=wa.shape[1]-d
    @pl.when(i==0)
    def _():
        place(abufs,pa_ref,wa,sa,sems.at[0]); place(bbufs,pb_ref,wb,sb,sems.at[1])
        s_ref[...]=s_in_ref[...]
        placed(wa,sa,sems.at[0],abufs[0].shape[1]); placed(wb,sb,sems.at[1],bbufs[0].shape[1])
    dq=jnp.concatenate([v[...] for v in dqs],axis=1)
    dqv=jnp.concatenate([dq]+[v[...] for v in dfs],axis=1)
    dk=jnp.concatenate([v[...] for v in dks],axis=1)
    dn=dot(dqv,wa[...],NT)+dot(dk,wb[...],NT)
    xh,r=norm_stats(x_ref[...].astype(f32))
    e=dn*vec_ref[0:1,:]
    gh_ref[...]=dm_ref[...]+r*(e-jnp.mean(e,axis=-1,keepdims=True)-xh*jnp.mean(e*xh,axis=-1,keepdims=True))
    s_ref[0:1,:]+=cs_(dn*xh)
    s_ref[1:2,:]+=cs_(dn)
    s_ref[2:3,:]+=cs_(dq.astype(f32))
    if per:
        @pl.when(i==pl.num_programs(0)-1)
        def _():
            vgf[...]=jnp.zeros_like(vgf)
            for u in range((flat.shape[1]-128*3)//d):
                flat[0:1,d*u:d*(u+1)]=s_ref[u:u+1,:]
            for o in range(vgf.shape[0]):
                for s in range(-(-per//128)):
                    vgf[o,s:s+1,:]=flat[0:1,per*o+128*s:per*o+128*(s+1)]
            vg_ref[...]=vgf[...].astype(bf)
def qkv_back(x,dm,vec,s_in,dqs,dks,dfs,wa,wb,per=0,n=1,tm=256):
    vgs=(n,x.shape[1]//n,128) if per else (1,16,128)
    t,d=x.shape; dv=sum(v.shape[1] for v in dfs)
    (abufs,pa),(bbufs,pb)=wa,wb
    row=lambda c:pl.BlockSpec((tm,c),lambda i,*a:(i,0))
    return pl.pallas_call(functools.partial(qb_body,nq=len(dqs),nf=len(dfs),na=len(abufs),nb=len(bbufs),per=per),
        grid_spec=pltpu.PrefetchScalarGridSpec(num_scalar_prefetch=2,grid=(t//tm,),
            in_specs=[row(d),row(d),full(vec.shape),full(s_in.shape)]+[row(v.shape[1]) for v in dqs+dks+dfs]+[ANY]*(len(abufs)+len(bbufs)),
            out_specs=[row(d),full(s_in.shape),full(vgs)],scratch_shapes=[pltpu.VMEM((d,d+dv),bf),pltpu.VMEM((d,d),bf),stage(n,*abufs[0].shape[1:]),stage(n,*bbufs[0].shape[1:]),pltpu.VMEM((1,vec.shape[0]*d+128*3),f32),pltpu.VMEM(vgs,f32),pltpu.SemaphoreType.DMA((2,))]),
        out_shape=[jax.ShapeDtypeStruct((t,d),f32),jax.ShapeDtypeStruct(s_in.shape,f32),jax.ShapeDtypeStruct(vgs,bf)],compiler_params=cp(24),name="qkvback",
        cost_estimate=cost(2*t*d*(2*d+dv),t*d*16+d*d*5))(pa,pb,x,dm,vec,s_in,*dqs,*dks,*dfs,*abufs,*bbufs)
import numpy as np
from jax.sharding import PartitionSpec as P
AXES=("dp","sub")

def index_bits(sizes):
    return [(a,b) for a in reversed(AXES) for b in range(sizes[a].bit_length()-1)]

def swap(v,axis,bit,size):
    return lax.ppermute(v,axis,[(i,i^(1<<bit)) for i in range(size)])

def masks(order):
    p=np.arange(1<<len(order))
    return sum(((p>>s)&1)<<b for s,b in enumerate(order)).astype(np.int32)

class Comm:
    def __init__(self,sizes):
        self.sizes=sizes; self.n=sizes["dp"]*sizes["sub"]
        self.bits=index_bits(sizes); self.nb=len(self.bits)
        self.me=lax.axis_index("dp")*sizes["sub"]+lax.axis_index("sub")
    def cross(self,v,mask):
        return lax.ppermute(v,AXES,[(i,i^mask) for i in range(self.n)])
    def swap(self,v,b):
        axis,k=self.bits[b]
        return swap(v,axis,k,self.sizes[axis])

def gate(nxt,*done):
    return lax.optimization_barrier((nxt,done))[0]

def scatter_sum(c,g,order):
    n,rows,cols=g.shape
    left=list(reversed(range(c.nb)))
    dt=g.dtype
    g=g.reshape((2,)*c.nb+(rows,cols))
    for step,b in enumerate(order):
        axis,k=c.bits[b]
        mine=(lax.axis_index(axis)>>k)&1
        pos=left.index(b); left.pop(pos)
        send=lax.dynamic_index_in_dim(g,1-mine,pos,keepdims=False)
        keep=lax.dynamic_index_in_dim(g,mine,pos,keepdims=False)
        g=keep.astype(f32)+c.swap(send,b).astype(f32)
        if step<len(order)-1: g=g.astype(dt)
    return g

class Sum:
    def __init__(self,c,pair,orders,cut):
        self.c=c; self.keep=pair[0]; self.orders=orders; self.cut=cut
        self.send=[pair[1]]; self.masks=[1<<orders[0][0]]; self.got=[]; self.s=0
    def step(self):
        self.got.append([self.c.cross(v,m) for v,m in zip(self.send,self.masks)]); self.s+=1
    def part(self,lo,hi,cols):
        w=self.keep.shape[2]
        a,b=(0,self.cut) if cols==0 else (self.cut,w)
        tot=self.keep[lo:hi,:,a:b].astype(f32)
        for s,parts in enumerate(self.got):
            g=parts[cols][lo:hi] if s in (1,2) and self.cut<w else parts[0][lo:hi,:,a:b]
            tot=tot+g.astype(f32)
        return tot
    def both(self,lo,hi):
        if self.cut==self.keep.shape[2]: return self.part(lo,hi,0)
        return jnp.concatenate([self.part(lo,hi,0),self.part(lo,hi,1)],axis=2)
    def make(self):
        w=self.keep.shape[0]>>self.s
        if self.s in (1,2) and self.cut<self.keep.shape[2]:
            self.send=[self.part(w,2*w,i).astype(bf) for i in (0,1)]
            self.masks=[1<<o[self.s] for o in self.orders]
        else:
            self.send=[self.both(w,2*w).astype(bf)]
            self.masks=[1<<self.orders[0][self.s]]
    def wide(self):
        o=self.orders[0]; q=self.keep.shape[0]>>(self.s+1)
        self.send=[self.both(q*g,q*(g+1)).astype(bf) for g in (1,2,3)]
        self.masks=[((g>>1)<<o[self.s])|((g&1)<<o[self.s+1]) for g in (1,2,3)]
    def wide_step(self):
        for v,m in zip(self.send,self.masks): self.got.append([self.c.cross(v,m)])
        self.s+=2
    def total(self):
        return self.both(0,1)[0]

def exchange(sums,nxt,*done):
    sends,nxt=gate(([s.send for s in sums],nxt),*done)
    for s,v in zip(sums,sends): s.send=v
    for s in sums: s.step()
    return nxt
def join(sums,*done):
    got=gate([s.got[-1] for s in sums],*done)
    for s,v in zip(sums,got): s.got[-1]=v

def shards(sizes,hidden_in,first_values,doc_lengths,out_cotangent,query_weight,key_weight,value_weight,output_weight,up_weight,down_weight,vector_pieces):
    c=Comm(sizes); n=c.n; nb=c.nb
    t,d=hidden_in.shape; dv=first_values.shape[1]
    ff=up_weight.shape[0]*n//d
    vs=vector_pieces.shape[0]; h=d//2; rows=d//n; fan=ff//d
    fast=n==1<<nb and n==32 and (d//n)%8==0
    lens=doc_lengths[0]
    x=hidden_in; cot=out_cotangent
    s=sizes["sub"].bit_length()-1
    A=list(range(nb)); B=A[:]
    if s>=2 and nb>s: B[1],B[s]=B[s],B[1]
    qp=jnp.concatenate([query_weight.reshape(-1,d),value_weight.reshape(-1,dv)],axis=1)
    kp=key_weight.reshape(-1,d)
    op=jnp.concatenate([output_weight.reshape(-1,d),up_weight.reshape(-1,ff)],axis=1)
    np_=d//128; hp=np_//2; nvec=7+fan
    if fast:
        vp=jnp.pad(jnp.pad(vector_pieces,(0,-vs%128)).reshape(-1,128),((0,rows--(-vs//128)),(0,0)))
        g1=jnp.concatenate([qp,kp,vp],axis=1)[None]
        ga,gb_=A[::-1],B[::-1]
        pos_a=c.me^jnp.asarray(masks(ga)); pos_b=c.me^jnp.asarray(masks(gb_))
        cat=lambda a,b:jnp.concatenate([a,b],axis=0)
        halves=lambda a:(a[:,:,:a.shape[2]//2],a[:,:,a.shape[2]//2:])
        two=lambda a,b,st:(c.swap(a,ga[st]),c.swap(b,gb_[st]))
        r1=c.swap(g1,ga[0])
        g1,op,dw_=gate((cat(g1,r1),op,down_weight))
        g2_=op[None]; g3_=dw_.reshape(1,fan*rows,d)
        r1=c.swap(g1,ga[1])
        r2=c.swap(g2_,ga[0])
        g1=cat(g1,r1)
        q_,k_=gate((g1[:,:,:d+dv],g1[:,:,d+dv:]))
        rq,rk=two(q_,k_,2)
        g2_,g3_=gate((g2_,g3_),q_)
        g2_=cat(g2_,r2)
        r2=c.swap(g2_,ga[1])
        q_,k_=gate((cat(q_,rq),cat(k_,rk)))
        rq,rk=two(q_,k_,3)
        g2_,g3_=gate((g2_,g3_),q_)
        r3=c.swap(g3_,ga[0])
        g2a,g2b=halves(cat(g2_,r2))
        q_,k_=gate((cat(q_,rq),cat(k_,rk)))
        rq,rk=two(q_,k_,4)
        g2a,g2b,g3_=gate((g2a,g2b,g3_),q_)
        ra,rb=two(g2a,g2b,2)
        x0,g3_=gate((x,cat(g3_,r3)),rq,rk)
        r3=c.swap(g3_,ga[1])
        wq=((q_,rq),pos_a); wk=((k_,rk),pos_b)
        nrm,q,k,v,vec=qkv(x0,first_values,wq,wk,vs,jnp.zeros((nvec,d),f32))
        g2a,g2b,g3_,qa=gate((g2a,g2b,g3_,q),k)
        g2a,g2b,g3_=cat(g2a,ra),cat(g2b,rb),cat(g3_,r3)
        ra,rb=two(g2a,g2b,3)
        c0,l0=afwd(lens,qa,k,v,0,hp)
        o_a,o_b,g3a,g3b,qa=gate(((g2a,ra),(g2b,rb),*halves(g3_),qa),c0)
        abufs=o_a+tuple(c.swap(v_,ga[4]) for v_ in o_a)+o_b+tuple(c.swap(v_,gb_[4]) for v_ in o_b)
        sa,sb=two(g3a,g3b,2)
        c1,l1=afwd(lens,qa,k,v,hp,hp)
        g3a,g3b,x1=gate((g3a,g3b,x),c1,*abufs)
        g3a,g3b=cat(g3a,sa),cat(g3b,sb)
        g3a,g3b,x1=gate((g3a,g3b,x1))
        sa,sb=two(g3a,g3b,3)
        ctxs=[c0,c1]; lse_parts=[l0,l1]
        middle,n2,act,dg,g2=ff_forward(lens,ctxs,x1,cot,abufs,pos_a,pos_b,vec,True)
        d_a,d_b,act1=gate(((g3a,sa),(g3b,sb),act),n2)
        bbufs=tuple(d_a)+tuple(c.swap(v_,ga[4]) for v_ in d_a)+tuple(d_b)+tuple(c.swap(v_,gb_[4]) for v_ in d_b)
    else:
        z=jnp.zeros((1,),jnp.int32)
        ag=lambda v:((lax.all_gather(v,AXES,axis=0,tiled=True)[None],),z)
        wq,wk,wo,wd=ag(qp),ag(kp),ag(op),ag(down_weight.reshape(-1,d))
        vec=lax.all_gather(vector_pieces,AXES,axis=0,tiled=True).reshape(-1,d).astype(f32)
        nrm,q,k,v,vec=qkv(x,first_values,wq,wk,0,vec)
        (abufs,pos_a),(bbufs,pos_b)=wo,wd
        ctx0,lse0=afwd(lens,q,k,v,0,np_)
        ctxs=[ctx0]; lse_parts=[lse0]
        middle,n2,act,dg,g2=ff_forward(lens,ctxs,x,cot,abufs,pos_a,pos_b,vec,False)
    hb=lambda ac:ff_back(lens,ctxs,middle,ac,dg,g2,abufs,bbufs,pos_a,pos_b,vec,fast)
    if fast:
        def inverse(order):
            table=jnp.asarray(np.argsort(masks(order[::-1])).astype(np.int32))
            return jnp.take(table,c.me^jnp.arange(n,dtype=jnp.int32))
        inv,act1=gate((jnp.stack([inverse(A),inverse(B)]),act1))
        s_d=Sum(c,wg([act1,g2],[dict(a=(0,d*u,d),bs=((1,0,d),),o0=u*n//fan,per=n//fan,col=0,parts=((0,h,0),(h,d,1))) for u in range(fan)],inv,n,rows*fan,d,"dwd"),(A,B),h)
        act2=exchange([s_d],act,*bbufs)
        out,gp,gb,dm,gc,dl,sv=hb(act2)
        join([s_d],gb); s_d.make()
        n2=exchange([s_d],n2)
        s_u=Sum(c,wg([n2,gp],[dict(a=(0,0,d),bs=((1,d*u,d),),o0=0,per=n,col=d*u,parts=((0,d,u*2//fan),)) for u in range(fan)],inv,n,rows,ff,"dwu"),(A,B),ff//2)
        back=lambda p,w,qv:abwd(lens,qv,k,v,gc,lse_parts[p//hp],p%hp,dl,p,w,bf if p<hp else f32)
        join([s_d],s_u.send); s_d.make()
        g=[back(0,hp-1,exchange([s_d,s_u],q))]
        join([s_d,s_u],g[0][0]); s_d.make(); s_u.make()
        g.append(back(hp-1,1,exchange([s_d,s_u],q)))
        wide=lambda e0,e1,i,at:((at,0,e0[i].shape[1]),(at+1,0,e1[i].shape[1]))
        s_1=Sum(c,wg([gate(nrm,g[1][0])]+[e[i] for i in range(3) for e in g]+[gb]+ctxs,
            [dict(a=(8+i,0,h),bs=((7,0,d),),o0=i*n//2,per=n//2,col=2*h+dv,parts=((0,d,1),)) for i in range(2)]
            +[dict(a=(0,0,d),bs=sum((wide(g[0],g[1],i,1+2*i) for i in range(3)),()),o0=0,per=n,col=0,parts=((0,2*h+dv,0),))],inv,n,rows,2*h+dv+d,"dw1"),(A,B),2*h+dv)
        join([s_d,s_u],s_1.send); s_d.make(); s_u.make()
        g.append(back(hp,hp-1,exchange([s_d,s_u,s_1],q)))
        join([s_d,s_u,s_1],g[2][0]); s_u.make(); s_1.make()
        g.append(back(2*hp-1,1,exchange([s_u,s_1],q)))
        gh,sv,vg=qkv_back(gate(x,g[3][0]),dm,vec,sv,[e[0] for e in g],[e[1] for e in g],[e[2] for e in g[:2]],wq,wk,vs,n)
        join([s_u,s_1],gh); s_u.make(); s_1.make()
        vg=exchange([s_u,s_1],vg)
        s_2=Sum(c,wg([nrm]+[e[i] for i in range(2) for e in g[2:]]+[vg],[dict(a=(0,0,d),bs=sum((wide(g[2],g[3],i,1+2*i) for i in range(2)),()),o0=0,per=n,col=0,parts=((0,2*h,0),))],inv,n,rows,2*h+128,"dw2",raw=True),(A,A),2*h+128)
        join([s_u,s_1],s_2.send)
        exchange([s_2],()); s_1.make(); exchange([s_1],())
        join([s_1,s_2])
        s_2.wide(); s_2.wide_step()
        s_1.make(); s_1.step()
        s_2.wide(); s_2.wide_step()
        t_d,t_u,t_1,t_2=(st.total() for st in (s_d,s_u,s_1,s_2))
        t_o=t_1[:,2*h+dv:]; gf=jnp.concatenate([g[2][2],g[3][2]],axis=1); gvec=t_2[:-(-vs//128),2*h:].reshape(-1)[:vs]
    else:
        out,gp,gb,dm,gc,dl,sv=hb(act)
        g=[abwd(lens,q,k,v,gc,lse_parts[0],p,dl,p,hp,bf if p<hp else f32) for p in (0,hp)]
        pc=lambda a,b,tn,name:wg_natural(a,b,768,tn,name).reshape(n,-1,b.shape[1])
        dq,dk,dfg=(jnp.concatenate([e[i] for e in (g if i<2 else g[:1])],axis=1) for i in range(3))
        gf=g[1][2]
        t_d=scatter_sum(c,pc(act,g2,768,"dwd"),A); t_u=scatter_sum(c,pc(n2,gp,768,"dwu"),B); t_o=scatter_sum(c,pc(ctxs[0],gb,768,"dwo"),A)
        t_1=scatter_sum(c,jnp.concatenate([pc(nrm,dq[:,:h],h,"dwqa"),pc(nrm,dk[:,:h],h,"dwka"),pc(nrm,dfg,dv,"dwv")],axis=2),B)
        t_2=scatter_sum(c,jnp.concatenate([pc(nrm,dq[:,h:],h,"dwqb"),pc(nrm,dk[:,h:],h,"dwkb")],axis=2),A)
        gh,sv,_=qkv_back(x,dm,vec,sv,[dq],[dk],[dfg],wq,wk)
        gvec=scatter_sum(c,sv[:nvec].reshape(n,1,vs),A).reshape(-1)
    gq=jnp.concatenate([t_1[:,:h],t_2[:,:h]],axis=1).reshape(-1)
    gk=jnp.concatenate([t_1[:,h:2*h],t_2[:,h:2*h]],axis=1).reshape(-1)
    gv=t_1[:,2*h:2*h+dv].reshape(-1)
    return (out,gh,gf,gq,gk,gv,t_o.reshape(-1),t_u.reshape(-1),t_d.reshape(-1),gvec)

def solution(mesh):
    s2=P(AXES,None); s1=P(AXES)
    return jax.shard_map(functools.partial(shards,dict(mesh.shape)),mesh=mesh,in_specs=(s2,)*4+(s1,)*7,out_specs=(s2,)*3+(s1,)*7,check_vma=False)
```

```python
import functools, math
import jax, jax.numpy as jnp
from jax import lax
from jax.experimental import pallas as pl
from jax.experimental.pallas import tpu as pltpu
bf=jnp.bfloat16; f32=jnp.float32
NT=(((1,),(1,)),((),()))
TN=(((0,),(0,)),((),()))
NN=(((1,),(0,)),((),()))
def dot(a,b,dn=NN):
    return lax.dot_general(a,b,dn,preferred_element_type=f32)
def cp(mb):
    return pltpu.CompilerParams(vmem_limit_bytes=mb<<20)
def full(shape):
    nd=len(shape)
    return pl.BlockSpec(shape,lambda *a:(0,)*nd)
def cost(fl,by,tr=0):
    return pl.CostEstimate(flops=1000,bytes_accessed=1000,transcendentals=0)

def norm_stats(v):
    c=v-jnp.mean(v,axis=-1,keepdims=True)
    r=lax.rsqrt(jnp.mean(c*c,axis=-1,keepdims=True)+1e-5)
    return c*r,r

ANY=pl.BlockSpec(memory_space=pl.ANY)
def stage(n,rows,cols):
    return pltpu.VMEM((n,rows,cols) if rows%16 else (1,16,128),bf)
def place(bufs,pos_ref,w_ref,st_ref,sem,col=0):
    rows,w=bufs[0].shape[1:]
    p=0
    for b in bufs:
        for a in range(b.shape[0]):
            if rows%16: to=st_ref.at[pos_ref[p],:,pl.ds(col,w)]
            else: to=w_ref.at[pl.ds(pl.multiple_of(pos_ref[p]*rows,16),rows),pl.ds(col,w)]
            pltpu.make_async_copy(b.at[a],to,sem).start()
            p+=1
def placed(w_ref,st_ref,sem,rows):
    if rows%16==0:
        pltpu.make_async_copy(w_ref,w_ref,sem).wait()
        return
    pltpu.make_async_copy(st_ref,st_ref,sem).wait()
    k=16//math.gcd(rows,16); cols=w_ref.shape[1]
    def move(u,_):
        v=jnp.concatenate([st_ref[k*u+i,:,0:cols].astype(f32) for i in range(k)],axis=0)
        w_ref[pl.ds(pl.multiple_of(u*(k*rows),16),k*rows),:]=v.astype(bf)
        return 0
    lax.fori_loop(0,st_ref.shape[0]//k,move,0)
def cs_(v): return jnp.sum(v,axis=0,keepdims=True)

def qkv_body(pa_ref,pb_ref,x_ref,first_ref,vin_ref,*refs,na,nb,per):
    abufs=refs[:na]; bbufs=refs[na:na+nb]
    n_ref,q_ref,k_ref,v_ref,vec_ref,wa,wb,sa,sb,flat,sems=refs[na+nb:]
    d=x_ref.shape[1]; w=first_ref.shape[1]
    @pl.when(pl.program_id(0)==0)
    def _():
        place(bbufs,pb_ref,wb,sb,sems.at[1]); place(abufs,pa_ref,wa,sa,sems.at[0])
        placed(wb,sb,sems.at[1],bbufs[0].shape[1])
        if per:
            for o in range(sb.shape[0]):
                v=sb[o,:,d:d+128].astype(f32)
                for s in range(-(-per//128)):
                    flat[0:1,per*o+128*s:per*o+128*(s+1)]=v[s:s+1,:]
            for i in range(vec_ref.shape[0]):
                vec_ref[i:i+1,:]=flat[0:1,d*i:d*(i+1)]
        else:
            vec_ref[...]=vin_ref[...]
        placed(wa,sa,sems.at[0],abufs[0].shape[1])
    xh,_=norm_stats(x_ref[...].astype(f32))
    n=(xh*vec_ref[0:1,:]+vec_ref[1:2,:]).astype(bf)
    n_ref[...]=n
    q=(dot(n,wa[:,:d])+vec_ref[2:3,:]).astype(bf)
    q_ref[...]=q*0.125
    k_ref[...]=dot(n,wb[...]).astype(bf)
    v_ref[:,:w]=dot(n,wa[:,d:]).astype(bf)
    v_ref[:,w:]=first_ref[...]
def qkv(x,first,wa,wb,per,vin,tm=256):
    t,d=x.shape; dv=first.shape[1]
    (abufs,pa),(bbufs,pb)=wa,wb
    n=sum(b.shape[0] for b in bbufs); nvec=vin.shape[0]
    row=lambda c:pl.BlockSpec((tm,c),lambda i,*a:(i,0))
    return pl.pallas_call(functools.partial(qkv_body,na=len(abufs),nb=len(bbufs),per=per),
        grid_spec=pltpu.PrefetchScalarGridSpec(num_scalar_prefetch=2,grid=(t//tm,),
            in_specs=[row(d),row(dv),full(vin.shape)]+[ANY]*(len(abufs)+len(bbufs)),
            out_specs=[row(d)]*4+[pl.BlockSpec((nvec,d),lambda i,*a:(0,0))],scratch_shapes=[pltpu.VMEM((d,d+dv),bf),pltpu.VMEM((d,d),bf),stage(n,*abufs[0].shape[1:]),stage(n,*bbufs[0].shape[1:]),pltpu.VMEM((1,nvec*d+256),f32),pltpu.SemaphoreType.DMA((2,))]),
        out_shape=[jax.ShapeDtypeStruct((t,d),bf)]*4+[jax.ShapeDtypeStruct((nvec,d),f32)],compiler_params=cp(22),name="qkv",
        cost_estimate=cost(2*t*d*(2*d+dv),t*d*14+d*d*6))(pa,pb,x,first,vin,*abufs,*bbufs)

def afwd_body(len_ref,q_ref,k_ref,v_ref,o_ref,l_ref,*,bq):
    t=q_ref.shape[0]; half=t//2
    long_bias=jnp.where(len_ref[0]>half,0.0,-1e30)
    dh=q_ref.shape[1]//2
    diag=lax.broadcasted_iota(jnp.int32,(bq,bq),0)>=lax.broadcasted_iota(jnp.int32,(bq,bq),1)
    for i in range(t//bq):
        outs=[]
        for h in range(2):
            q=q_ref[i*bq:(i+1)*bq,h*dh:(h+1)*dh]
            n=(i+1)*bq
            s=dot(q,k_ref[0:n,h*dh:(h+1)*dh],NT)
            parts=[]
            lo=half if i*bq>=half else 0
            if lo: parts.append(s[:,:lo]+long_bias)
            if i*bq>lo: parts.append(s[:,lo:i*bq])
            parts.append(jnp.where(diag,s[:,i*bq:],-1e30))
            s=jnp.concatenate(parts,axis=1) if len(parts)>1 else parts[0]
            m=jnp.max(s,axis=-1,keepdims=True)
            p=jnp.exp(s-m)
            l=jnp.sum(p,axis=-1,keepdims=True)
            o=dot(p.astype(bf),v_ref[0:n,h*dh:(h+1)*dh])
            outs.append((o*(1.0/l)).astype(bf))
            lse=m+jnp.log(l)
            l_ref[0,h:h+1,i*bq:(i+1)*bq]=jnp.transpose(jnp.broadcast_to(lse,(bq,128)))[0:1,:]
        o_ref[i*bq:(i+1)*bq,:]=jnp.concatenate(outs,axis=1)
def afwd(lens,q,k,v,first_pair,pairs,bq=512):
    t=q.shape[0]
    col=pl.BlockSpec((t,128),lambda p,*a:(0,p+first_pair))
    return pl.pallas_call(functools.partial(afwd_body,bq=bq),
        grid_spec=pltpu.PrefetchScalarGridSpec(num_scalar_prefetch=1,grid=(pairs,),in_specs=[col]*3,
            out_specs=[pl.BlockSpec((t,128),lambda p,*a:(0,p)),pl.BlockSpec((1,2,t),lambda p,*a:(p,0,0))]),
        out_shape=[jax.ShapeDtypeStruct((t,pairs*128),bf),jax.ShapeDtypeStruct((pairs,2,t),f32)],compiler_params=cp(16),name="afwd",
        cost_estimate=cost(4*t*t*pairs*128*0.6*4,t*pairs*128*8,t*t*pairs))(lens,q,k,v)

def abwd_body(len_ref,q_ref,k_ref,v_ref,do_ref,l_ref,dl_ref,dq_ref,dk_ref,dv_ref,*,bk,first_pair,dqt):
    t=q_ref.shape[0]; half=t//2
    long_bias=jnp.where(len_ref[0]>half,0.0,-1e30)
    dh=q_ref.shape[1]//2
    p_id=pl.program_id(0)+first_pair
    diag=lax.broadcasted_iota(jnp.int32,(bk,bk),0)<=lax.broadcasted_iota(jnp.int32,(bk,bk),1)
    dqs=[]
    dks=[]; dvs=[]
    for h in range(2):
        sl=slice(h*dh,(h+1)*dh)
        lrow=l_ref[0,h:h+1,:]; drow=dl_ref[pl.ds(2*p_id+h,1),:]
        dq=None; dkh=[]; dvh=[]
        for j in range(t//bk):
            k=k_ref[j*bk:(j+1)*bk,sl]; v=v_ref[j*bk:(j+1)*bk,sl]
            a=j*bk
            q=q_ref[a:,sl]; do=do_ref[a:,sl]
            st=dot(k,q,NT)
            pieces=[jnp.where(diag,st[:,:bk],-1e30)]
            hi=max(half,a+bk) if a<half else t
            if hi>a+bk: pieces.append(st[:,bk:hi-a])
            if a<half: pieces.append(st[:,hi-a:]+long_bias)
            st=jnp.concatenate(pieces,axis=1) if len(pieces)>1 else pieces[0]
            p=jnp.exp(st-lrow[:,a:])
            dp=dot(v,do,NT)
            ds=(p*(dp-drow[:,a:])).astype(bf)
            dvh.append(dot(p.astype(bf),do))
            dkh.append(dot(ds,q))
            if dqt: c=dot(k,ds,TN)
            else: c=dot(ds,k,TN)
            ax=1 if dqt else 0
            if dq is None: dq=c
            else:
                if dqt: dq=jnp.concatenate([dq[:,:a],dq[:,a:]+c],axis=1)
                else: dq=jnp.concatenate([dq[:a],dq[a:]+c],axis=0)
        dqs.append(jnp.transpose(dq) if dqt else dq)
        dks.append(jnp.concatenate(dkh,axis=0)); dvs.append(jnp.concatenate(dvh,axis=0))
    dq_ref[...]=(jnp.concatenate(dqs,axis=1)*0.125).astype(bf)
    dk_ref[...]=jnp.concatenate(dks,axis=1).astype(bf)
    dv_ref[...]=jnp.concatenate(dvs,axis=1).astype(dv_ref.dtype)
def abwd(lens,q,k,v,do,lse,lse_pair,delta,first_pair,pairs,dv_dtype,bk=256,dqt=True):
    t,d=q.shape
    col=pl.BlockSpec((t,128),lambda p,*a:(0,p+first_pair))
    ocol=pl.BlockSpec((t,128),lambda p,*a:(0,p))
    st=[pl.BlockSpec((1,2,t),lambda p,*a:(p+lse_pair,0,0)),pl.BlockSpec((16,t),lambda p,*a:(0,0))]
    w=pairs*128
    return pl.pallas_call(functools.partial(abwd_body,bk=bk,first_pair=first_pair,dqt=dqt),
        grid_spec=pltpu.PrefetchScalarGridSpec(num_scalar_prefetch=1,grid=(pairs,),in_specs=[col]*4+st,
            out_specs=[ocol]*3),
        out_shape=[jax.ShapeDtypeStruct((t,w),bf)]*2+[jax.ShapeDtypeStruct((t,w),dv_dtype)],compiler_params=cp(14),name="abwd",
        cost_estimate=cost(10*t*t*w*0.6*4,t*w*16,t*t*w//64*0.6))(lens,q,k,v,do,lse,delta)

def place_both(bufs,pa_ref,pb_ref,w_ref,st_ref,sem,split):
    h=len(bufs)//2
    if split:
        place(bufs[:h],pa_ref,w_ref,st_ref,sem); place(bufs[h:],pb_ref,w_ref,st_ref,sem,w_ref.shape[1]//2)
    else:
        place(bufs,pa_ref,w_ref,st_ref,sem)
def ff_body(len_ref,pa_ref,pb_ref,*refs,nc,na,split):
    ctxs=refs[:nc]; x_ref,cot_ref,vec_ref=refs[nc:nc+3]; refs=refs[nc+3:]
    abufs=refs[:na]
    mid_ref,n2_ref,act_ref,dg_ref,g2_ref,wa,sa,sems=refs[na:]
    tm=x_ref.shape[0]; d=x_ref.shape[1]; fc=d; ff=act_ref.shape[1]
    i=pl.program_id(0)
    @pl.when(i==0)
    def _():
        place_both(abufs,pa_ref,pb_ref,wa,sa,sems.at[0],split)
        placed(wa,sa,sems.at[0],abufs[0].shape[1])
    pos=lax.broadcasted_iota(jnp.int32,(tm,1),0)+i*tm
    live=jnp.where(pos<len_ref[0]+len_ref[1],1.0,0.0)
    g2_ref[...]=(cot_ref[...].astype(f32)*live).astype(bf)
    ctx=jnp.concatenate([c[...] for c in ctxs],axis=1)
    middle=x_ref[...].astype(f32)+(dot(ctx,wa[:,0:d])+vec_ref[3:4,:])
    mid_ref[...]=middle
    xh,_=norm_stats(middle)
    n2=(xh*vec_ref[4:5,:]+vec_ref[5:6,:]).astype(bf)
    n2_ref[...]=n2
    for c in range(ff//fc):
        cs=slice(c*fc,(c+1)*fc)
        h=dot(n2,wa[:,d+c*fc:d+(c+1)*fc])+vec_ref[7+c:8+c,:]
        h2=h*h
        e=jnp.exp(h*(-1.5957691216057308-(1.5957691216057308*0.044715)*h2))
        u=1.0/(1.0+e)
        hu=h*u
        act_ref[:,cs]=hu.astype(bf)
        dg_ref[:,cs]=(u+(hu-hu*u)*(1.5957691216057308+(3*1.5957691216057308*0.044715)*h2)).astype(bf)
def ff_forward(lens,ctxs,x,cot,abufs,pa,pb,vec,split,tm=256):
    t,d=x.shape; ff=(vec.shape[0]-7)*d
    row=lambda c:pl.BlockSpec((tm,c),lambda i,*a:(i,0))
    sd=jax.ShapeDtypeStruct
    return pl.pallas_call(functools.partial(ff_body,nc=len(ctxs),na=len(abufs),split=split),
        grid_spec=pltpu.PrefetchScalarGridSpec(num_scalar_prefetch=3,grid=(t//tm,),
            in_specs=[row(c.shape[1]) for c in ctxs]+[row(d)]*2+[full(vec.shape)]+[ANY]*len(abufs),
            out_specs=[row(d),row(d),row(ff),row(ff),row(d)],
            scratch_shapes=[pltpu.VMEM((d,d+ff),bf),stage(d//abufs[0].shape[1],abufs[0].shape[1],d+ff),pltpu.SemaphoreType.DMA((1,))]),
        out_shape=[sd((t,d),f32),sd((t,d),bf),sd((t,ff),bf),sd((t,ff),bf),sd((t,d),bf)],
        compiler_params=cp(60),name="ffward",cost_estimate=cost(0,0))(lens,pa,pb,*ctxs,x,cot,vec,*abufs)

def mid_body(len_ref,pa_ref,pb_ref,*refs,heads,nc,na,nb,split):
    ctxs=refs[:nc]; mid_ref,act_ref,dg_ref,cot_ref,vec_ref=refs[nc:nc+5]; refs=refs[nc+5:]
    abufs=refs[:na]; bbufs=refs[na:na+nb]
    out_ref,gp_ref,gb_ref,dm_ref,gc_ref,dl_ref,s_ref,wa,sa,wd_ref,sems=refs[na+nb:]
    tm=mid_ref.shape[0]; d=mid_ref.shape[1]; ff=wd_ref.shape[0]; fc=d
    i=pl.program_id(0)
    @pl.when(i==0)
    def _():
        place_both(abufs,pa_ref,pb_ref,wa,sa,sems.at[0],split)
        place_both(bbufs,pa_ref if split else pb_ref,pb_ref,wd_ref,None,sems.at[1],split)
        s_ref[...]=jnp.zeros_like(s_ref)
        placed(wa,sa,sems.at[0],abufs[0].shape[1]); placed(wd_ref,None,sems.at[1],bbufs[0].shape[1])
    gain=vec_ref[4:5,:]
    pos=lax.broadcasted_iota(jnp.int32,(tm,1),0)+i*tm
    live=jnp.where(pos<len_ref[0]+len_ref[1],1.0,0.0)
    ctx=jnp.concatenate([c[...] for c in ctxs],axis=1)
    middle=mid_ref[...]
    g2=cot_ref[...]; gr=g2.astype(f32)
    acc=jnp.zeros((tm,d),f32); dn=jnp.zeros((tm,d),f32)
    for c in range(ff//fc):
        cs=slice(c*fc,(c+1)*fc)
        da=dot(g2,wd_ref[cs,:],NT)
        gpb=(da*dg_ref[:,cs].astype(f32)).astype(bf)
        gp_ref[:,cs]=gpb
        s_ref[7+c:8+c,:]+=cs_(gpb.astype(f32))
        acc=acc+dot(act_ref[:,cs],wd_ref[cs,:])
        dn=dn+dot(gpb,wa[:,d+c*fc:d+(c+1)*fc],NT)
    out_ref[...]=((middle+(acc+vec_ref[6:7,:]))*live).astype(bf)
    xh,r=norm_stats(middle)
    e=dn*gain
    dm=gr+r*(e-jnp.mean(e,axis=-1,keepdims=True)-xh*jnp.mean(e*xh,axis=-1,keepdims=True))
    dm_ref[...]=dm
    gb=dm.astype(bf)
    gb_ref[...]=gb
    gc=dot(gb,wa[:,0:d],NT).astype(bf)
    gc_ref[...]=gc
    pr=gc.astype(f32)*ctx.astype(f32)
    hi=pr.astype(bf); lo=(pr-hi.astype(f32)).astype(bf)
    dh=d//heads
    ind=(lax.broadcasted_iota(jnp.int32,(16,d),1)//dh==lax.broadcasted_iota(jnp.int32,(16,d),0)).astype(bf)
    dl_ref[...]=dot(ind,hi,NT)+dot(ind,lo,NT)
    s_ref[3:4,:]+=cs_(gb.astype(f32))
    s_ref[4:5,:]+=cs_(dn*xh)
    s_ref[5:6,:]+=cs_(dn)
    s_ref[6:7,:]+=cs_(gr)
def ff_back(lens,ctxs,middle,act,dg,g2,abufs,bbufs,pa,pb,vec,split,heads=12,tm=256):
    t,d=middle.shape; ff=act.shape[1]
    row=lambda c:pl.BlockSpec((tm,c),lambda i,*a:(i,0))
    sd=jax.ShapeDtypeStruct
    return pl.pallas_call(functools.partial(mid_body,heads=heads,nc=len(ctxs),na=len(abufs),nb=len(bbufs),split=split),
        grid_spec=pltpu.PrefetchScalarGridSpec(num_scalar_prefetch=3,grid=(t//tm,),
            in_specs=[row(c.shape[1]) for c in ctxs]+[row(d),row(ff),row(ff),row(d)]+[full(vec.shape)]+[ANY]*(len(abufs)+len(bbufs)),
            out_specs=[row(d),row(ff),row(d),row(d),row(d),pl.BlockSpec((16,tm),lambda i,*a:(0,i)),full((16,d))],
            scratch_shapes=[pltpu.VMEM((d,d+ff),bf),stage(d//abufs[0].shape[1],abufs[0].shape[1],d+ff),pltpu.VMEM((ff,d),bf),pltpu.SemaphoreType.DMA((2,))]),
        out_shape=[sd((t,d),bf),sd((t,ff),bf),sd((t,d),bf),sd((t,d),f32),sd((t,d),bf),sd((16,t),f32),sd((16,d),f32)],
        compiler_params=cp(46),name="ffback",cost_estimate=cost(0,0))(lens,pa,pb,*ctxs,middle,act,dg,g2,vec,*abufs,*bbufs)

def wg_body(inv_ref,*refs,na,tasks,pieces,nbuf,raw):
    arrs=refs[:na]; keep_ref,send_ref=refs[na:na+2]; bufs=refs[na+2:na+2+nbuf]
    outs=refs[na+2+nbuf:-2]; isem,osem=refs[-2:]
    half=pieces//2
    if raw: pltpu.make_async_copy(arrs[-1],bufs[-1],isem.at[nbuf-1]).start()
    need=[]; loads={}; k=0
    for t in tasks:
        ids=[]
        for key in tuple(t["a"])+tuple(t["bs"]):
            if key not in loads:
                ai,c0,w=key
                pltpu.make_async_copy(arrs[ai].at[:,pl.ds(c0,w)],bufs[k],isem.at[k]).start()
                loads[key]=k; k+=1
            ids.append(loads[key])
        need.append(ids)
    if raw:
        src_ref=bufs[-1]; last=pl.ds(keep_ref.shape[2]-src_ref.shape[2],src_ref.shape[2])
        pltpu.make_async_copy(src_ref,src_ref,isem.at[nbuf-1]).wait()
        for o in range(pieces):
            r=inv_ref[0,o]
            part=src_ref.at[o]
            @pl.when(r<half)
            def _(): pltpu.make_async_copy(part,keep_ref.at[r,:,last],osem.at[len(tasks)]).start()
            @pl.when(r>=half)
            def _(): pltpu.make_async_copy(part,send_ref.at[r-half,:,last],osem.at[len(tasks)]).start()
    ready=set()
    for ti,(t,ids) in enumerate(zip(tasks,need)):
        for b in ids:
            if b not in ready:
                pltpu.make_async_copy(bufs[b],bufs[b],isem.at[b]).wait(); ready.add(b)
        ka=len(t["a"]); lhs=[bufs[b][...] for b in ids[:ka]]
        lhs=jnp.concatenate(lhs,axis=1) if ka>1 else lhs[0]
        rhs=[bufs[b][...] for b in ids[ka:]]
        rhs=jnp.concatenate(rhs,axis=1) if len(rhs)>1 else rhs[0]
        scr=outs[ti]
        acc=dot(lhs,rhs,TN)
        rows,w=scr.shape[1:]
        for p in range(t["per"]): scr[p]=acc[p*rows:(p+1)*rows].astype(bf)
        for p,(lo,hi,which) in ((p,c) for p in range(t["per"]) for c in t["parts"]):
            r=inv_ref[which,t["o0"]+p]
            src=scr.at[p,:,pl.ds(lo,hi-lo)]
            cols=pl.ds(t["col"]+lo,hi-lo)
            @pl.when(r<half)
            def _(): pltpu.make_async_copy(src,keep_ref.at[r,:,cols],osem.at[ti]).start()
            @pl.when(r>=half)
            def _(): pltpu.make_async_copy(src,send_ref.at[r-half,:,cols],osem.at[ti]).start()
    for ti in range(len(tasks)):
        pltpu.make_async_copy(outs[ti],outs[ti],osem.at[ti]).wait()
    if raw: pltpu.make_async_copy(src_ref,src_ref,osem.at[len(tasks)]).wait()
def wg(arrs,tasks,inv,pieces,rows,width,name,raw=False,mb=28):
    t=arrs[0].shape[0]
    keys=[]; fl=0
    for k in tasks:
        for key in tuple(k["a"])+tuple(k["bs"]):
            if key not in keys: keys.append(key)
        fl+=2*t*sum(a[2] for a in k["a"])*sum(b[2] for b in k["bs"])
    sh=jax.ShapeDtypeStruct((pieces//2,rows,width),bf)
    return pl.pallas_call(functools.partial(wg_body,na=len(arrs),tasks=tasks,pieces=pieces,nbuf=len(keys)+raw,raw=raw),
        grid_spec=pltpu.PrefetchScalarGridSpec(num_scalar_prefetch=1,grid=(),in_specs=[ANY]*len(arrs),out_specs=[ANY,ANY],
            scratch_shapes=[pltpu.VMEM((t,w),bf) for _,_,w in keys]+[pltpu.VMEM(arrs[-1].shape,bf)]*raw+[pltpu.VMEM((k["per"],sum(a[2] for a in k["a"])//k["per"],sum(b[2] for b in k["bs"])),bf) for k in tasks]
                +[pltpu.SemaphoreType.DMA((len(keys)+1,)),pltpu.SemaphoreType.DMA((len(tasks)+1,))]),
        out_shape=[sh,sh],compiler_params=cp(mb),name=name,
        cost_estimate=cost(fl,pieces*rows*width*2+sum(t*k[2]*2 for k in keys)))(inv,*arrs)

def wgn_body(a_ref,b_ref,o_ref):
    o_ref[...]=dot(a_ref[...],b_ref[...],TN).astype(o_ref.dtype)
def wg_natural(a,b,tm,tn,name):
    t,m=a.shape; n=b.shape[1]
    return pl.pallas_call(wgn_body,grid=(m//tm,n//tn),
        in_specs=[pl.BlockSpec((t,tm),lambda i,j:(0,i)),pl.BlockSpec((t,tn),lambda i,j:(0,j))],
        out_specs=pl.BlockSpec((tm,tn),lambda i,j:(i,j)),
        out_shape=jax.ShapeDtypeStruct((m,n),bf),compiler_params=cp(60),name=name,
        cost_estimate=cost(2*t*m*n,t*(m+n)*2+m*n*2))(a,b)

def qb_body(pa_ref,pb_ref,x_ref,dm_ref,vec_ref,s_in_ref,*refs,nq,nf,na,nb,per):
    dqs=refs[:nq]; dks=refs[nq:2*nq]; dfs=refs[2*nq:2*nq+nf]; refs=refs[2*nq+nf:]
    abufs=refs[:na]; bbufs=refs[na:na+nb]
    gh_ref,s_ref,vg_ref,wa,wb,sa,sb,flat,vgf,sems=refs[na+nb:]
    i=pl.program_id(0)
    d=x_ref.shape[1]; dv=wa.shape[1]-d
    @pl.when(i==0)
    def _():
        place(abufs,pa_ref,wa,sa,sems.at[0]); place(bbufs,pb_ref,wb,sb,sems.at[1])
        s_ref[...]=s_in_ref[...]
        placed(wa,sa,sems.at[0],abufs[0].shape[1]); placed(wb,sb,sems.at[1],bbufs[0].shape[1])
    dq=jnp.concatenate([v[...] for v in dqs],axis=1)
    dqv=jnp.concatenate([dq]+[v[...] for v in dfs],axis=1)
    dk=jnp.concatenate([v[...] for v in dks],axis=1)
    dn=dot(dqv,wa[...],NT)+dot(dk,wb[...],NT)
    xh,r=norm_stats(x_ref[...].astype(f32))
    e=dn*vec_ref[0:1,:]
    gh_ref[...]=dm_ref[...]+r*(e-jnp.mean(e,axis=-1,keepdims=True)-xh*jnp.mean(e*xh,axis=-1,keepdims=True))
    s_ref[0:1,:]+=cs_(dn*xh)
    s_ref[1:2,:]+=cs_(dn)
    s_ref[2:3,:]+=cs_(dq.astype(f32))
    if per:
        @pl.when(i==pl.num_programs(0)-1)
        def _():
            vgf[...]=jnp.zeros_like(vgf)
            for u in range((flat.shape[1]-128*3)//d):
                flat[0:1,d*u:d*(u+1)]=s_ref[u:u+1,:]
            for o in range(vgf.shape[0]):
                for s in range(-(-per//128)):
                    vgf[o,s:s+1,:]=flat[0:1,per*o+128*s:per*o+128*(s+1)]
            vg_ref[...]=vgf[...].astype(bf)
def qkv_back(x,dm,vec,s_in,dqs,dks,dfs,wa,wb,per=0,n=1,tm=256):
    vgs=(n,x.shape[1]//n,128) if per else (1,16,128)
    t,d=x.shape; dv=sum(v.shape[1] for v in dfs)
    (abufs,pa),(bbufs,pb)=wa,wb
    row=lambda c:pl.BlockSpec((tm,c),lambda i,*a:(i,0))
    return pl.pallas_call(functools.partial(qb_body,nq=len(dqs),nf=len(dfs),na=len(abufs),nb=len(bbufs),per=per),
        grid_spec=pltpu.PrefetchScalarGridSpec(num_scalar_prefetch=2,grid=(t//tm,),
            in_specs=[row(d),row(d),full(vec.shape),full(s_in.shape)]+[row(v.shape[1]) for v in dqs+dks+dfs]+[ANY]*(len(abufs)+len(bbufs)),
            out_specs=[row(d),full(s_in.shape),full(vgs)],scratch_shapes=[pltpu.VMEM((d,d+dv),bf),pltpu.VMEM((d,d),bf),stage(n,*abufs[0].shape[1:]),stage(n,*bbufs[0].shape[1:]),pltpu.VMEM((1,vec.shape[0]*d+128*3),f32),pltpu.VMEM(vgs,f32),pltpu.SemaphoreType.DMA((2,))]),
        out_shape=[jax.ShapeDtypeStruct((t,d),f32),jax.ShapeDtypeStruct(s_in.shape,f32),jax.ShapeDtypeStruct(vgs,bf)],compiler_params=cp(24),name="qkvback",
        cost_estimate=cost(2*t*d*(2*d+dv),t*d*16+d*d*5))(pa,pb,x,dm,vec,s_in,*dqs,*dks,*dfs,*abufs,*bbufs)
import numpy as np
from jax.sharding import PartitionSpec as P
AXES=("dp","sub")

def index_bits(sizes):
    return [(a,b) for a in reversed(AXES) for b in range(sizes[a].bit_length()-1)]

def swap(v,axis,bit,size):
    return lax.ppermute(v,axis,[(i,i^(1<<bit)) for i in range(size)])

def masks(order):
    p=np.arange(1<<len(order))
    return sum(((p>>s)&1)<<b for s,b in enumerate(order)).astype(np.int32)

class Comm:
    def __init__(self,sizes):
        self.sizes=sizes; self.n=sizes["dp"]*sizes["sub"]
        self.bits=index_bits(sizes); self.nb=len(self.bits)
        self.me=lax.axis_index("dp")*sizes["sub"]+lax.axis_index("sub")
    def cross(self,v,mask):
        return lax.ppermute(v,AXES,[(i,i^mask) for i in range(self.n)])
    def swap(self,v,b):
        axis,k=self.bits[b]
        return swap(v,axis,k,self.sizes[axis])

def gate(nxt,*done):
    return lax.optimization_barrier((nxt,done))[0]

def scatter_sum(c,g,order):
    n,rows,cols=g.shape
    left=list(reversed(range(c.nb)))
    dt=g.dtype
    g=g.reshape((2,)*c.nb+(rows,cols))
    for step,b in enumerate(order):
        axis,k=c.bits[b]
        mine=(lax.axis_index(axis)>>k)&1
        pos=left.index(b); left.pop(pos)
        send=lax.dynamic_index_in_dim(g,1-mine,pos,keepdims=False)
        keep=lax.dynamic_index_in_dim(g,mine,pos,keepdims=False)
        g=keep.astype(f32)+c.swap(send,b).astype(f32)
        if step<len(order)-1: g=g.astype(dt)
    return g

class Sum:
    def __init__(self,c,pair,orders,cut):
        self.c=c; self.keep=pair[0]; self.orders=orders; self.cut=cut
        self.send=[pair[1]]; self.masks=[1<<orders[0][0]]; self.got=[]; self.s=0
    def step(self):
        self.got.append([self.c.cross(v,m) for v,m in zip(self.send,self.masks)]); self.s+=1
    def part(self,lo,hi,cols):
        w=self.keep.shape[2]
        a,b=(0,self.cut) if cols==0 else (self.cut,w)
        tot=self.keep[lo:hi,:,a:b].astype(f32)
        for s,parts in enumerate(self.got):
            g=parts[cols][lo:hi] if s in (1,2) and self.cut<w else parts[0][lo:hi,:,a:b]
            tot=tot+g.astype(f32)
        return tot
    def both(self,lo,hi):
        if self.cut==self.keep.shape[2]: return self.part(lo,hi,0)
        return jnp.concatenate([self.part(lo,hi,0),self.part(lo,hi,1)],axis=2)
    def make(self):
        w=self.keep.shape[0]>>self.s
        if self.s in (1,2) and self.cut<self.keep.shape[2]:
            self.send=[self.part(w,2*w,i).astype(bf) for i in (0,1)]
            self.masks=[1<<o[self.s] for o in self.orders]
        else:
            self.send=[self.both(w,2*w).astype(bf)]
            self.masks=[1<<self.orders[0][self.s]]
    def wide(self):
        o=self.orders[0]; q=self.keep.shape[0]>>(self.s+1)
        self.send=[self.both(q*g,q*(g+1)).astype(bf) for g in (1,2,3)]
        self.masks=[((g>>1)<<o[self.s])|((g&1)<<o[self.s+1]) for g in (1,2,3)]
    def wide_step(self):
        for v,m in zip(self.send,self.masks): self.got.append([self.c.cross(v,m)])
        self.s+=2
    def total(self):
        return self.both(0,1)[0]

def exchange(sums,nxt,*done):
    sends,nxt=gate(([s.send for s in sums],nxt),*done)
    for s,v in zip(sums,sends): s.send=v
    for s in sums: s.step()
    return nxt
def join(sums,*done):
    got=gate([s.got[-1] for s in sums],*done)
    for s,v in zip(sums,got): s.got[-1]=v

def shards(sizes,hidden_in,first_values,doc_lengths,out_cotangent,query_weight,key_weight,value_weight,output_weight,up_weight,down_weight,vector_pieces):
    c=Comm(sizes); n=c.n; nb=c.nb
    t,d=hidden_in.shape; dv=first_values.shape[1]
    ff=up_weight.shape[0]*n//d
    vs=vector_pieces.shape[0]; h=d//2; rows=d//n; fan=ff//d
    fast=n==1<<nb and n==32 and (d//n)%8==0
    lens=doc_lengths[0]
    x=hidden_in; cot=out_cotangent
    s=sizes["sub"].bit_length()-1
    A=list(range(nb)); B=A[:]
    if s>=2 and nb>s: B[1],B[s]=B[s],B[1]
    qp=jnp.concatenate([query_weight.reshape(-1,d),value_weight.reshape(-1,dv)],axis=1)
    kp=key_weight.reshape(-1,d)
    op=jnp.concatenate([output_weight.reshape(-1,d),up_weight.reshape(-1,ff)],axis=1)
    np_=d//128; hp=np_//2; nvec=7+fan
    if fast:
        vp=jnp.pad(jnp.pad(vector_pieces,(0,-vs%128)).reshape(-1,128),((0,rows--(-vs//128)),(0,0)))
        g1=jnp.concatenate([qp,kp,vp],axis=1)[None]
        ga,gb_=A[::-1],B[::-1]
        pos_a=c.me^jnp.asarray(masks(ga)); pos_b=c.me^jnp.asarray(masks(gb_))
        cat=lambda a,b:jnp.concatenate([a,b],axis=0)
        halves=lambda a:(a[:,:,:a.shape[2]//2],a[:,:,a.shape[2]//2:])
        two=lambda a,b,st:(c.swap(a,ga[st]),c.swap(b,gb_[st]))
        r1=c.swap(g1,ga[0])
        g1,op,dw_=gate((cat(g1,r1),op,down_weight))
        g2_=op[None]; g3_=dw_.reshape(1,fan*rows,d)
        r1=c.swap(g1,ga[1])
        r2=c.swap(g2_,ga[0])
        g1=cat(g1,r1)
        def inverse(order):
            table=jnp.asarray(np.argsort(masks(order[::-1])).astype(np.int32))
            return jnp.take(table,c.me^jnp.arange(n,dtype=jnp.int32))
        q_,k_,inv,pos_a,pos_b=gate((g1[:,:,:d+dv],g1[:,:,d+dv:],jnp.stack([inverse(A),inverse(B)]),pos_a,pos_b))
        rq,rk=two(q_,k_,2)
        g2_,g3_=gate((g2_,g3_),q_)
        g2_=cat(g2_,r2)
        r2=c.swap(g2_,ga[1])
        q_,k_=gate((cat(q_,rq),cat(k_,rk)))
        rq,rk=two(q_,k_,3)
        g2_,g3_=gate((g2_,g3_),q_)
        r3=c.swap(g3_,ga[0])
        g2a,g2b=halves(cat(g2_,r2))
        q_,k_=gate((cat(q_,rq),cat(k_,rk)))
        rq,rk=two(q_,k_,4)
        g2a,g2b,g3_=gate((g2a,g2b,g3_),q_)
        ra,rb=two(g2a,g2b,2)
        x0,g3_=gate((x,cat(g3_,r3)),rq,rk)
        r3=c.swap(g3_,ga[1])
        wq=((q_,rq),pos_a); wk=((k_,rk),pos_b)
        nrm,q,k,v,vec=qkv(x0,first_values,wq,wk,vs,jnp.zeros((nvec,d),f32))
        g2a,g2b,g3_,qa=gate((g2a,g2b,g3_,q),k)
        g2a,g2b,g3_=cat(g2a,ra),cat(g2b,rb),cat(g3_,r3)
        ra,rb=two(g2a,g2b,3)
        w0=hp+1
        c0,l0=afwd(lens,qa,k,v,0,w0)
        o_a,o_b,g3a,g3b,qa=gate(((g2a,ra),(g2b,rb),*halves(g3_),qa),c0)
        abufs=o_a+tuple(c.swap(v_,ga[4]) for v_ in o_a)+o_b+tuple(c.swap(v_,gb_[4]) for v_ in o_b)
        sa,sb=two(g3a,g3b,2)
        c1,l1=afwd(lens,qa,k,v,w0,np_-w0)
        g3a,g3b,x1=gate((g3a,g3b,x),c1,*abufs)
        g3a,g3b=cat(g3a,sa),cat(g3b,sb)
        g3a,g3b,x1=gate((g3a,g3b,x1))
        sa,sb=two(g3a,g3b,3)
        ctxs=[c0,c1]; lse_parts=[l0,l1]
        middle,n2,act,dg,g2=ff_forward(lens,ctxs,x1,cot,abufs,pos_a,pos_b,vec,True)
        d_a,d_b,act1=gate(((g3a,sa),(g3b,sb),act),n2)
        bbufs=tuple(d_a)+tuple(c.swap(v_,ga[4]) for v_ in d_a)+tuple(d_b)+tuple(c.swap(v_,gb_[4]) for v_ in d_b)
    else:
        z=jnp.zeros((1,),jnp.int32)
        ag=lambda v:((lax.all_gather(v,AXES,axis=0,tiled=True)[None],),z)
        wq,wk,wo,wd=ag(qp),ag(kp),ag(op),ag(down_weight.reshape(-1,d))
        vec=lax.all_gather(vector_pieces,AXES,axis=0,tiled=True).reshape(-1,d).astype(f32)
        nrm,q,k,v,vec=qkv(x,first_values,wq,wk,0,vec)
        (abufs,pos_a),(bbufs,pos_b)=wo,wd
        ctx0,lse0=afwd(lens,q,k,v,0,np_)
        ctxs=[ctx0]; lse_parts=[lse0]
        middle,n2,act,dg,g2=ff_forward(lens,ctxs,x,cot,abufs,pos_a,pos_b,vec,False)
    hb=lambda ac:ff_back(lens,ctxs,middle,ac,dg,g2,abufs,bbufs,pos_a,pos_b,vec,fast)
    if fast:
        s_d=Sum(c,wg([act1,g2],[dict(a=((0,d*u,d),),bs=((1,0,d),),o0=u*n//fan,per=n//fan,col=0,parts=((0,h,0),(h,d,1))) for u in range(fan)],inv,n,rows*fan,d,"dwd",mb=60),(A,B),h)
        act2=exchange([s_d],act,*bbufs)
        out,gp,gb,dm,gc,dl,sv=hb(act2)
        join([s_d],gb); s_d.make()
        n2=exchange([s_d],n2)
        s_u=Sum(c,wg([n2,gp],[dict(a=((0,0,d),),bs=((1,d*u,d),),o0=0,per=n,col=d*u,parts=((0,d,u*2//fan),)) for u in range(fan)],inv,n,rows,ff,"dwu"),(A,B),ff//2)
        back=lambda p,w,qv:abwd(lens,qv,k,v,gc,lse_parts[int(p>=w0)],p-w0*int(p>=w0),dl,p,w,bf if p<hp else f32)
        join([s_d],s_u.send); s_d.make()
        g=[back(0,hp-1,exchange([s_d,s_u],q))]
        join([s_d,s_u],g[0][0]); s_d.make(); s_u.make()
        g.append(back(hp-1,1,exchange([s_d,s_u],q)))
        wide=lambda e0,e1,i,at:((at,0,e0[i].shape[1]),(at+1,0,e1[i].shape[1]))
        s_1=Sum(c,wg([gate(nrm,g[1][0])]+[e[i] for i in range(3) for e in g]+[gb]+ctxs,
            [dict(a=tuple((8+i,0,v_.shape[1]) for i,v_ in enumerate(ctxs)),bs=((7,0,d),),o0=0,per=n,col=2*h+dv,parts=((0,d,1),))]
            +[dict(a=((0,0,d),),bs=sum((wide(g[0],g[1],i,1+2*i) for i in range(3)),()),o0=0,per=n,col=0,parts=((0,2*h+dv,0),))],inv,n,rows,2*h+dv+d,"dw1"),(A,B),2*h+dv)
        join([s_d,s_u],s_1.send); s_d.make(); s_u.make()
        late=back(w0,hp-1,exchange([s_d,s_u,s_1],q))
        join([s_d,s_u,s_1],late[0]); s_u.make(); s_1.make()
        g+=[back(hp,1,exchange([s_u,s_1],q)),late]
        gh,sv,vg=qkv_back(gate(x,g[2][0]),dm,vec,sv,[e[0] for e in g],[e[1] for e in g],[e[2] for e in g[:2]],wq,wk,vs,n)
        join([s_u,s_1],gh); s_u.make(); s_1.make()
        vg=exchange([s_u,s_1],vg)
        s_2=Sum(c,wg([nrm]+[e[i] for i in range(2) for e in g[2:]]+[vg],[dict(a=((0,0,d),),bs=sum((wide(g[2],g[3],i,1+2*i) for i in range(2)),()),o0=0,per=n,col=0,parts=((0,2*h,0),))],inv,n,rows,2*h+128,"dw2",raw=True),(A,A),2*h+128)
        join([s_u,s_1],s_2.send)
        exchange([s_2],()); s_1.make(); exchange([s_1],())
        join([s_1,s_2])
        s_2.wide(); s_2.wide_step()
        s_1.make(); s_1.step()
        s_2.wide(); s_2.wide_step()
        t_d,t_u,t_1,t_2=(st.total() for st in (s_d,s_u,s_1,s_2))
        t_o=t_1[:,2*h+dv:]; gf=jnp.concatenate([g[2][2],g[3][2]],axis=1); gvec=t_2[:-(-vs//128),2*h:].reshape(-1)[:vs]
    else:
        out,gp,gb,dm,gc,dl,sv=hb(act)
        g=[abwd(lens,q,k,v,gc,lse_parts[0],p,dl,p,hp,bf if p<hp else f32) for p in (0,hp)]
        pc=lambda a,b,tn,name:wg_natural(a,b,768,tn,name).reshape(n,-1,b.shape[1])
        dq,dk,dfg=(jnp.concatenate([e[i] for e in (g if i<2 else g[:1])],axis=1) for i in range(3))
        gf=g[1][2]
        t_d=scatter_sum(c,pc(act,g2,768,"dwd"),A); t_u=scatter_sum(c,pc(n2,gp,768,"dwu"),B); t_o=scatter_sum(c,pc(ctxs[0],gb,768,"dwo"),A)
        t_1=scatter_sum(c,jnp.concatenate([pc(nrm,dq[:,:h],h,"dwqa"),pc(nrm,dk[:,:h],h,"dwka"),pc(nrm,dfg,dv,"dwv")],axis=2),B)
        t_2=scatter_sum(c,jnp.concatenate([pc(nrm,dq[:,h:],h,"dwqb"),pc(nrm,dk[:,h:],h,"dwkb")],axis=2),A)
        gh,sv,_=qkv_back(x,dm,vec,sv,[dq],[dk],[dfg],wq,wk)
        gvec=scatter_sum(c,sv[:nvec].reshape(n,1,vs),A).reshape(-1)
    gq=jnp.concatenate([t_1[:,:h],t_2[:,:h]],axis=1).reshape(-1)
    gk=jnp.concatenate([t_1[:,h:2*h],t_2[:,h:2*h]],axis=1).reshape(-1)
    gv=t_1[:,2*h:2*h+dv].reshape(-1)
    return (out,gh,gf,gq,gk,gv,t_o.reshape(-1),t_u.reshape(-1),t_d.reshape(-1),gvec)

def solution(mesh):
    s2=P(AXES,None); s1=P(AXES)
    return jax.shard_map(functools.partial(shards,dict(mesh.shape)),mesh=mesh,in_specs=(s2,)*4+(s1,)*7,out_specs=(s2,)*3+(s1,)*7,check_vma=False)
```

```python
import functools, math
import jax, jax.numpy as jnp
from jax import lax
from jax.experimental import pallas as pl
from jax.experimental.pallas import tpu as pltpu
bf=jnp.bfloat16; f32=jnp.float32
NT=(((1,),(1,)),((),()))
TN=(((0,),(0,)),((),()))
NN=(((1,),(0,)),((),()))
def dot(a,b,dn=NN):
    return lax.dot_general(a,b,dn,preferred_element_type=f32)
def cp(mb):
    return pltpu.CompilerParams(vmem_limit_bytes=mb<<20)
def full(shape):
    nd=len(shape)
    return pl.BlockSpec(shape,lambda *a:(0,)*nd)
def cost(fl,by,tr=0):
    return pl.CostEstimate(flops=1000,bytes_accessed=1000,transcendentals=0)

def norm_stats(v):
    c=v-jnp.mean(v,axis=-1,keepdims=True)
    r=lax.rsqrt(jnp.mean(c*c,axis=-1,keepdims=True)+1e-5)
    return c*r,r

ANY=pl.BlockSpec(memory_space=pl.ANY)
def stage(n,rows,cols):
    return pltpu.VMEM((n,rows,cols) if rows%16 else (1,16,128),bf)
def place(bufs,pos_ref,w_ref,st_ref,sem,col=0):
    rows,w=bufs[0].shape[1:]
    p=0
    for b in bufs:
        for a in range(b.shape[0]):
            if rows%16: to=st_ref.at[pos_ref[p],:,pl.ds(col,w)]
            else: to=w_ref.at[pl.ds(pl.multiple_of(pos_ref[p]*rows,16),rows),pl.ds(col,w)]
            pltpu.make_async_copy(b.at[a],to,sem).start()
            p+=1
def placed(w_ref,st_ref,sem,rows):
    if rows%16==0:
        pltpu.make_async_copy(w_ref,w_ref,sem).wait()
        return
    pltpu.make_async_copy(st_ref,st_ref,sem).wait()
    k=16//math.gcd(rows,16); cols=w_ref.shape[1]
    def move(u,_):
        v=jnp.concatenate([st_ref[k*u+i,:,0:cols].astype(f32) for i in range(k)],axis=0)
        w_ref[pl.ds(pl.multiple_of(u*(k*rows),16),k*rows),:]=v.astype(bf)
        return 0
    lax.fori_loop(0,st_ref.shape[0]//k,move,0)
def cs_(v): return jnp.sum(v,axis=0,keepdims=True)

def qkv_body(pa_ref,pb_ref,x_ref,first_ref,vin_ref,*refs,na,nb,per):
    abufs=refs[:na]; bbufs=refs[na:na+nb]
    n_ref,q_ref,k_ref,v_ref,vec_ref,wa,wb,sa,sb,flat,sems=refs[na+nb:]
    d=x_ref.shape[1]; w=first_ref.shape[1]
    @pl.when(pl.program_id(0)==0)
    def _():
        place(bbufs,pb_ref,wb,sb,sems.at[1]); place(abufs,pa_ref,wa,sa,sems.at[0])
        placed(wb,sb,sems.at[1],bbufs[0].shape[1])
        if per:
            for o in range(sb.shape[0]):
                v=sb[o,:,d:d+128].astype(f32)
                for s in range(-(-per//128)):
                    flat[0:1,per*o+128*s:per*o+128*(s+1)]=v[s:s+1,:]
            for i in range(vec_ref.shape[0]):
                vec_ref[i:i+1,:]=flat[0:1,d*i:d*(i+1)]
        else:
            vec_ref[...]=vin_ref[...]
        placed(wa,sa,sems.at[0],abufs[0].shape[1])
    xh,_=norm_stats(x_ref[...].astype(f32))
    n=(xh*vec_ref[0:1,:]+vec_ref[1:2,:]).astype(bf)
    n_ref[...]=n
    q=(dot(n,wa[:,:d])+vec_ref[2:3,:]).astype(bf)
    q_ref[...]=q*0.125
    k_ref[...]=dot(n,wb[...]).astype(bf)
    v_ref[:,:w]=dot(n,wa[:,d:]).astype(bf)
    v_ref[:,w:]=first_ref[...]
def qkv(x,first,wa,wb,per,vin,tm=256):
    t,d=x.shape; dv=first.shape[1]
    (abufs,pa),(bbufs,pb)=wa,wb
    n=sum(b.shape[0] for b in bbufs); nvec=vin.shape[0]
    row=lambda c:pl.BlockSpec((tm,c),lambda i,*a:(i,0))
    return pl.pallas_call(functools.partial(qkv_body,na=len(abufs),nb=len(bbufs),per=per),
        grid_spec=pltpu.PrefetchScalarGridSpec(num_scalar_prefetch=2,grid=(t//tm,),
            in_specs=[row(d),row(dv),full(vin.shape)]+[ANY]*(len(abufs)+len(bbufs)),
            out_specs=[row(d)]*4+[pl.BlockSpec((nvec,d),lambda i,*a:(0,0))],scratch_shapes=[pltpu.VMEM((d,d+dv),bf),pltpu.VMEM((d,d),bf),stage(n,*abufs[0].shape[1:]),stage(n,*bbufs[0].shape[1:]),pltpu.VMEM((1,nvec*d+256),f32),pltpu.SemaphoreType.DMA((2,))]),
        out_shape=[jax.ShapeDtypeStruct((t,d),bf)]*4+[jax.ShapeDtypeStruct((nvec,d),f32)],compiler_params=cp(22),name="qkv",
        cost_estimate=cost(2*t*d*(2*d+dv),t*d*14+d*d*6))(pa,pb,x,first,vin,*abufs,*bbufs)

def afwd_body(len_ref,q_ref,k_ref,v_ref,o_ref,l_ref,*,bq):
    t=q_ref.shape[0]; half=t//2
    long_bias=jnp.where(len_ref[0]>half,0.0,-1e30)
    dh=q_ref.shape[1]//2
    diag=lax.broadcasted_iota(jnp.int32,(bq,bq),0)>=lax.broadcasted_iota(jnp.int32,(bq,bq),1)
    for i in range(t//bq):
        outs=[]
        for h in range(2):
            q=q_ref[i*bq:(i+1)*bq,h*dh:(h+1)*dh]
            n=(i+1)*bq
            s=dot(q,k_ref[0:n,h*dh:(h+1)*dh],NT)
            parts=[]
            lo=half if i*bq>=half else 0
            if lo: parts.append(s[:,:lo]+long_bias)
            if i*bq>lo: parts.append(s[:,lo:i*bq])
            parts.append(jnp.where(diag,s[:,i*bq:],-1e30))
            s=jnp.concatenate(parts,axis=1) if len(parts)>1 else parts[0]
            m=jnp.max(s,axis=-1,keepdims=True)
            p=jnp.exp(s-m)
            l=jnp.sum(p,axis=-1,keepdims=True)
            o=dot(p.astype(bf),v_ref[0:n,h*dh:(h+1)*dh])
            outs.append((o*(1.0/l)).astype(bf))
            lse=m+jnp.log(l)
            l_ref[0,h:h+1,i*bq:(i+1)*bq]=jnp.transpose(jnp.broadcast_to(lse,(bq,128)))[0:1,:]
        o_ref[i*bq:(i+1)*bq,:]=jnp.concatenate(outs,axis=1)
def afwd(lens,q,k,v,first_pair,pairs,bq=512):
    t=q.shape[0]
    col=pl.BlockSpec((t,128),lambda p,*a:(0,p+first_pair))
    return pl.pallas_call(functools.partial(afwd_body,bq=bq),
        grid_spec=pltpu.PrefetchScalarGridSpec(num_scalar_prefetch=1,grid=(pairs,),in_specs=[col]*3,
            out_specs=[pl.BlockSpec((t,128),lambda p,*a:(0,p)),pl.BlockSpec((1,2,t),lambda p,*a:(p,0,0))]),
        out_shape=[jax.ShapeDtypeStruct((t,pairs*128),bf),jax.ShapeDtypeStruct((pairs,2,t),f32)],compiler_params=cp(30),name="afwd",
        cost_estimate=cost(4*t*t*pairs*128*0.6*4,t*pairs*128*8,t*t*pairs))(lens,q,k,v)

def abwd_body(len_ref,q_ref,k_ref,v_ref,do_ref,l_ref,dl_ref,dq_ref,dk_ref,dv_ref,*,bk,first_pair,dqt):
    t=q_ref.shape[0]; half=t//2
    long_bias=jnp.where(len_ref[0]>half,0.0,-1e30)
    dh=q_ref.shape[1]//2
    p_id=pl.program_id(0)+first_pair
    diag=lax.broadcasted_iota(jnp.int32,(bk,bk),0)<=lax.broadcasted_iota(jnp.int32,(bk,bk),1)
    dqs=[]
    dks=[]; dvs=[]
    for h in range(2):
        sl=slice(h*dh,(h+1)*dh)
        lrow=l_ref[0,h:h+1,:]; drow=dl_ref[pl.ds(2*p_id+h,1),:]
        dq=None; dkh=[]; dvh=[]
        for j in range(t//bk):
            k=k_ref[j*bk:(j+1)*bk,sl]; v=v_ref[j*bk:(j+1)*bk,sl]
            a=j*bk
            q=q_ref[a:,sl]; do=do_ref[a:,sl]
            st=dot(k,q,NT)
            pieces=[jnp.where(diag,st[:,:bk],-1e30)]
            hi=max(half,a+bk) if a<half else t
            if hi>a+bk: pieces.append(st[:,bk:hi-a])
            if a<half: pieces.append(st[:,hi-a:]+long_bias)
            st=jnp.concatenate(pieces,axis=1) if len(pieces)>1 else pieces[0]
            p=jnp.exp(st-lrow[:,a:])
            dp=dot(v,do,NT)
            ds=(p*(dp-drow[:,a:])).astype(bf)
            dvh.append(dot(p.astype(bf),do))
            dkh.append(dot(ds,q))
            if dqt: c=dot(k,ds,TN)
            else: c=dot(ds,k,TN)
            ax=1 if dqt else 0
            if dq is None: dq=c
            else:
                if dqt: dq=jnp.concatenate([dq[:,:a],dq[:,a:]+c],axis=1)
                else: dq=jnp.concatenate([dq[:a],dq[a:]+c],axis=0)
        dqs.append(jnp.transpose(dq) if dqt else dq)
        dks.append(jnp.concatenate(dkh,axis=0)); dvs.append(jnp.concatenate(dvh,axis=0))
    dq_ref[...]=(jnp.concatenate(dqs,axis=1)*0.125).astype(bf)
    dk_ref[...]=jnp.concatenate(dks,axis=1).astype(bf)
    dv_ref[...]=jnp.concatenate(dvs,axis=1).astype(dv_ref.dtype)
def abwd(lens,q,k,v,do,lse,lse_pair,delta,first_pair,pairs,dv_dtype,bk=256,dqt=True):
    t,d=q.shape
    col=pl.BlockSpec((t,128),lambda p,*a:(0,p+first_pair))
    ocol=pl.BlockSpec((t,128),lambda p,*a:(0,p))
    st=[pl.BlockSpec((1,2,t),lambda p,*a:(p+lse_pair,0,0)),pl.BlockSpec((16,t),lambda p,*a:(0,0))]
    w=pairs*128
    return pl.pallas_call(functools.partial(abwd_body,bk=bk,first_pair=first_pair,dqt=dqt),
        grid_spec=pltpu.PrefetchScalarGridSpec(num_scalar_prefetch=1,grid=(pairs,),in_specs=[col]*4+st,
            out_specs=[ocol]*3),
        out_shape=[jax.ShapeDtypeStruct((t,w),bf)]*2+[jax.ShapeDtypeStruct((t,w),dv_dtype)],compiler_params=cp(24),name="abwd",
        cost_estimate=cost(10*t*t*w*0.6*4,t*w*16,t*t*w//64*0.6))(lens,q,k,v,do,lse,delta)

def place_both(bufs,pa_ref,pb_ref,w_ref,st_ref,sem,split):
    h=len(bufs)//2
    if split:
        place(bufs[:h],pa_ref,w_ref,st_ref,sem); place(bufs[h:],pb_ref,w_ref,st_ref,sem,w_ref.shape[1]//2)
    else:
        place(bufs,pa_ref,w_ref,st_ref,sem)
def ff_body(len_ref,pa_ref,pb_ref,*refs,nc,na,split):
    ctxs=refs[:nc]; x_ref,cot_ref,vec_ref=refs[nc:nc+3]; refs=refs[nc+3:]
    abufs=refs[:na]
    mid_ref,n2_ref,act_ref,dg_ref,g2_ref,wa,sa,sems=refs[na:]
    tm=x_ref.shape[0]; d=x_ref.shape[1]; fc=d; ff=act_ref.shape[1]
    i=pl.program_id(0)
    @pl.when(i==0)
    def _():
        place_both(abufs,pa_ref,pb_ref,wa,sa,sems.at[0],split)
        placed(wa,sa,sems.at[0],abufs[0].shape[1])
    pos=lax.broadcasted_iota(jnp.int32,(tm,1),0)+i*tm
    live=jnp.where(pos<len_ref[0]+len_ref[1],1.0,0.0)
    g2_ref[...]=(cot_ref[...].astype(f32)*live).astype(bf)
    ctx=jnp.concatenate([c[...] for c in ctxs],axis=1)
    middle=x_ref[...].astype(f32)+(dot(ctx,wa[:,0:d])+vec_ref[3:4,:])
    mid_ref[...]=middle
    xh,_=norm_stats(middle)
    n2=(xh*vec_ref[4:5,:]+vec_ref[5:6,:]).astype(bf)
    n2_ref[...]=n2
    for c in range(ff//fc):
        cs=slice(c*fc,(c+1)*fc)
        h=dot(n2,wa[:,d+c*fc:d+(c+1)*fc])+vec_ref[7+c:8+c,:]
        h2=h*h
        e=jnp.exp(h*(-1.5957691216057308-(1.5957691216057308*0.044715)*h2))
        u=1.0/(1.0+e)
        hu=h*u
        act_ref[:,cs]=hu.astype(bf)
        dg_ref[:,cs]=(u+(hu-hu*u)*(1.5957691216057308+(3*1.5957691216057308*0.044715)*h2)).astype(bf)
def ff_forward(lens,ctxs,x,cot,abufs,pa,pb,vec,split,tm=256):
    t,d=x.shape; ff=(vec.shape[0]-7)*d
    row=lambda c:pl.BlockSpec((tm,c),lambda i,*a:(i,0))
    sd=jax.ShapeDtypeStruct
    return pl.pallas_call(functools.partial(ff_body,nc=len(ctxs),na=len(abufs),split=split),
        grid_spec=pltpu.PrefetchScalarGridSpec(num_scalar_prefetch=3,grid=(t//tm,),
            in_specs=[row(c.shape[1]) for c in ctxs]+[row(d)]*2+[full(vec.shape)]+[ANY]*len(abufs),
            out_specs=[row(d),row(d),row(ff),row(ff),row(d)],
            scratch_shapes=[pltpu.VMEM((d,d+ff),bf),stage(d//abufs[0].shape[1],abufs[0].shape[1],d+ff),pltpu.SemaphoreType.DMA((1,))]),
        out_shape=[sd((t,d),f32),sd((t,d),bf),sd((t,ff),bf),sd((t,ff),bf),sd((t,d),bf)],
        compiler_params=cp(60),name="ffward",cost_estimate=cost(0,0))(lens,pa,pb,*ctxs,x,cot,vec,*abufs)

def mid_body(len_ref,pa_ref,pb_ref,*refs,heads,nc,na,nb,split):
    ctxs=refs[:nc]; mid_ref,act_ref,dg_ref,cot_ref,vec_ref=refs[nc:nc+5]; refs=refs[nc+5:]
    abufs=refs[:na]; bbufs=refs[na:na+nb]
    out_ref,gp_ref,gb_ref,dm_ref,gc_ref,dl_ref,s_ref,wa,sa,wd_ref,sems=refs[na+nb:]
    tm=mid_ref.shape[0]; d=mid_ref.shape[1]; ff=wd_ref.shape[0]; fc=d
    i=pl.program_id(0)
    @pl.when(i==0)
    def _():
        place_both(abufs,pa_ref,pb_ref,wa,sa,sems.at[0],split)
        place_both(bbufs,pa_ref if split else pb_ref,pb_ref,wd_ref,None,sems.at[1],split)
        s_ref[...]=jnp.zeros_like(s_ref)
        placed(wa,sa,sems.at[0],abufs[0].shape[1]); placed(wd_ref,None,sems.at[1],bbufs[0].shape[1])
    gain=vec_ref[4:5,:]
    pos=lax.broadcasted_iota(jnp.int32,(tm,1),0)+i*tm
    live=jnp.where(pos<len_ref[0]+len_ref[1],1.0,0.0)
    ctx=jnp.concatenate([c[...] for c in ctxs],axis=1)
    middle=mid_ref[...]
    g2=cot_ref[...]; gr=g2.astype(f32)
    acc=jnp.zeros((tm,d),f32); dn=jnp.zeros((tm,d),f32)
    for c in range(ff//fc):
        cs=slice(c*fc,(c+1)*fc)
        da=dot(g2,wd_ref[cs,:],NT)
        gpb=(da*dg_ref[:,cs].astype(f32)).astype(bf)
        gp_ref[:,cs]=gpb
        s_ref[7+c:8+c,:]+=cs_(gpb.astype(f32))
        acc=acc+dot(act_ref[:,cs],wd_ref[cs,:])
        dn=dn+dot(gpb,wa[:,d+c*fc:d+(c+1)*fc],NT)
    out_ref[...]=((middle+(acc+vec_ref[6:7,:]))*live).astype(bf)
    xh,r=norm_stats(middle)
    e=dn*gain
    dm=gr+r*(e-jnp.mean(e,axis=-1,keepdims=True)-xh*jnp.mean(e*xh,axis=-1,keepdims=True))
    dm_ref[...]=dm
    gb=dm.astype(bf)
    gb_ref[...]=gb
    gc=dot(gb,wa[:,0:d],NT).astype(bf)
    gc_ref[...]=gc
    pr=gc.astype(f32)*ctx.astype(f32)
    hi=pr.astype(bf); lo=(pr-hi.astype(f32)).astype(bf)
    dh=d//heads
    ind=(lax.broadcasted_iota(jnp.int32,(16,d),1)//dh==lax.broadcasted_iota(jnp.int32,(16,d),0)).astype(bf)
    dl_ref[...]=dot(ind,hi,NT)+dot(ind,lo,NT)
    s_ref[3:4,:]+=cs_(gb.astype(f32))
    s_ref[4:5,:]+=cs_(dn*xh)
    s_ref[5:6,:]+=cs_(dn)
    s_ref[6:7,:]+=cs_(gr)
def ff_back(lens,ctxs,middle,act,dg,g2,abufs,bbufs,pa,pb,vec,split,heads=12,tm=256):
    t,d=middle.shape; ff=act.shape[1]
    row=lambda c:pl.BlockSpec((tm,c),lambda i,*a:(i,0))
    sd=jax.ShapeDtypeStruct
    return pl.pallas_call(functools.partial(mid_body,heads=heads,nc=len(ctxs),na=len(abufs),nb=len(bbufs),split=split),
        grid_spec=pltpu.PrefetchScalarGridSpec(num_scalar_prefetch=3,grid=(t//tm,),
            in_specs=[row(c.shape[1]) for c in ctxs]+[row(d),row(ff),row(ff),row(d)]+[full(vec.shape)]+[ANY]*(len(abufs)+len(bbufs)),
            out_specs=[row(d),row(ff),row(d),row(d),row(d),pl.BlockSpec((16,tm),lambda i,*a:(0,i)),full((16,d))],
            scratch_shapes=[pltpu.VMEM((d,d+ff),bf),stage(d//abufs[0].shape[1],abufs[0].shape[1],d+ff),pltpu.VMEM((ff,d),bf),pltpu.SemaphoreType.DMA((2,))]),
        out_shape=[sd((t,d),bf),sd((t,ff),bf),sd((t,d),bf),sd((t,d),f32),sd((t,d),bf),sd((16,t),f32),sd((16,d),f32)],
        compiler_params=cp(46),name="ffback",cost_estimate=cost(0,0))(lens,pa,pb,*ctxs,middle,act,dg,g2,vec,*abufs,*bbufs)

def wg_body(inv_ref,*refs,na,tasks,pieces,nbuf,raw):
    arrs=refs[:na]; keep_ref,send_ref=refs[na:na+2]; bufs=refs[na+2:na+2+nbuf]
    outs=refs[na+2+nbuf:-2]; isem,osem=refs[-2:]
    half=pieces//2
    if raw: pltpu.make_async_copy(arrs[-1],bufs[-1],isem.at[nbuf-1]).start()
    need=[]; loads={}; k=0
    for t in tasks:
        ids=[]
        for key in tuple(t["a"])+tuple(t["bs"]):
            if key not in loads:
                ai,c0,w=key
                pltpu.make_async_copy(arrs[ai].at[:,pl.ds(c0,w)],bufs[k],isem.at[k]).start()
                loads[key]=k; k+=1
            ids.append(loads[key])
        need.append(ids)
    if raw:
        src_ref=bufs[-1]; last=pl.ds(keep_ref.shape[2]-src_ref.shape[2],src_ref.shape[2])
        pltpu.make_async_copy(src_ref,src_ref,isem.at[nbuf-1]).wait()
        for o in range(pieces):
            r=inv_ref[0,o]
            part=src_ref.at[o]
            @pl.when(r<half)
            def _(): pltpu.make_async_copy(part,keep_ref.at[r,:,last],osem.at[len(tasks)]).start()
            @pl.when(r>=half)
            def _(): pltpu.make_async_copy(part,send_ref.at[r-half,:,last],osem.at[len(tasks)]).start()
    ready=set()
    for ti,(t,ids) in enumerate(zip(tasks,need)):
        for b in ids:
            if b not in ready:
                pltpu.make_async_copy(bufs[b],bufs[b],isem.at[b]).wait(); ready.add(b)
        ka=len(t["a"]); lhs=[bufs[b][...] for b in ids[:ka]]
        lhs=jnp.concatenate(lhs,axis=1) if ka>1 else lhs[0]
        rhs=[bufs[b][...] for b in ids[ka:]]
        rhs=jnp.concatenate(rhs,axis=1) if len(rhs)>1 else rhs[0]
        scr=outs[ti]
        acc=dot(lhs,rhs,TN)
        rows,w=scr.shape[1:]
        for p in range(t["per"]): scr[p]=acc[p*rows:(p+1)*rows].astype(bf)
        for p,(lo,hi,which) in ((p,c) for p in range(t["per"]) for c in t["parts"]):
            r=inv_ref[which,t["o0"]+p]
            src=scr.at[p,:,pl.ds(lo,hi-lo)]
            cols=pl.ds(t["col"]+lo,hi-lo)
            @pl.when(r<half)
            def _(): pltpu.make_async_copy(src,keep_ref.at[r,:,cols],osem.at[ti]).start()
            @pl.when(r>=half)
            def _(): pltpu.make_async_copy(src,send_ref.at[r-half,:,cols],osem.at[ti]).start()
    for ti in range(len(tasks)):
        pltpu.make_async_copy(outs[ti],outs[ti],osem.at[ti]).wait()
    if raw: pltpu.make_async_copy(src_ref,src_ref,osem.at[len(tasks)]).wait()
def wg(arrs,tasks,inv,pieces,rows,width,name,raw=False,mb=28):
    t=arrs[0].shape[0]
    keys=[]; fl=0
    for k in tasks:
        for key in tuple(k["a"])+tuple(k["bs"]):
            if key not in keys: keys.append(key)
        fl+=2*t*sum(a[2] for a in k["a"])*sum(b[2] for b in k["bs"])
    sh=jax.ShapeDtypeStruct((pieces//2,rows,width),bf)
    return pl.pallas_call(functools.partial(wg_body,na=len(arrs),tasks=tasks,pieces=pieces,nbuf=len(keys)+raw,raw=raw),
        grid_spec=pltpu.PrefetchScalarGridSpec(num_scalar_prefetch=1,grid=(),in_specs=[ANY]*len(arrs),out_specs=[ANY,ANY],
            scratch_shapes=[pltpu.VMEM((t,w),bf) for _,_,w in keys]+[pltpu.VMEM(arrs[-1].shape,bf)]*raw+[pltpu.VMEM((k["per"],sum(a[2] for a in k["a"])//k["per"],sum(b[2] for b in k["bs"])),bf) for k in tasks]
                +[pltpu.SemaphoreType.DMA((len(keys)+1,)),pltpu.SemaphoreType.DMA((len(tasks)+1,))]),
        out_shape=[sh,sh],compiler_params=cp(mb),name=name,
        cost_estimate=cost(fl,pieces*rows*width*2+sum(t*k[2]*2 for k in keys)))(inv,*arrs)

def wgn_body(a_ref,b_ref,o_ref):
    o_ref[...]=dot(a_ref[...],b_ref[...],TN).astype(o_ref.dtype)
def wg_natural(a,b,tm,tn,name):
    t,m=a.shape; n=b.shape[1]
    return pl.pallas_call(wgn_body,grid=(m//tm,n//tn),
        in_specs=[pl.BlockSpec((t,tm),lambda i,j:(0,i)),pl.BlockSpec((t,tn),lambda i,j:(0,j))],
        out_specs=pl.BlockSpec((tm,tn),lambda i,j:(i,j)),
        out_shape=jax.ShapeDtypeStruct((m,n),bf),compiler_params=cp(60),name=name,
        cost_estimate=cost(2*t*m*n,t*(m+n)*2+m*n*2))(a,b)

def qb_body(pa_ref,pb_ref,x_ref,dm_ref,vec_ref,s_in_ref,*refs,nq,nf,na,nb,per):
    dqs=refs[:nq]; dks=refs[nq:2*nq]; dfs=refs[2*nq:2*nq+nf]; refs=refs[2*nq+nf:]
    abufs=refs[:na]; bbufs=refs[na:na+nb]
    gh_ref,s_ref,vg_ref,wa,wb,sa,sb,flat,vgf,sems=refs[na+nb:]
    i=pl.program_id(0)
    d=x_ref.shape[1]; dv=wa.shape[1]-d
    @pl.when(i==0)
    def _():
        place(abufs,pa_ref,wa,sa,sems.at[0]); place(bbufs,pb_ref,wb,sb,sems.at[1])
        s_ref[...]=s_in_ref[...]
        placed(wa,sa,sems.at[0],abufs[0].shape[1]); placed(wb,sb,sems.at[1],bbufs[0].shape[1])
    dq=jnp.concatenate([v[...] for v in dqs],axis=1)
    dqv=jnp.concatenate([dq]+[v[...] for v in dfs],axis=1)
    dk=jnp.concatenate([v[...] for v in dks],axis=1)
    dn=dot(dqv,wa[...],NT)+dot(dk,wb[...],NT)
    xh,r=norm_stats(x_ref[...].astype(f32))
    e=dn*vec_ref[0:1,:]
    gh_ref[...]=dm_ref[...]+r*(e-jnp.mean(e,axis=-1,keepdims=True)-xh*jnp.mean(e*xh,axis=-1,keepdims=True))
    s_ref[0:1,:]+=cs_(dn*xh)
    s_ref[1:2,:]+=cs_(dn)
    s_ref[2:3,:]+=cs_(dq.astype(f32))
    if per:
        @pl.when(i==pl.num_programs(0)-1)
        def _():
            vgf[...]=jnp.zeros_like(vgf)
            for u in range((flat.shape[1]-128*3)//d):
                flat[0:1,d*u:d*(u+1)]=s_ref[u:u+1,:]
            for o in range(vgf.shape[0]):
                for s in range(-(-per//128)):
                    vgf[o,s:s+1,:]=flat[0:1,per*o+128*s:per*o+128*(s+1)]
            vg_ref[...]=vgf[...].astype(bf)
def qkv_back(x,dm,vec,s_in,dqs,dks,dfs,wa,wb,per=0,n=1,tm=256):
    vgs=(n,x.shape[1]//n,128) if per else (1,16,128)
    t,d=x.shape; dv=sum(v.shape[1] for v in dfs)
    (abufs,pa),(bbufs,pb)=wa,wb
    row=lambda c:pl.BlockSpec((tm,c),lambda i,*a:(i,0))
    return pl.pallas_call(functools.partial(qb_body,nq=len(dqs),nf=len(dfs),na=len(abufs),nb=len(bbufs),per=per),
        grid_spec=pltpu.PrefetchScalarGridSpec(num_scalar_prefetch=2,grid=(t//tm,),
            in_specs=[row(d),row(d),full(vec.shape),full(s_in.shape)]+[row(v.shape[1]) for v in dqs+dks+dfs]+[ANY]*(len(abufs)+len(bbufs)),
            out_specs=[row(d),full(s_in.shape),full(vgs)],scratch_shapes=[pltpu.VMEM((d,d+dv),bf),pltpu.VMEM((d,d),bf),stage(n,*abufs[0].shape[1:]),stage(n,*bbufs[0].shape[1:]),pltpu.VMEM((1,vec.shape[0]*d+128*3),f32),pltpu.VMEM(vgs,f32),pltpu.SemaphoreType.DMA((2,))]),
        out_shape=[jax.ShapeDtypeStruct((t,d),f32),jax.ShapeDtypeStruct(s_in.shape,f32),jax.ShapeDtypeStruct(vgs,bf)],compiler_params=cp(24),name="qkvback",
        cost_estimate=cost(2*t*d*(2*d+dv),t*d*16+d*d*5))(pa,pb,x,dm,vec,s_in,*dqs,*dks,*dfs,*abufs,*bbufs)
import numpy as np
from jax.sharding import PartitionSpec as P
AXES=("dp","sub")

def index_bits(sizes):
    return [(a,b) for a in reversed(AXES) for b in range(sizes[a].bit_length()-1)]

def swap(v,axis,bit,size):
    return lax.ppermute(v,axis,[(i,i^(1<<bit)) for i in range(size)])

def masks(order):
    p=np.arange(1<<len(order))
    return sum(((p>>s)&1)<<b for s,b in enumerate(order)).astype(np.int32)

class Comm:
    def __init__(self,sizes):
        self.sizes=sizes; self.n=sizes["dp"]*sizes["sub"]
        self.bits=index_bits(sizes); self.nb=len(self.bits)
        self.me=lax.axis_index("dp")*sizes["sub"]+lax.axis_index("sub")
    def cross(self,v,mask):
        return lax.ppermute(v,AXES,[(i,i^mask) for i in range(self.n)])
    def swap(self,v,b):
        axis,k=self.bits[b]
        return swap(v,axis,k,self.sizes[axis])

def gate(nxt,*done):
    return lax.optimization_barrier((nxt,done))[0]

def scatter_sum(c,g,order):
    n,rows,cols=g.shape
    left=list(reversed(range(c.nb)))
    dt=g.dtype
    g=g.reshape((2,)*c.nb+(rows,cols))
    for step,b in enumerate(order):
        axis,k=c.bits[b]
        mine=(lax.axis_index(axis)>>k)&1
        pos=left.index(b); left.pop(pos)
        send=lax.dynamic_index_in_dim(g,1-mine,pos,keepdims=False)
        keep=lax.dynamic_index_in_dim(g,mine,pos,keepdims=False)
        g=keep.astype(f32)+c.swap(send,b).astype(f32)
        if step<len(order)-1: g=g.astype(dt)
    return g

class Sum:
    def __init__(self,c,pair,orders,cut):
        self.c=c; self.keep=pair[0]; self.orders=orders; self.cut=cut
        self.send=[pair[1]]; self.masks=[1<<orders[0][0]]; self.got=[]; self.s=0
    def step(self):
        self.got.append([self.c.cross(v,m) for v,m in zip(self.send,self.masks)]); self.s+=1
    def part(self,lo,hi,cols):
        w=self.keep.shape[2]
        a,b=(0,self.cut) if cols==0 else (self.cut,w)
        tot=self.keep[lo:hi,:,a:b].astype(f32)
        for s,parts in enumerate(self.got):
            g=parts[cols][lo:hi] if s in (1,2) and self.cut<w else parts[0][lo:hi,:,a:b]
            tot=tot+g.astype(f32)
        return tot
    def both(self,lo,hi):
        if self.cut==self.keep.shape[2]: return self.part(lo,hi,0)
        return jnp.concatenate([self.part(lo,hi,0),self.part(lo,hi,1)],axis=2)
    def make(self):
        w=self.keep.shape[0]>>self.s
        if self.s in (1,2) and self.cut<self.keep.shape[2]:
            self.send=[self.part(w,2*w,i).astype(bf) for i in (0,1)]
            self.masks=[1<<o[self.s] for o in self.orders]
        else:
            self.send=[self.both(w,2*w).astype(bf)]
            self.masks=[1<<self.orders[0][self.s]]
    def wide(self):
        o=self.orders[0]; q=self.keep.shape[0]>>(self.s+1)
        self.send=[self.both(q*g,q*(g+1)).astype(bf) for g in (1,2,3)]
        self.masks=[((g>>1)<<o[self.s])|((g&1)<<o[self.s+1]) for g in (1,2,3)]
    def wide_step(self):
        for v,m in zip(self.send,self.masks): self.got.append([self.c.cross(v,m)])
        self.s+=2
    def total(self):
        return self.both(0,1)[0]

def exchange(sums,nxt,*done):
    sends,nxt=gate(([s.send for s in sums],nxt),*done)
    for s,v in zip(sums,sends): s.send=v
    for s in sums: s.step()
    return nxt
def join(sums,*done):
    got=gate([s.got[-1] for s in sums],*done)
    for s,v in zip(sums,got): s.got[-1]=v

def shards(sizes,hidden_in,first_values,doc_lengths,out_cotangent,query_weight,key_weight,value_weight,output_weight,up_weight,down_weight,vector_pieces):
    c=Comm(sizes); n=c.n; nb=c.nb
    t,d=hidden_in.shape; dv=first_values.shape[1]
    ff=up_weight.shape[0]*n//d
    vs=vector_pieces.shape[0]; h=d//2; rows=d//n; fan=ff//d
    fast=n==1<<nb and n==32 and (d//n)%8==0
    lens=doc_lengths[0]
    x=hidden_in; cot=out_cotangent
    s=sizes["sub"].bit_length()-1
    A=list(range(nb)); B=A[:]
    if s>=2 and nb>s: B[1],B[s]=B[s],B[1]
    qp=jnp.concatenate([query_weight.reshape(-1,d),value_weight.reshape(-1,dv)],axis=1)
    kp=key_weight.reshape(-1,d)
    op=jnp.concatenate([output_weight.reshape(-1,d),up_weight.reshape(-1,ff)],axis=1)
    np_=d//128; hp=np_//2; nvec=7+fan
    if fast:
        vp=jnp.pad(jnp.pad(vector_pieces,(0,-vs%128)).reshape(-1,128),((0,rows--(-vs//128)),(0,0)))
        g1=jnp.concatenate([qp,kp,vp],axis=1)[None]
        ga,gb_=A[::-1],B[::-1]
        pos_a=c.me^jnp.asarray(masks(ga)); pos_b=c.me^jnp.asarray(masks(gb_))
        cat=lambda a,b:jnp.concatenate([a,b],axis=0)
        halves=lambda a:(a[:,:,:a.shape[2]//2],a[:,:,a.shape[2]//2:])
        two=lambda a,b,st:(c.swap(a,ga[st]),c.swap(b,gb_[st]))
        z1,z0=1<<ga[0],1<<ga[1]
        r1=[c.cross(g1,m) for m in (z1,z0,z1|z0)]
        g1=jnp.concatenate([g1]+r1,axis=0)
        def inverse(order):
            table=jnp.asarray(np.argsort(masks(order[::-1])).astype(np.int32))
            return jnp.take(table,c.me^jnp.arange(n,dtype=jnp.int32))
        q_,k_,op,inv,pos_a,pos_b=gate((g1[:,:,:d+dv],g1[:,:,d+dv:],op,jnp.stack([inverse(A),inverse(B)]),pos_a,pos_b))
        g2_=op[None]
        rq,rk=two(q_,k_,2)
        r2=c.swap(g2_,ga[0])
        q_,k_=gate((cat(q_,rq),cat(k_,rk)))
        rq,rk=two(q_,k_,3)
        g2_,dw_=gate((g2_,down_weight),q_)
        g2_=cat(g2_,r2)
        r2=c.swap(g2_,ga[1])
        g3_=dw_.reshape(1,fan*rows,d)
        q_,k_=gate((cat(q_,rq),cat(k_,rk)))
        rq,rk=two(q_,k_,4)
        g2_=gate(g2_,q_)
        g2a,g2b=halves(cat(g2_,r2))
        ra,rb=two(g2a,g2b,2)
        x0,g3_=gate((x,g3_),rq,rk)
        r3=c.swap(g3_,ga[0])
        wq=((q_,rq),pos_a); wk=((k_,rk),pos_b)
        nrm,q,k,v,vec=qkv(x0,first_values,wq,wk,vs,jnp.zeros((nvec,d),f32))
        g2a,g2b,g3_,r3,qa=gate((g2a,g2b,g3_,r3,q),k)
        g2a,g2b,g3_=cat(g2a,ra),cat(g2b,rb),cat(g3_,r3)
        ra,rb=two(g2a,g2b,3)
        r3=c.swap(g3_,ga[1])
        w0=hp+1
        c0,l0=afwd(lens,qa,k,v,0,w0)
        o_a,o_b,g3_,r3,qa=gate(((g2a,ra),(g2b,rb),g3_,r3,qa),c0)
        g3a,g3b=halves(cat(g3_,r3))
        abufs=o_a+tuple(c.swap(v_,ga[4]) for v_ in o_a)+o_b+tuple(c.swap(v_,gb_[4]) for v_ in o_b)
        sa,sb=two(g3a,g3b,2)
        c1,l1=afwd(lens,qa,k,v,w0,np_-w0)
        g3a,g3b,x1=gate((g3a,g3b,x),c1,*abufs)
        g3a,g3b=cat(g3a,sa),cat(g3b,sb)
        g3a,g3b,x1=gate((g3a,g3b,x1))
        sa,sb=two(g3a,g3b,3)
        ctxs=[c0,c1]; lse_parts=[l0,l1]
        middle,n2,act,dg,g2=ff_forward(lens,ctxs,x1,cot,abufs,pos_a,pos_b,vec,True)
        d_a,d_b,act1=gate(((g3a,sa),(g3b,sb),act),n2)
        bbufs=tuple(d_a)+tuple(c.swap(v_,ga[4]) for v_ in d_a)+tuple(d_b)+tuple(c.swap(v_,gb_[4]) for v_ in d_b)
    else:
        z=jnp.zeros((1,),jnp.int32)
        ag=lambda v:((lax.all_gather(v,AXES,axis=0,tiled=True)[None],),z)
        wq,wk,wo,wd=ag(qp),ag(kp),ag(op),ag(down_weight.reshape(-1,d))
        vec=lax.all_gather(vector_pieces,AXES,axis=0,tiled=True).reshape(-1,d).astype(f32)
        nrm,q,k,v,vec=qkv(x,first_values,wq,wk,0,vec)
        (abufs,pos_a),(bbufs,pos_b)=wo,wd
        ctx0,lse0=afwd(lens,q,k,v,0,np_)
        ctxs=[ctx0]; lse_parts=[lse0]
        middle,n2,act,dg,g2=ff_forward(lens,ctxs,x,cot,abufs,pos_a,pos_b,vec,False)
    hb=lambda ac:ff_back(lens,ctxs,middle,ac,dg,g2,abufs,bbufs,pos_a,pos_b,vec,fast)
    if fast:
        s_d=Sum(c,wg([act1,g2],[dict(a=((0,d*u,d),),bs=((1,0,d),),o0=u*n//fan,per=n//fan,col=0,parts=((0,h,0),(h,d,1))) for u in range(fan)],inv,n,rows*fan,d,"dwd",mb=60),(A,B),h)
        act2=exchange([s_d],act,*bbufs)
        out,gp,gb,dm,gc,dl,sv=hb(act2)
        join([s_d],gb); s_d.make()
        n2=exchange([s_d],n2)
        s_u=Sum(c,wg([n2,gp],[dict(a=((0,0,d),),bs=((1,d*u,d),),o0=0,per=n,col=d*u,parts=((0,d,u*2//fan),)) for u in range(fan)],inv,n,rows,ff,"dwu"),(A,B),ff//2)
        back=lambda p,w,qv:abwd(lens,qv,k,v,gc,lse_parts[int(p>=w0)],p-w0*int(p>=w0),dl,p,w,bf if p<hp else f32)
        join([s_d],s_u.send); s_d.make()
        g=[back(0,hp-1,exchange([s_d,s_u],q))]
        join([s_d,s_u],g[0][0]); s_d.make(); s_u.make()
        g.append(back(hp-1,1,exchange([s_d,s_u],q)))
        wide=lambda e0,e1,i,at:((at,0,e0[i].shape[1]),(at+1,0,e1[i].shape[1]))
        s_1=Sum(c,wg([gate(nrm,g[1][0])]+[e[i] for i in range(3) for e in g]+[gb]+ctxs,
            [dict(a=tuple((8+i,0,v_.shape[1]) for i,v_ in enumerate(ctxs)),bs=((7,0,d),),o0=0,per=n,col=2*h+dv,parts=((0,d,1),))]
            +[dict(a=((0,0,d),),bs=sum((wide(g[0],g[1],i,1+2*i) for i in range(3)),()),o0=0,per=n,col=0,parts=((0,2*h+dv,0),))],inv,n,rows,2*h+dv+d,"dw1"),(A,B),2*h+dv)
        join([s_d,s_u],s_1.send); s_d.make(); s_u.make()
        late=back(w0,hp-1,exchange([s_d,s_u,s_1],q))
        join([s_d,s_u,s_1],late[0]); s_u.make(); s_1.make()
        g+=[back(hp,1,exchange([s_u,s_1],q)),late]
        gh,sv,vg=qkv_back(gate(x,g[2][0]),dm,vec,sv,[e[0] for e in g],[e[1] for e in g],[e[2] for e in g[:2]],wq,wk,vs,n)
        join([s_u,s_1],gh); s_u.make(); s_1.make()
        vg=exchange([s_u,s_1],vg)
        s_2=Sum(c,wg([nrm]+[e[i] for i in range(2) for e in g[2:]]+[vg],[dict(a=((0,0,d),),bs=sum((wide(g[2],g[3],i,1+2*i) for i in range(2)),()),o0=0,per=n,col=0,parts=((0,2*h,0),))],inv,n,rows,2*h+128,"dw2",raw=True),(A,A),2*h+128)
        join([s_u,s_1],s_2.send)
        exchange([s_2],()); s_1.make(); exchange([s_1],())
        join([s_1,s_2])
        s_2.wide(); s_2.wide_step()
        s_1.make(); s_1.step()
        s_2.wide(); s_2.wide_step()
        t_d,t_u,t_1,t_2=(st.total() for st in (s_d,s_u,s_1,s_2))
        t_o=t_1[:,2*h+dv:]; gf=jnp.concatenate([g[2][2],g[3][2]],axis=1); gvec=t_2[:-(-vs//128),2*h:].reshape(-1)[:vs]
    else:
        out,gp,gb,dm,gc,dl,sv=hb(act)
        g=[abwd(lens,q,k,v,gc,lse_parts[0],p,dl,p,hp,bf if p<hp else f32) for p in (0,hp)]
        pc=lambda a,b,tn,name:wg_natural(a,b,768,tn,name).reshape(n,-1,b.shape[1])
        dq,dk,dfg=(jnp.concatenate([e[i] for e in (g if i<2 else g[:1])],axis=1) for i in range(3))
        gf=g[1][2]
        t_d=scatter_sum(c,pc(act,g2,768,"dwd"),A); t_u=scatter_sum(c,pc(n2,gp,768,"dwu"),B); t_o=scatter_sum(c,pc(ctxs[0],gb,768,"dwo"),A)
        t_1=scatter_sum(c,jnp.concatenate([pc(nrm,dq[:,:h],h,"dwqa"),pc(nrm,dk[:,:h],h,"dwka"),pc(nrm,dfg,dv,"dwv")],axis=2),B)
        t_2=scatter_sum(c,jnp.concatenate([pc(nrm,dq[:,h:],h,"dwqb"),pc(nrm,dk[:,h:],h,"dwkb")],axis=2),A)
        gh,sv,_=qkv_back(x,dm,vec,sv,[dq],[dk],[dfg],wq,wk)
        gvec=scatter_sum(c,sv[:nvec].reshape(n,1,vs),A).reshape(-1)
    gq=jnp.concatenate([t_1[:,:h],t_2[:,:h]],axis=1).reshape(-1)
    gk=jnp.concatenate([t_1[:,h:2*h],t_2[:,h:2*h]],axis=1).reshape(-1)
    gv=t_1[:,2*h:2*h+dv].reshape(-1)
    return (out,gh,gf,gq,gk,gv,t_o.reshape(-1),t_u.reshape(-1),t_d.reshape(-1),gvec)

def solution(mesh):
    s2=P(AXES,None); s1=P(AXES)
    return jax.shard_map(functools.partial(shards,dict(mesh.shape)),mesh=mesh,in_specs=(s2,)*4+(s1,)*7,out_specs=(s2,)*3+(s1,)*7,check_vma=False)
```

```python
import functools, math
import jax, jax.numpy as jnp
from jax import lax
from jax.experimental import pallas as pl
from jax.experimental.pallas import tpu as pltpu
bf=jnp.bfloat16; f32=jnp.float32
NT=(((1,),(1,)),((),()))
TN=(((0,),(0,)),((),()))
NN=(((1,),(0,)),((),()))
def dot(a,b,dn=NN):
    return lax.dot_general(a,b,dn,preferred_element_type=f32)
def cp(mb):
    return pltpu.CompilerParams(vmem_limit_bytes=mb<<20)
def full(shape):
    nd=len(shape)
    return pl.BlockSpec(shape,lambda *a:(0,)*nd)
def cost(fl,by,tr=0):
    return pl.CostEstimate(flops=1000,bytes_accessed=1000,transcendentals=0)

def norm_stats(v):
    c=v-jnp.mean(v,axis=-1,keepdims=True)
    r=lax.rsqrt(jnp.mean(c*c,axis=-1,keepdims=True)+1e-5)
    return c*r,r

ANY=pl.BlockSpec(memory_space=pl.ANY)
def stage(n,rows,cols):
    return pltpu.VMEM((n,rows,cols) if rows%16 else (1,16,128),bf)
def place(bufs,pos_ref,w_ref,st_ref,sem,col=0):
    rows,w=bufs[0].shape[1:]
    p=0
    for b in bufs:
        for a in range(b.shape[0]):
            if rows%16: to=st_ref.at[pos_ref[p],:,pl.ds(col,w)]
            else: to=w_ref.at[pl.ds(pl.multiple_of(pos_ref[p]*rows,16),rows),pl.ds(col,w)]
            pltpu.make_async_copy(b.at[a],to,sem).start()
            p+=1
def placed(w_ref,st_ref,sem,rows):
    if rows%16==0:
        pltpu.make_async_copy(w_ref,w_ref,sem).wait()
        return
    pltpu.make_async_copy(st_ref,st_ref,sem).wait()
    k=16//math.gcd(rows,16); cols=w_ref.shape[1]
    def move(u,_):
        v=jnp.concatenate([st_ref[k*u+i,:,0:cols].astype(f32) for i in range(k)],axis=0)
        w_ref[pl.ds(pl.multiple_of(u*(k*rows),16),k*rows),:]=v.astype(bf)
        return 0
    lax.fori_loop(0,st_ref.shape[0]//k,move,0)
def cs_(v): return jnp.sum(v,axis=0,keepdims=True)

def qkv_body(pa_ref,pb_ref,x_ref,first_ref,vin_ref,*refs,na,nb,per):
    abufs=refs[:na]; bbufs=refs[na:na+nb]
    n_ref,q_ref,k_ref,v_ref,vec_ref,wa,wb,sa,sb,flat,sems=refs[na+nb:]
    d=x_ref.shape[1]; w=first_ref.shape[1]
    @pl.when(pl.program_id(0)==0)
    def _():
        place(bbufs,pb_ref,wb,sb,sems.at[1]); place(abufs,pa_ref,wa,sa,sems.at[0])
        placed(wb,sb,sems.at[1],bbufs[0].shape[1])
        if per:
            for o in range(sb.shape[0]):
                v=sb[o,:,d:d+128].astype(f32)
                for s in range(-(-per//128)):
                    flat[0:1,per*o+128*s:per*o+128*(s+1)]=v[s:s+1,:]
            for i in range(vec_ref.shape[0]):
                vec_ref[i:i+1,:]=flat[0:1,d*i:d*(i+1)]
        else:
            vec_ref[...]=vin_ref[...]
        placed(wa,sa,sems.at[0],abufs[0].shape[1])
    xh,_=norm_stats(x_ref[...].astype(f32))
    n=(xh*vec_ref[0:1,:]+vec_ref[1:2,:]).astype(bf)
    n_ref[...]=n
    q=(dot(n,wa[:,:d])+vec_ref[2:3,:]).astype(bf)
    q_ref[...]=q*0.125
    k_ref[...]=dot(n,wb[...]).astype(bf)
    v_ref[:,:w]=dot(n,wa[:,d:]).astype(bf)
    v_ref[:,w:]=first_ref[...]
def qkv(x,first,wa,wb,per,vin,tm=256):
    t,d=x.shape; dv=first.shape[1]
    (abufs,pa),(bbufs,pb)=wa,wb
    n=sum(b.shape[0] for b in bbufs); nvec=vin.shape[0]
    row=lambda c:pl.BlockSpec((tm,c),lambda i,*a:(i,0))
    return pl.pallas_call(functools.partial(qkv_body,na=len(abufs),nb=len(bbufs),per=per),
        grid_spec=pltpu.PrefetchScalarGridSpec(num_scalar_prefetch=2,grid=(t//tm,),
            in_specs=[row(d),row(dv),full(vin.shape)]+[ANY]*(len(abufs)+len(bbufs)),
            out_specs=[row(d)]*4+[pl.BlockSpec((nvec,d),lambda i,*a:(0,0))],scratch_shapes=[pltpu.VMEM((d,d+dv),bf),pltpu.VMEM((d,d),bf),stage(n,*abufs[0].shape[1:]),stage(n,*bbufs[0].shape[1:]),pltpu.VMEM((1,nvec*d+256),f32),pltpu.SemaphoreType.DMA((2,))]),
        out_shape=[jax.ShapeDtypeStruct((t,d),bf)]*4+[jax.ShapeDtypeStruct((nvec,d),f32)],compiler_params=cp(22),name="qkv",
        cost_estimate=cost(2*t*d*(2*d+dv),t*d*14+d*d*6))(pa,pb,x,first,vin,*abufs,*bbufs)

def afwd_body(len_ref,q_ref,k_ref,v_ref,o_ref,l_ref,*,bq):
    t=q_ref.shape[0]; half=t//2
    long_bias=jnp.where(len_ref[0]>half,0.0,-1e30)
    dh=q_ref.shape[1]//2
    diag=lax.broadcasted_iota(jnp.int32,(bq,bq),0)>=lax.broadcasted_iota(jnp.int32,(bq,bq),1)
    for i in range(t//bq):
        outs=[]
        for h in range(2):
            q=q_ref[i*bq:(i+1)*bq,h*dh:(h+1)*dh]
            n=(i+1)*bq
            s=dot(q,k_ref[0:n,h*dh:(h+1)*dh],NT)
            parts=[]
            lo=half if i*bq>=half else 0
            if lo: parts.append(s[:,:lo]+long_bias)
            if i*bq>lo: parts.append(s[:,lo:i*bq])
            parts.append(jnp.where(diag,s[:,i*bq:],-1e30))
            s=jnp.concatenate(parts,axis=1) if len(parts)>1 else parts[0]
            m=jnp.max(s,axis=-1,keepdims=True)
            p=jnp.exp(s-m)
            l=jnp.sum(p,axis=-1,keepdims=True)
            o=dot(p.astype(bf),v_ref[0:n,h*dh:(h+1)*dh])
            outs.append((o*(1.0/l)).astype(bf))
            lse=m+jnp.log(l)
            l_ref[0,h:h+1,i*bq:(i+1)*bq]=jnp.transpose(jnp.broadcast_to(lse,(bq,128)))[0:1,:]
        o_ref[i*bq:(i+1)*bq,:]=jnp.concatenate(outs,axis=1)
def afwd(lens,q,k,v,first_pair,pairs,bq=512):
    t=q.shape[0]
    col=pl.BlockSpec((t,128),lambda p,*a:(0,p+first_pair))
    return pl.pallas_call(functools.partial(afwd_body,bq=bq),
        grid_spec=pltpu.PrefetchScalarGridSpec(num_scalar_prefetch=1,grid=(pairs,),in_specs=[col]*3,
            out_specs=[pl.BlockSpec((t,128),lambda p,*a:(0,p)),pl.BlockSpec((1,2,t),lambda p,*a:(p,0,0))]),
        out_shape=[jax.ShapeDtypeStruct((t,pairs*128),bf),jax.ShapeDtypeStruct((pairs,2,t),f32)],compiler_params=cp(30),name="afwd",
        cost_estimate=cost(4*t*t*pairs*128*0.6*4,t*pairs*128*8,t*t*pairs))(lens,q,k,v)

def abwd_body(len_ref,q_ref,k_ref,v_ref,do_ref,l_ref,dl_ref,dq_ref,dk_ref,dv_ref,*,bk,first_pair,dqt):
    t=q_ref.shape[0]; half=t//2
    long_bias=jnp.where(len_ref[0]>half,0.0,-1e30)
    dh=q_ref.shape[1]//2
    p_id=pl.program_id(0)+first_pair
    diag=lax.broadcasted_iota(jnp.int32,(bk,bk),0)<=lax.broadcasted_iota(jnp.int32,(bk,bk),1)
    dqs=[]
    dks=[]; dvs=[]
    for h in range(2):
        sl=slice(h*dh,(h+1)*dh)
        lrow=l_ref[0,h:h+1,:]; drow=dl_ref[pl.ds(2*p_id+h,1),:]
        dq=None; dkh=[]; dvh=[]
        for j in range(t//bk):
            k=k_ref[j*bk:(j+1)*bk,sl]; v=v_ref[j*bk:(j+1)*bk,sl]
            a=j*bk
            q=q_ref[a:,sl]; do=do_ref[a:,sl]
            st=dot(k,q,NT)
            pieces=[jnp.where(diag,st[:,:bk],-1e30)]
            hi=max(half,a+bk) if a<half else t
            if hi>a+bk: pieces.append(st[:,bk:hi-a])
            if a<half: pieces.append(st[:,hi-a:]+long_bias)
            st=jnp.concatenate(pieces,axis=1) if len(pieces)>1 else pieces[0]
            p=jnp.exp(st-lrow[:,a:])
            dp=dot(v,do,NT)
            ds=(p*(dp-drow[:,a:])).astype(bf)
            dvh.append(dot(p.astype(bf),do))
            dkh.append(dot(ds,q))
            if dqt: c=dot(k,ds,TN)
            else: c=dot(ds,k,TN)
            ax=1 if dqt else 0
            if dq is None: dq=c
            else:
                if dqt: dq=jnp.concatenate([dq[:,:a],dq[:,a:]+c],axis=1)
                else: dq=jnp.concatenate([dq[:a],dq[a:]+c],axis=0)
        dqs.append(jnp.transpose(dq) if dqt else dq)
        dks.append(jnp.concatenate(dkh,axis=0)); dvs.append(jnp.concatenate(dvh,axis=0))
    dq_ref[...]=(jnp.concatenate(dqs,axis=1)*0.125).astype(bf)
    dk_ref[...]=jnp.concatenate(dks,axis=1).astype(bf)
    dv_ref[...]=jnp.concatenate(dvs,axis=1).astype(dv_ref.dtype)
def abwd(lens,q,k,v,do,lse,lse_pair,delta,first_pair,pairs,dv_dtype,bk=256,dqt=True):
    t,d=q.shape
    col=pl.BlockSpec((t,128),lambda p,*a:(0,p+first_pair))
    ocol=pl.BlockSpec((t,128),lambda p,*a:(0,p))
    st=[pl.BlockSpec((1,2,t),lambda p,*a:(p+lse_pair,0,0)),pl.BlockSpec((16,t),lambda p,*a:(0,0))]
    w=pairs*128
    return pl.pallas_call(functools.partial(abwd_body,bk=bk,first_pair=first_pair,dqt=dqt),
        grid_spec=pltpu.PrefetchScalarGridSpec(num_scalar_prefetch=1,grid=(pairs,),in_specs=[col]*4+st,
            out_specs=[ocol]*3),
        out_shape=[jax.ShapeDtypeStruct((t,w),bf)]*2+[jax.ShapeDtypeStruct((t,w),dv_dtype)],compiler_params=cp(24),name="abwd",
        cost_estimate=cost(10*t*t*w*0.6*4,t*w*16,t*t*w//64*0.6))(lens,q,k,v,do,lse,delta)

def place_both(bufs,pa_ref,pb_ref,w_ref,st_ref,sem,split):
    h=len(bufs)//2
    if split:
        place(bufs[:h],pa_ref,w_ref,st_ref,sem); place(bufs[h:],pb_ref,w_ref,st_ref,sem,w_ref.shape[1]//2)
    else:
        place(bufs,pa_ref,w_ref,st_ref,sem)
def ff_body(len_ref,pa_ref,pb_ref,*refs,nc,na,split):
    ctxs=refs[:nc]; x_ref,cot_ref,vec_ref=refs[nc:nc+3]; refs=refs[nc+3:]
    abufs=refs[:na]
    mid_ref,n2_ref,act_ref,dg_ref,g2_ref,wa,sa,sems=refs[na:]
    tm=x_ref.shape[0]; d=x_ref.shape[1]; fc=d; ff=act_ref.shape[1]
    i=pl.program_id(0)
    @pl.when(i==0)
    def _():
        place_both(abufs,pa_ref,pb_ref,wa,sa,sems.at[0],split)
        placed(wa,sa,sems.at[0],abufs[0].shape[1])
    pos=lax.broadcasted_iota(jnp.int32,(tm,1),0)+i*tm
    live=jnp.where(pos<len_ref[0]+len_ref[1],1.0,0.0)
    g2_ref[...]=(cot_ref[...].astype(f32)*live).astype(bf)
    ctx=jnp.concatenate([c[...] for c in ctxs],axis=1)
    middle=x_ref[...].astype(f32)+(dot(ctx,wa[:,0:d])+vec_ref[3:4,:])
    mid_ref[...]=middle
    xh,_=norm_stats(middle)
    n2=(xh*vec_ref[4:5,:]+vec_ref[5:6,:]).astype(bf)
    n2_ref[...]=n2
    for c in range(ff//fc):
        cs=slice(c*fc,(c+1)*fc)
        h=dot(n2,wa[:,d+c*fc:d+(c+1)*fc])+vec_ref[7+c:8+c,:]
        h2=h*h
        e=jnp.exp(h*(-1.5957691216057308-(1.5957691216057308*0.044715)*h2))
        u=1.0/(1.0+e)
        hu=h*u
        act_ref[:,cs]=hu.astype(bf)
        dg_ref[:,cs]=(u+(hu-hu*u)*(1.5957691216057308+(3*1.5957691216057308*0.044715)*h2)).astype(bf)
def ff_forward(lens,ctxs,x,cot,abufs,pa,pb,vec,split,tm=256):
    t,d=x.shape; ff=(vec.shape[0]-7)*d
    row=lambda c:pl.BlockSpec((tm,c),lambda i,*a:(i,0))
    sd=jax.ShapeDtypeStruct
    return pl.pallas_call(functools.partial(ff_body,nc=len(ctxs),na=len(abufs),split=split),
        grid_spec=pltpu.PrefetchScalarGridSpec(num_scalar_prefetch=3,grid=(t//tm,),
            in_specs=[row(c.shape[1]) for c in ctxs]+[row(d)]*2+[full(vec.shape)]+[ANY]*len(abufs),
            out_specs=[row(d),row(d),row(ff),row(ff),row(d)],
            scratch_shapes=[pltpu.VMEM((d,d+ff),bf),stage(d//abufs[0].shape[1],abufs[0].shape[1],d+ff),pltpu.SemaphoreType.DMA((1,))]),
        out_shape=[sd((t,d),f32),sd((t,d),bf),sd((t,ff),bf),sd((t,ff),bf),sd((t,d),bf)],
        compiler_params=cp(60),name="ffward",cost_estimate=cost(0,0))(lens,pa,pb,*ctxs,x,cot,vec,*abufs)

def mid_body(len_ref,pa_ref,pb_ref,*refs,heads,nc,na,nb,split):
    ctxs=refs[:nc]; mid_ref,act_ref,dg_ref,cot_ref,vec_ref=refs[nc:nc+5]; refs=refs[nc+5:]
    abufs=refs[:na]; bbufs=refs[na:na+nb]
    out_ref,gp_ref,gb_ref,dm_ref,gc_ref,dl_ref,s_ref,wa,sa,wd_ref,sems=refs[na+nb:]
    tm=mid_ref.shape[0]; d=mid_ref.shape[1]; ff=wd_ref.shape[0]; fc=d
    i=pl.program_id(0)
    @pl.when(i==0)
    def _():
        place_both(abufs,pa_ref,pb_ref,wa,sa,sems.at[0],split)
        place_both(bbufs,pa_ref if split else pb_ref,pb_ref,wd_ref,None,sems.at[1],split)
        s_ref[...]=jnp.zeros_like(s_ref)
        placed(wa,sa,sems.at[0],abufs[0].shape[1]); placed(wd_ref,None,sems.at[1],bbufs[0].shape[1])
    gain=vec_ref[4:5,:]
    pos=lax.broadcasted_iota(jnp.int32,(tm,1),0)+i*tm
    live=jnp.where(pos<len_ref[0]+len_ref[1],1.0,0.0)
    ctx=jnp.concatenate([c[...] for c in ctxs],axis=1)
    middle=mid_ref[...]
    g2=cot_ref[...]; gr=g2.astype(f32)
    acc=jnp.zeros((tm,d),f32); dn=jnp.zeros((tm,d),f32)
    for c in range(ff//fc):
        cs=slice(c*fc,(c+1)*fc)
        da=dot(g2,wd_ref[cs,:],NT)
        gpb=(da*dg_ref[:,cs].astype(f32)).astype(bf)
        gp_ref[:,cs]=gpb
        s_ref[7+c:8+c,:]+=cs_(gpb.astype(f32))
        acc=acc+dot(act_ref[:,cs],wd_ref[cs,:])
        dn=dn+dot(gpb,wa[:,d+c*fc:d+(c+1)*fc],NT)
    out_ref[...]=((middle+(acc+vec_ref[6:7,:]))*live).astype(bf)
    xh,r=norm_stats(middle)
    e=dn*gain
    dm=gr+r*(e-jnp.mean(e,axis=-1,keepdims=True)-xh*jnp.mean(e*xh,axis=-1,keepdims=True))
    dm_ref[...]=dm
    gb=dm.astype(bf)
    gb_ref[...]=gb
    gc=dot(gb,wa[:,0:d],NT).astype(bf)
    gc_ref[...]=gc
    pr=gc.astype(f32)*ctx.astype(f32)
    hi=pr.astype(bf); lo=(pr-hi.astype(f32)).astype(bf)
    dh=d//heads
    ind=(lax.broadcasted_iota(jnp.int32,(16,d),1)//dh==lax.broadcasted_iota(jnp.int32,(16,d),0)).astype(bf)
    dl_ref[...]=dot(ind,hi,NT)+dot(ind,lo,NT)
    s_ref[3:4,:]+=cs_(gb.astype(f32))
    s_ref[4:5,:]+=cs_(dn*xh)
    s_ref[5:6,:]+=cs_(dn)
    s_ref[6:7,:]+=cs_(gr)
def ff_back(lens,ctxs,middle,act,dg,g2,abufs,bbufs,pa,pb,vec,split,heads=12,tm=256):
    t,d=middle.shape; ff=act.shape[1]
    row=lambda c:pl.BlockSpec((tm,c),lambda i,*a:(i,0))
    sd=jax.ShapeDtypeStruct
    return pl.pallas_call(functools.partial(mid_body,heads=heads,nc=len(ctxs),na=len(abufs),nb=len(bbufs),split=split),
        grid_spec=pltpu.PrefetchScalarGridSpec(num_scalar_prefetch=3,grid=(t//tm,),
            in_specs=[row(c.shape[1]) for c in ctxs]+[row(d),row(ff),row(ff),row(d)]+[full(vec.shape)]+[ANY]*(len(abufs)+len(bbufs)),
            out_specs=[row(d),row(ff),row(d),row(d),row(d),pl.BlockSpec((16,tm),lambda i,*a:(0,i)),full((16,d))],
            scratch_shapes=[pltpu.VMEM((d,d+ff),bf),stage(d//abufs[0].shape[1],abufs[0].shape[1],d+ff),pltpu.VMEM((ff,d),bf),pltpu.SemaphoreType.DMA((2,))]),
        out_shape=[sd((t,d),bf),sd((t,ff),bf),sd((t,d),bf),sd((t,d),f32),sd((t,d),bf),sd((16,t),f32),sd((16,d),f32)],
        compiler_params=cp(46),name="ffback",cost_estimate=cost(0,0))(lens,pa,pb,*ctxs,middle,act,dg,g2,vec,*abufs,*bbufs)

def wg_body(inv_ref,*refs,na,tasks,pieces,nbuf,raw):
    arrs=refs[:na]; keep_ref,send_ref=refs[na:na+2]; bufs=refs[na+2:na+2+nbuf]
    outs=refs[na+2+nbuf:-2]; isem,osem=refs[-2:]
    half=pieces//2
    if raw: pltpu.make_async_copy(arrs[-1],bufs[-1],isem.at[nbuf-1]).start()
    need=[]; loads={}; k=0
    for t in tasks:
        ids=[]
        for key in tuple(t["a"])+tuple(t["bs"]):
            if key not in loads:
                ai,c0,w=key
                pltpu.make_async_copy(arrs[ai].at[:,pl.ds(c0,w)],bufs[k],isem.at[k]).start()
                loads[key]=k; k+=1
            ids.append(loads[key])
        need.append(ids)
    if raw:
        src_ref=bufs[-1]; last=pl.ds(keep_ref.shape[2]-src_ref.shape[2],src_ref.shape[2])
        pltpu.make_async_copy(src_ref,src_ref,isem.at[nbuf-1]).wait()
        for o in range(pieces):
            r=inv_ref[0,o]
            part=src_ref.at[o]
            @pl.when(r<half)
            def _(): pltpu.make_async_copy(part,keep_ref.at[r,:,last],osem.at[len(tasks)]).start()
            @pl.when(r>=half)
            def _(): pltpu.make_async_copy(part,send_ref.at[r-half,:,last],osem.at[len(tasks)]).start()
    ready=set()
    for ti,(t,ids) in enumerate(zip(tasks,need)):
        for b in ids:
            if b not in ready:
                pltpu.make_async_copy(bufs[b],bufs[b],isem.at[b]).wait(); ready.add(b)
        ka=len(t["a"]); lhs=[bufs[b][...] for b in ids[:ka]]
        lhs=jnp.concatenate(lhs,axis=1) if ka>1 else lhs[0]
        rhs=[bufs[b][...] for b in ids[ka:]]
        rhs=jnp.concatenate(rhs,axis=1) if len(rhs)>1 else rhs[0]
        scr=outs[ti]
        acc=dot(lhs,rhs,TN)
        rows,w=scr.shape[1:]
        for p in range(t["per"]): scr[p]=acc[p*rows:(p+1)*rows].astype(bf)
        for p,(lo,hi,which) in ((p,c) for p in range(t["per"]) for c in t["parts"]):
            r=inv_ref[which,t["o0"]+p]
            src=scr.at[p,:,pl.ds(lo,hi-lo)]
            cols=pl.ds(t["col"]+lo,hi-lo)
            @pl.when(r<half)
            def _(): pltpu.make_async_copy(src,keep_ref.at[r,:,cols],osem.at[ti]).start()
            @pl.when(r>=half)
            def _(): pltpu.make_async_copy(src,send_ref.at[r-half,:,cols],osem.at[ti]).start()
    for ti in range(len(tasks)):
        pltpu.make_async_copy(outs[ti],outs[ti],osem.at[ti]).wait()
    if raw: pltpu.make_async_copy(src_ref,src_ref,osem.at[len(tasks)]).wait()
def wg(arrs,tasks,inv,pieces,rows,width,name,raw=False,mb=26):
    t=arrs[0].shape[0]
    keys=[]; fl=0
    for k in tasks:
        for key in tuple(k["a"])+tuple(k["bs"]):
            if key not in keys: keys.append(key)
        fl+=2*t*sum(a[2] for a in k["a"])*sum(b[2] for b in k["bs"])
    sh=jax.ShapeDtypeStruct((pieces//2,rows,width),bf)
    return pl.pallas_call(functools.partial(wg_body,na=len(arrs),tasks=tasks,pieces=pieces,nbuf=len(keys)+raw,raw=raw),
        grid_spec=pltpu.PrefetchScalarGridSpec(num_scalar_prefetch=1,grid=(),in_specs=[ANY]*len(arrs),out_specs=[ANY,ANY],
            scratch_shapes=[pltpu.VMEM((t,w),bf) for _,_,w in keys]+[pltpu.VMEM(arrs[-1].shape,bf)]*raw+[pltpu.VMEM((k["per"],sum(a[2] for a in k["a"])//k["per"],sum(b[2] for b in k["bs"])),bf) for k in tasks]
                +[pltpu.SemaphoreType.DMA((len(keys)+1,)),pltpu.SemaphoreType.DMA((len(tasks)+1,))]),
        out_shape=[sh,sh],compiler_params=cp(mb),name=name,
        cost_estimate=cost(fl,pieces*rows*width*2+sum(t*k[2]*2 for k in keys)))(inv,*arrs)

def wgn_body(a_ref,b_ref,o_ref):
    o_ref[...]=dot(a_ref[...],b_ref[...],TN).astype(o_ref.dtype)
def wg_natural(a,b,tm,tn,name):
    t,m=a.shape; n=b.shape[1]
    return pl.pallas_call(wgn_body,grid=(m//tm,n//tn),
        in_specs=[pl.BlockSpec((t,tm),lambda i,j:(0,i)),pl.BlockSpec((t,tn),lambda i,j:(0,j))],
        out_specs=pl.BlockSpec((tm,tn),lambda i,j:(i,j)),
        out_shape=jax.ShapeDtypeStruct((m,n),bf),compiler_params=cp(60),name=name,
        cost_estimate=cost(2*t*m*n,t*(m+n)*2+m*n*2))(a,b)

def qb_body(pa_ref,pb_ref,x_ref,dm_ref,vec_ref,s_in_ref,*refs,nq,nf,na,nb,per):
    dqs=refs[:nq]; dks=refs[nq:2*nq]; dfs=refs[2*nq:2*nq+nf]; refs=refs[2*nq+nf:]
    abufs=refs[:na]; bbufs=refs[na:na+nb]
    gh_ref,s_ref,vg_ref,wa,wb,sa,sb,flat,vgf,sems=refs[na+nb:]
    i=pl.program_id(0)
    d=x_ref.shape[1]; dv=wa.shape[1]-d
    @pl.when(i==0)
    def _():
        place(abufs,pa_ref,wa,sa,sems.at[0]); place(bbufs,pb_ref,wb,sb,sems.at[1])
        s_ref[...]=s_in_ref[...]
        placed(wa,sa,sems.at[0],abufs[0].shape[1]); placed(wb,sb,sems.at[1],bbufs[0].shape[1])
    dq=jnp.concatenate([v[...] for v in dqs],axis=1)
    dqv=jnp.concatenate([dq]+[v[...] for v in dfs],axis=1)
    dk=jnp.concatenate([v[...] for v in dks],axis=1)
    dn=dot(dqv,wa[...],NT)+dot(dk,wb[...],NT)
    xh,r=norm_stats(x_ref[...].astype(f32))
    e=dn*vec_ref[0:1,:]
    gh_ref[...]=dm_ref[...]+r*(e-jnp.mean(e,axis=-1,keepdims=True)-xh*jnp.mean(e*xh,axis=-1,keepdims=True))
    s_ref[0:1,:]+=cs_(dn*xh)
    s_ref[1:2,:]+=cs_(dn)
    s_ref[2:3,:]+=cs_(dq.astype(f32))
    if per:
        @pl.when(i==pl.num_programs(0)-1)
        def _():
            vgf[...]=jnp.zeros_like(vgf)
            for u in range((flat.shape[1]-128*3)//d):
                flat[0:1,d*u:d*(u+1)]=s_ref[u:u+1,:]
            for o in range(vgf.shape[0]):
                for s in range(-(-per//128)):
                    vgf[o,s:s+1,:]=flat[0:1,per*o+128*s:per*o+128*(s+1)]
            vg_ref[...]=vgf[...].astype(bf)
def qkv_back(x,dm,vec,s_in,dqs,dks,dfs,wa,wb,per=0,n=1,tm=256):
    vgs=(n,x.shape[1]//n,128) if per else (1,16,128)
    t,d=x.shape; dv=sum(v.shape[1] for v in dfs)
    (abufs,pa),(bbufs,pb)=wa,wb
    row=lambda c:pl.BlockSpec((tm,c),lambda i,*a:(i,0))
    return pl.pallas_call(functools.partial(qb_body,nq=len(dqs),nf=len(dfs),na=len(abufs),nb=len(bbufs),per=per),
        grid_spec=pltpu.PrefetchScalarGridSpec(num_scalar_prefetch=2,grid=(t//tm,),
            in_specs=[row(d),row(d),full(vec.shape),full(s_in.shape)]+[row(v.shape[1]) for v in dqs+dks+dfs]+[ANY]*(len(abufs)+len(bbufs)),
            out_specs=[row(d),full(s_in.shape),full(vgs)],scratch_shapes=[pltpu.VMEM((d,d+dv),bf),pltpu.VMEM((d,d),bf),stage(n,*abufs[0].shape[1:]),stage(n,*bbufs[0].shape[1:]),pltpu.VMEM((1,vec.shape[0]*d+128*3),f32),pltpu.VMEM(vgs,f32),pltpu.SemaphoreType.DMA((2,))]),
        out_shape=[jax.ShapeDtypeStruct((t,d),f32),jax.ShapeDtypeStruct(s_in.shape,f32),jax.ShapeDtypeStruct(vgs,bf)],compiler_params=cp(20),name="qkvback",
        cost_estimate=cost(2*t*d*(2*d+dv),t*d*16+d*d*5))(pa,pb,x,dm,vec,s_in,*dqs,*dks,*dfs,*abufs,*bbufs)
import numpy as np
from jax.sharding import PartitionSpec as P
AXES=("dp","sub")

def index_bits(sizes):
    return [(a,b) for a in reversed(AXES) for b in range(sizes[a].bit_length()-1)]

def swap(v,axis,bit,size):
    return lax.ppermute(v,axis,[(i,i^(1<<bit)) for i in range(size)])

def masks(order):
    p=np.arange(1<<len(order))
    return sum(((p>>s)&1)<<b for s,b in enumerate(order)).astype(np.int32)

class Comm:
    def __init__(self,sizes):
        self.sizes=sizes; self.n=sizes["dp"]*sizes["sub"]
        self.bits=index_bits(sizes); self.nb=len(self.bits)
        self.me=lax.axis_index("dp")*sizes["sub"]+lax.axis_index("sub")
    def cross(self,v,mask):
        return lax.ppermute(v,AXES,[(i,i^mask) for i in range(self.n)])
    def swap(self,v,b):
        axis,k=self.bits[b]
        return swap(v,axis,k,self.sizes[axis])

def gate(nxt,*done):
    return lax.optimization_barrier((nxt,done))[0]

def scatter_sum(c,g,order):
    n,rows,cols=g.shape
    left=list(reversed(range(c.nb)))
    dt=g.dtype
    g=g.reshape((2,)*c.nb+(rows,cols))
    for step,b in enumerate(order):
        axis,k=c.bits[b]
        mine=(lax.axis_index(axis)>>k)&1
        pos=left.index(b); left.pop(pos)
        send=lax.dynamic_index_in_dim(g,1-mine,pos,keepdims=False)
        keep=lax.dynamic_index_in_dim(g,mine,pos,keepdims=False)
        g=keep.astype(f32)+c.swap(send,b).astype(f32)
        if step<len(order)-1: g=g.astype(dt)
    return g

class Sum:
    def __init__(self,c,pair,orders,cut):
        self.c=c; self.keep=pair[0]; self.orders=orders; self.cut=cut
        self.send=[pair[1]]; self.masks=[1<<orders[0][0]]; self.got=[]; self.s=0
    def step(self):
        self.got.append([self.c.cross(v,m) for v,m in zip(self.send,self.masks)]); self.s+=1
    def part(self,lo,hi,cols):
        w=self.keep.shape[2]
        a,b=(0,self.cut) if cols==0 else (self.cut,w)
        tot=self.keep[lo:hi,:,a:b].astype(f32)
        for s,parts in enumerate(self.got):
            g=parts[cols][lo:hi] if s in (1,2) and self.cut<w else parts[0][lo:hi,:,a:b]
            tot=tot+g.astype(f32)
        return tot
    def both(self,lo,hi):
        if self.cut==self.keep.shape[2]: return self.part(lo,hi,0)
        return jnp.concatenate([self.part(lo,hi,0),self.part(lo,hi,1)],axis=2)
    def make(self):
        w=self.keep.shape[0]>>self.s
        if self.s in (1,2) and self.cut<self.keep.shape[2]:
            self.send=[self.part(w,2*w,i).astype(bf) for i in (0,1)]
            self.masks=[1<<o[self.s] for o in self.orders]
        else:
            self.send=[self.both(w,2*w).astype(bf)]
            self.masks=[1<<self.orders[0][self.s]]
    def wide(self):
        o=self.orders[0]; q=self.keep.shape[0]>>(self.s+1)
        self.send=[self.both(q*g,q*(g+1)).astype(bf) for g in (1,2,3)]
        self.masks=[((g>>1)<<o[self.s])|((g&1)<<o[self.s+1]) for g in (1,2,3)]
    def wide_step(self):
        for v,m in zip(self.send,self.masks): self.got.append([self.c.cross(v,m)])
        self.s+=2
    def total(self):
        return self.both(0,1)[0]

def exchange(sums,nxt,*done):
    sends,nxt=gate(([s.send for s in sums],nxt),*done)
    for s,v in zip(sums,sends): s.send=v
    for s in sums: s.step()
    return nxt
def join(sums,*done):
    got=gate([s.got[-1] for s in sums],*done)
    for s,v in zip(sums,got): s.got[-1]=v

def shards(sizes,hidden_in,first_values,doc_lengths,out_cotangent,query_weight,key_weight,value_weight,output_weight,up_weight,down_weight,vector_pieces):
    c=Comm(sizes); n=c.n; nb=c.nb
    t,d=hidden_in.shape; dv=first_values.shape[1]
    ff=up_weight.shape[0]*n//d
    vs=vector_pieces.shape[0]; h=d//2; rows=d//n; fan=ff//d
    fast=n==1<<nb and n==32 and (d//n)%8==0
    lens=doc_lengths[0]
    x=hidden_in; cot=out_cotangent
    s=sizes["sub"].bit_length()-1
    A=list(range(nb)); B=A[:]
    if s>=2 and nb>s: B[1],B[s]=B[s],B[1]
    qp=jnp.concatenate([query_weight.reshape(-1,d),value_weight.reshape(-1,dv)],axis=1)
    kp=key_weight.reshape(-1,d)
    op=jnp.concatenate([output_weight.reshape(-1,d),up_weight.reshape(-1,ff)],axis=1)
    np_=d//128; hp=np_//2; nvec=7+fan
    if fast:
        vp=jnp.pad(jnp.pad(vector_pieces,(0,-vs%128)).reshape(-1,128),((0,rows--(-vs//128)),(0,0)))
        g1=jnp.concatenate([qp,kp,vp],axis=1)[None]
        ga,gb_=A[::-1],B[::-1]
        pos_a=c.me^jnp.asarray(masks(ga)); pos_b=c.me^jnp.asarray(masks(gb_))
        cat=lambda a,b:jnp.concatenate([a,b],axis=0)
        halves=lambda a:(a[:,:,:a.shape[2]//2],a[:,:,a.shape[2]//2:])
        two=lambda a,b,st:(c.swap(a,ga[st]),c.swap(b,gb_[st]))
        z1,z0=1<<ga[0],1<<ga[1]
        r1=[c.cross(g1,m) for m in (z1,z0,z1|z0)]
        g1=jnp.concatenate([g1]+r1,axis=0)
        def inverse(order):
            table=jnp.asarray(np.argsort(masks(order[::-1])).astype(np.int32))
            return jnp.take(table,c.me^jnp.arange(n,dtype=jnp.int32))
        q_,k_,op,inv,pos_a,pos_b=gate((g1[:,:,:d+dv],g1[:,:,d+dv:],op,jnp.stack([inverse(A),inverse(B)]),pos_a,pos_b))
        g2_=op[None]
        rq,rk=two(q_,k_,2)
        r2=c.swap(g2_,ga[0])
        q_,k_=gate((cat(q_,rq),cat(k_,rk)))
        rq,rk=two(q_,k_,3)
        g2_,dw_=gate((g2_,down_weight),q_)
        g2_=cat(g2_,r2)
        r2=c.swap(g2_,ga[1])
        g3_=dw_.reshape(1,fan*rows,d)
        q_,k_=gate((cat(q_,rq),cat(k_,rk)))
        rq,rk=two(q_,k_,4)
        g2_=gate(g2_,q_)
        g2a,g2b=halves(cat(g2_,r2))
        ra,rb=two(g2a,g2b,2)
        x0,g3_=gate((x,g3_),rq,rk)
        r3=c.swap(g3_,ga[0])
        wq=((q_,rq),pos_a); wk=((k_,rk),pos_b)
        nrm,q,k,v,vec=qkv(x0,first_values,wq,wk,vs,jnp.zeros((nvec,d),f32))
        g2a,g2b,g3_,r3,qa=gate((g2a,g2b,g3_,r3,q),k)
        g2a,g2b,g3_=cat(g2a,ra),cat(g2b,rb),cat(g3_,r3)
        ra,rb=two(g2a,g2b,3)
        r3=c.swap(g3_,ga[1])
        w0=hp+1
        c0,l0=afwd(lens,qa,k,v,0,w0)
        o_a,o_b,g3_,r3,qa=gate(((g2a,ra),(g2b,rb),g3_,r3,qa),c0)
        g3a,g3b=halves(cat(g3_,r3))
        abufs=o_a+tuple(c.swap(v_,ga[4]) for v_ in o_a)+o_b+tuple(c.swap(v_,gb_[4]) for v_ in o_b)
        sa,sb=two(g3a,g3b,2)
        c1,l1=afwd(lens,qa,k,v,w0,np_-w0)
        g3a,g3b,x1=gate((g3a,g3b,x),c1,*abufs)
        g3a,g3b=cat(g3a,sa),cat(g3b,sb)
        g3a,g3b,x1=gate((g3a,g3b,x1))
        sa,sb=two(g3a,g3b,3)
        ctxs=[c0,c1]; lse_parts=[l0,l1]
        middle,n2,act,dg,g2=ff_forward(lens,ctxs,x1,cot,abufs,pos_a,pos_b,vec,True)
        d_a,d_b,act1=gate(((g3a,sa),(g3b,sb),act),n2)
        bbufs=tuple(d_a)+tuple(c.swap(v_,ga[4]) for v_ in d_a)+tuple(d_b)+tuple(c.swap(v_,gb_[4]) for v_ in d_b)
    else:
        z=jnp.zeros((1,),jnp.int32)
        ag=lambda v:((lax.all_gather(v,AXES,axis=0,tiled=True)[None],),z)
        wq,wk,wo,wd=ag(qp),ag(kp),ag(op),ag(down_weight.reshape(-1,d))
        vec=lax.all_gather(vector_pieces,AXES,axis=0,tiled=True).reshape(-1,d).astype(f32)
        nrm,q,k,v,vec=qkv(x,first_values,wq,wk,0,vec)
        (abufs,pos_a),(bbufs,pos_b)=wo,wd
        ctx0,lse0=afwd(lens,q,k,v,0,np_)
        ctxs=[ctx0]; lse_parts=[lse0]
        middle,n2,act,dg,g2=ff_forward(lens,ctxs,x,cot,abufs,pos_a,pos_b,vec,False)
    hb=lambda ac:ff_back(lens,ctxs,middle,ac,dg,g2,abufs,bbufs,pos_a,pos_b,vec,fast)
    if fast:
        s_d=Sum(c,wg([act1,g2],[dict(a=((0,d*u,d),),bs=((1,0,d),),o0=u*n//fan,per=n//fan,col=0,parts=((0,h,0),(h,d,1))) for u in range(fan)],inv,n,rows*fan,d,"dwd",mb=60),(A,B),h)
        act2=exchange([s_d],act,*bbufs)
        out,gp,gb,dm,gc,dl,sv=hb(act2)
        join([s_d],gb); s_d.make()
        n2=exchange([s_d],n2)
        s_u=Sum(c,wg([n2,gp],[dict(a=((0,0,d),),bs=((1,d*u,d),),o0=0,per=n,col=d*u,parts=((0,d,u*2//fan),)) for u in range(fan)],inv,n,rows,ff,"dwu"),(A,B),ff//2)
        back=lambda p,w,qv:abwd(lens,qv,k,v,gc,lse_parts[int(p>=w0)],p-w0*int(p>=w0),dl,p,w,bf if p<hp else f32)
        join([s_d],s_u.send); s_d.make()
        g=[back(0,hp-1,exchange([s_d,s_u],q))]
        join([s_d,s_u],g[0][0]); s_d.make(); s_u.make()
        g.append(back(hp-1,1,exchange([s_d,s_u],q)))
        wide=lambda e0,e1,i,at:((at,0,e0[i].shape[1]),(at+1,0,e1[i].shape[1]))
        s_1=Sum(c,wg([gate(nrm,g[1][0])]+[e[i] for i in range(3) for e in g]+[gb]+ctxs,
            [dict(a=tuple((8+i,0,v_.shape[1]) for i,v_ in enumerate(ctxs)),bs=((7,0,d),),o0=0,per=n,col=2*h+dv,parts=((0,d,1),))]
            +[dict(a=((0,0,d),),bs=sum((wide(g[0],g[1],i,1+2*i) for i in range(3)),()),o0=0,per=n,col=0,parts=((0,2*h+dv,0),))],inv,n,rows,2*h+dv+d,"dw1"),(A,B),2*h+dv)
        join([s_d,s_u],s_1.send); s_d.make(); s_u.make()
        late=back(w0,hp-1,exchange([s_d,s_u,s_1],q))
        join([s_d,s_u,s_1],late[0]); s_u.make(); s_1.make()
        g+=[back(hp,1,exchange([s_u,s_1],q)),late]
        gh,sv,vg=qkv_back(gate(x,g[2][0]),dm,vec,sv,[e[0] for e in g],[e[1] for e in g],[e[2] for e in g[:2]],wq,wk,vs,n)
        join([s_u,s_1],gh); s_u.make(); s_1.make()
        vg=exchange([s_u,s_1],vg)
        s_2=Sum(c,wg([nrm]+[e[i] for i in range(2) for e in g[2:]]+[vg],[dict(a=((0,0,d),),bs=sum((wide(g[2],g[3],i,1+2*i) for i in range(2)),()),o0=0,per=n,col=0,parts=((0,2*h,0),))],inv,n,rows,2*h+128,"dw2",raw=True),(A,A),2*h+128)
        join([s_u,s_1],s_2.send)
        exchange([s_2],()); s_1.make(); exchange([s_1],())
        join([s_1,s_2])
        s_2.wide(); s_2.wide_step()
        s_1.make(); s_1.step()
        s_2.wide(); s_2.wide_step()
        t_d,t_u,t_1,t_2=(st.total() for st in (s_d,s_u,s_1,s_2))
        t_o=t_1[:,2*h+dv:]; gf=jnp.concatenate([g[2][2],g[3][2]],axis=1); gvec=t_2[:-(-vs//128),2*h:].reshape(-1)[:vs]
    else:
        out,gp,gb,dm,gc,dl,sv=hb(act)
        g=[abwd(lens,q,k,v,gc,lse_parts[0],p,dl,p,hp,bf if p<hp else f32) for p in (0,hp)]
        pc=lambda a,b,tn,name:wg_natural(a,b,768,tn,name).reshape(n,-1,b.shape[1])
        dq,dk,dfg=(jnp.concatenate([e[i] for e in (g if i<2 else g[:1])],axis=1) for i in range(3))
        gf=g[1][2]
        t_d=scatter_sum(c,pc(act,g2,768,"dwd"),A); t_u=scatter_sum(c,pc(n2,gp,768,"dwu"),B); t_o=scatter_sum(c,pc(ctxs[0],gb,768,"dwo"),A)
        t_1=scatter_sum(c,jnp.concatenate([pc(nrm,dq[:,:h],h,"dwqa"),pc(nrm,dk[:,:h],h,"dwka"),pc(nrm,dfg,dv,"dwv")],axis=2),B)
        t_2=scatter_sum(c,jnp.concatenate([pc(nrm,dq[:,h:],h,"dwqb"),pc(nrm,dk[:,h:],h,"dwkb")],axis=2),A)
        gh,sv,_=qkv_back(x,dm,vec,sv,[dq],[dk],[dfg],wq,wk)
        gvec=scatter_sum(c,sv[:nvec].reshape(n,1,vs),A).reshape(-1)
    gq=jnp.concatenate([t_1[:,:h],t_2[:,:h]],axis=1).reshape(-1)
    gk=jnp.concatenate([t_1[:,h:2*h],t_2[:,h:2*h]],axis=1).reshape(-1)
    gv=t_1[:,2*h:2*h+dv].reshape(-1)
    return (out,gh,gf,gq,gk,gv,t_o.reshape(-1),t_u.reshape(-1),t_d.reshape(-1),gvec)

def solution(mesh):
    s2=P(AXES,None); s1=P(AXES)
    return jax.shard_map(functools.partial(shards,dict(mesh.shape)),mesh=mesh,in_specs=(s2,)*4+(s1,)*7,out_specs=(s2,)*3+(s1,)*7,check_vma=False)
```
